32 devices in a mesh: dp: 8 (over z, y), tensor: 4 (over x, core).
Axes of the slice: x: 2, y: 2, z: 4, core: 2. Of those that a mesh axis runs over, the one named last changes fastest.
Arguments:
- tokens: bfloat16 [6144, 1120], P('dp', 'tensor'), may hold values from -6 to 6
- first_gain: float32 [1120], replicated, may hold values from 0.5 to 1.5
- first_shift: float32 [1120], replicated, may hold values from -3 to 3
- triple_weight: bfloat16 [1120, 3, 1120], P(None, None, 'tensor'), may hold values from -0.1875 to 0.1875
- triple_bias: float32 [2, 1120], P(None, 'tensor'), may hold values from -3 to 3
- output_weight: bfloat16 [1120, 1120], P('tensor'), may hold values from -0.5 to 0.5
- output_bias: float32 [1120], replicated, may hold values from -3 to 3
- second_gain: float32 [1120], replicated, may hold values from 0.5 to 1.5
- second_shift: float32 [1120], replicated, may hold values from -3 to 3
- up_weight: bfloat16 [1120, 4480], P(None, 'tensor'), may hold values from -0.1875 to 0.1875
- up_bias: float32 [4480], P('tensor'), may hold values from -3 to 3
- down_weight: bfloat16 [4480, 1120], P('tensor'), may hold values from -0.09375 to 0.09375
- down_bias: float32 [1120], replicated, may hold values from -3 to 3
- cotangent: bfloat16 [6144, 1120], P('dp', 'tensor'), may hold values from -6 to 6
- lengths: int32 [16], P('dp'), may hold values from 96 to 384
Outputs:
- layer_out: bfloat16 [6144, 1120], P('dp', 'tensor')
- input_grad: bfloat16 [6144, 1120], P('dp', 'tensor')
- first_gain_grad: float32 [1120], replicated
- first_shift_grad: float32 [1120], replicated
- triple_weight_grad: float32 [1120, 3, 1120], P(None, None, 'tensor')
- triple_bias_grad: float32 [2, 1120], P(None, 'tensor')
- output_weight_grad: float32 [1120, 1120], P('tensor')
- output_bias_grad: float32 [1120], replicated
- second_gain_grad: float32 [1120], replicated
- second_shift_grad: float32 [1120], replicated
- up_weight_grad: float32 [1120, 4480], P(None, 'tensor')
- up_bias_grad: float32 [4480], P('tensor')
- down_weight_grad: float32 [4480, 1120], P('tensor')
- down_bias_grad: float32 [1120], replicated
The draws below stay inside these ranges and needn't reach their ends.
All inputs are finite; a program needn't handle non-finite values.
Results may differ from the reference program's by a relative error of at most 0.019.
Values may be sent and summed in bfloat16 or wider, within the bound.
No kernel may reach another device: no remote copies, remote signals or barrier semaphores. Data moves between devices by JAX's collectives and lax.ppermute only.
A program may use at most 128 MiB of HBM per device.

```python
import jax
import jax.numpy as jnp
from jax import lax

HEADS = 20
HEAD_DIM = 56
D = 1120
FF = 4480
CELL_LEN = 384
CELLS = 16
TOKENS = 6144


def place_ends(drawn, key, smallest, top_value):
    place = [jax.random.randint(jax.random.fold_in(key, axis), (), 0, length) for axis, length in enumerate(drawn.shape)]
    longest = drawn.shape.index(max(drawn.shape))
    beside = place[:longest] + [(place[longest] + 1) % drawn.shape[longest]] + place[longest + 1:]
    return drawn.at[tuple(place)].set(smallest).at[tuple(beside)].set(top_value)


def levels(rng, extent, cuts, least, top_value):
    def one(position, blocks):
        draws = jax.random.uniform(jax.random.fold_in(jax.random.fold_in(rng, 6), position), (blocks,), jnp.float32, least / len(cuts), top_value / len(cuts))
        return jnp.repeat(jnp.exp(draws), extent[position] // blocks).reshape((-1,) + (1,) * (len(extent) - position - 1))

    factor_of = one(*cuts[0])
    for cut in cuts[1:]:
        factor_of = factor_of * one(*cut)
    return factor_of


def scatter_about(own_key, extent, width, bound, cuts=(), dtype=jnp.bfloat16):
    values = jax.random.normal(own_key, extent, jnp.float32) * width
    if len(cuts) > 0:
        values = levels(own_key, extent, cuts, -0.22, 0.18) * values
    return jnp.clip(values, min=-bound, max=bound).astype(dtype)


def setup_inputs(seed: int = 0) -> dict:
    seeds = jax.random.split(jax.random.key(seed), 16)
    return {
        "tokens": scatter_about(seeds[0], (TOKENS, D), 1.0, 6.0, ((0, 8), (1, 4))),
        "first_gain": jnp.clip(1.0 + 0.1 * jax.random.normal(seeds[1], (D,), jnp.float32), 0.5, 1.5),
        "first_shift": scatter_about(seeds[2], (D,), 0.5, 3.0, (), jnp.float32),
        "triple_weight": scatter_about(seeds[3], (D, 3, D), D ** -0.5, 0.1875, ((2, 4),)),
        "triple_bias": scatter_about(seeds[4], (2, D), 0.5, 3.0, ((1, 4),), jnp.float32),
        "output_weight": scatter_about(seeds[5], (D, D), (D // 8) ** -0.5, 0.5, ((0, 4),)),
        "output_bias": scatter_about(seeds[6], (D,), 0.5, 3.0, (), jnp.float32),
        "second_gain": jnp.clip(1.0 + 0.1 * jax.random.normal(seeds[7], (D,), jnp.float32), 0.5, 1.5),
        "second_shift": scatter_about(seeds[8], (D,), 0.5, 3.0, (), jnp.float32),
        "up_weight": scatter_about(seeds[9], (D, FF), D ** -0.5, 0.1875, ((1, 4),)),
        "up_bias": scatter_about(seeds[10], (FF,), 0.5, 3.0, ((0, 4),), jnp.float32),
        "down_weight": scatter_about(seeds[11], (FF, D), FF ** -0.5, 0.09375, ((0, 4),)),
        "down_bias": scatter_about(seeds[12], (D,), 0.5, 3.0, (), jnp.float32),
        "cotangent": scatter_about(seeds[13], (TOKENS, D), 1.0, 6.0, ((0, 8), (1, 4))),
        "lengths": place_ends(jax.random.randint(seeds[14], (CELLS,), CELL_LEN // 4, CELL_LEN + 1), jax.random.fold_in(seeds[14], 1), CELL_LEN // 4, CELL_LEN).astype(jnp.int32),
    }


epsilon = 1e-05
highest = lax.Precision.HIGHEST

@jax.custom_vjp
def low(v):
    return lax.optimization_barrier(v.astype(jnp.bfloat16)).astype(jnp.float32)

@jax.custom_vjp
def low_back(v):
    return v

def low_keep(v):
    return (low(v), None)

def low_pass(kept, grad):
    return (grad,)

def back_keep(v):
    return (v, None)

def back_low(kept, grad):
    return (low(grad),)
low.defvjp(low_keep, low_pass)
low_back.defvjp(back_keep, back_low)

def layer_norm(field, gain, shift):
    center = field - lax.optimization_barrier(jnp.mean(field, -1, keepdims=True))
    spread = lax.optimization_barrier(jnp.mean(center * center, -1, keepdims=True))
    return center * lax.rsqrt(spread + epsilon) * gain + shift

def matmul(left, right):
    return jnp.dot(left, right, precision=highest)

def attend(item):
    queries, key_rows, value_rows, length = item
    raw = jnp.einsum('qhd,khd->hqk', queries, key_rows, precision=highest)
    scores = low_back(raw) * HEAD_DIM ** (-0.5)
    places = jnp.arange(CELL_LEN)
    allowed = (places[None, :] <= places[:, None]) & (places[None, :] < length)
    masked = jnp.where(allowed[None], scores, -1e+30)
    largest = lax.optimization_barrier(jnp.max(masked, -1, keepdims=True))
    expo = jnp.exp(masked - largest)
    probs = expo / lax.optimization_barrier(jnp.sum(expo, -1, keepdims=True))
    context = jnp.einsum('hqk,khd->qhd', low(probs), value_rows, precision=highest)
    return context.reshape(CELL_LEN, D)

def forward(tokens, first_gain, first_shift, triple_weight, triple_bias, output_weight, output_bias, second_gain, second_shift, up_weight, up_bias, down_weight, down_bias, lengths):
    first_normed = low(layer_norm(tokens, first_gain, first_shift))
    queries = low(low_back(matmul(first_normed, triple_weight[:, 0, :])) + triple_bias[0])
    key_rows = low(low_back(matmul(first_normed, triple_weight[:, 1, :])))
    value_rows = low(low_back(matmul(first_normed, triple_weight[:, 2, :])) + triple_bias[1])
    shape = (CELLS, CELL_LEN, HEADS, HEAD_DIM)
    context = lax.map(jax.checkpoint(attend), (queries.reshape(shape), key_rows.reshape(shape), value_rows.reshape(shape), lengths))
    context = low_back(low(context.reshape(TOKENS, D)))
    resid = tokens + low_back(matmul(context, output_weight)) + output_bias
    second_normed = low(layer_norm(resid, second_gain, second_shift))
    hidden_pre = low_back(matmul(second_normed, up_weight)) + up_bias
    hidden = low(jax.nn.gelu(hidden_pre, approximate=True))
    return resid + matmul(hidden, down_weight) + down_bias

def reference(tokens, first_gain, first_shift, triple_weight, triple_bias, output_weight, output_bias, second_gain, second_shift, up_weight, up_bias, down_weight, down_bias, cotangent, lengths):
    params = tuple((item.astype(jnp.float32) for item in (tokens, first_gain, first_shift, triple_weight, triple_bias, output_weight, output_bias, second_gain, second_shift, up_weight, up_bias, down_weight, down_bias)))

    def runner(*inner):
        return forward(*inner, lengths)
    result, backward = jax.vjp(runner, *params)
    grads = backward(cotangent.astype(jnp.float32))
    return (result.astype(jnp.bfloat16), grads[0].astype(jnp.bfloat16), grads[1], grads[2], grads[3], grads[4], grads[5], grads[6], grads[7], grads[8], grads[9], grads[10], grads[11], grads[12])
```

```python
import functools

import jax
import jax.numpy as jnp
from jax import lax
from jax.sharding import PartitionSpec as P

HEAD_DIM = 56
CELL_LEN = 384


epsilon = 1e-05


def layer_norm(field, gain, shift):
    center = field - jnp.mean(field, -1, keepdims=True)
    spread = jnp.mean(center * center, -1, keepdims=True)
    return center * lax.rsqrt(spread + epsilon) * gain + shift


def smooth_gate(field):
    return jax.nn.gelu(field, approximate=True)


def swap_core(value, size):
    return lax.ppermute(value, "tensor", [(place, place ^ 1) for place in range(size)])


def swap_chip(value, size):
    return lax.ppermute(value, "tensor", [(place, place ^ 2) for place in range(size)])


def ordered(bit, mine, other, axis):
    low = jnp.where(bit == 0, mine, other)
    high = jnp.where(bit == 0, other, mine)
    return jnp.concatenate([low, high], axis)


def gather_features(share, size):
    if size != 4:
        return lax.all_gather(share, "tensor", axis=1, tiled=True)
    place = lax.axis_index("tensor")
    core, chip = place % 2, place // 2
    far = swap_chip(share, size)
    near_pair = ordered(core, share, swap_core(share, size), 1)
    far_pair = ordered(core, far, swap_core(far, size), 1)
    return ordered(chip, near_pair, far_pair, 1)


def add_low(left, right):
    return (left.astype(jnp.float32) + right.astype(jnp.float32)).astype(jnp.bfloat16)


def take_half(value, index, axis):
    half = value.shape[axis] // 2
    return lax.dynamic_slice_in_dim(value, index * half, half, axis)


def sum_features(part, size):
    if size != 4:
        return lax.psum(part, "tensor")
    core = lax.axis_index("tensor") % 2
    near = add_low(take_half(part, core, 0), swap_core(take_half(part, 1 - core, 0), size))
    total = add_low(near, swap_chip(near, size))
    return ordered(core, total, swap_core(total, size), 0)


def scatter_features(part, size):
    if size != 4:
        return lax.psum_scatter(part, "tensor", scatter_dimension=1, tiled=True)
    place = lax.axis_index("tensor")
    core, chip = place % 2, place // 2
    share = part.shape[1] // 4
    blocks = [part[:, place * share : (place + 1) * share] for place in range(4)]

    def pick(bit, first, second):
        return jnp.where(bit == 0, first, second)

    send = jnp.concatenate([pick(core, blocks[1], blocks[0]), pick(core, blocks[3], blocks[2])], 0)
    got = swap_core(send, size)
    rows = part.shape[0]
    lower = add_low(pick(core, blocks[0], blocks[1]), got[:rows])
    upper = add_low(pick(core, blocks[2], blocks[3]), got[rows:])
    away = swap_chip(pick(chip, upper, lower), size)
    return pick(chip, lower, upper).astype(jnp.float32) + away.astype(jnp.float32)


def line_pairs(pairs):
    return [(2 * source + side, 2 * target + side) for source, target in pairs for side in (0, 1)]


INWARD = line_pairs([(0, 1), (3, 2)])
MIDDLE = line_pairs([(1, 2), (2, 1)])
OUTWARD = line_pairs([(1, 0), (2, 3)])
ACROSS = [(place, place ^ 1) for place in range(8)]
ACROSS_MIDDLE = [(2, 3), (3, 2), (4, 5), (5, 4)]


def hop(value, pairs):
    return lax.ppermute(value, "dp", pairs)


def sum_across_first(value):
    place = lax.axis_index("dp")
    side, row = place % 2, place // 2
    at_end = (row == 0) | (row == 3)
    value = add_low(take_half(value, side, 0), hop(take_half(value, 1 - side, 0), ACROSS))
    value = add_low(value, hop(value, INWARD))
    value = add_low(value, hop(value, MIDDLE))
    value = jnp.where(at_end, hop(value, OUTWARD), value)
    return ordered(side, value, hop(value, ACROSS), 0)


def sum_along_first(value):
    place = lax.axis_index("dp")
    row = place // 2
    at_end = (row == 0) | (row == 3)
    upper = row // 2
    value = add_low(value, hop(value, INWARD))
    value = add_low(take_half(value, upper, 0), hop(take_half(value, 1 - upper, 0), MIDDLE))
    value = add_low(value, hop(value, ACROSS_MIDDLE))
    value = ordered(upper, value, hop(value, MIDDLE), 0)
    return jnp.where(at_end, hop(value, OUTWARD), value)


def sum_cells(value, groups):
    value = value.astype(jnp.bfloat16)
    if groups != 8:
        return lax.psum(value, "dp").astype(jnp.float32)
    half = value.shape[0] // 2
    first = sum_across_first(value[:half])
    second = sum_along_first(value[half:])
    return jnp.concatenate([first, second], 0).astype(jnp.float32)


def sum_small(value, groups):
    if groups != 8:
        return lax.psum(value, "dp")
    for step in (1, 4, 2):
        value = value + hop(value, [(place, place ^ step) for place in range(8)])
    return value


def body(
    groups,
    size,
    tokens,
    first_gain,
    first_shift,
    triple_weight,
    triple_bias,
    output_weight,
    output_bias,
    second_gain,
    second_shift,
    up_weight,
    up_bias,
    down_weight,
    down_bias,
    cotangent,
    lengths,
):
    row_count = tokens.shape[0]
    share_width = tokens.shape[1]
    width = triple_weight.shape[0]
    head_width = triple_weight.shape[2]
    local_heads = head_width // HEAD_DIM
    cell_count = row_count // CELL_LEN
    factor = HEAD_DIM ** (-0.5)
    offset = lax.axis_index("tensor") * share_width
    shape = (cell_count, CELL_LEN, local_heads, HEAD_DIM)
    whole_rows = gather_features(tokens, size)
    grad_rows = gather_features(cotangent, size)
    floats = whole_rows.astype(jnp.float32)
    first_normed = layer_norm(floats, first_gain, first_shift).astype(jnp.bfloat16)
    triple_flat = triple_weight.reshape(width, 3 * head_width)
    projected = jnp.dot(first_normed, triple_flat, preferred_element_type=jnp.float32)
    projected = projected.reshape(row_count, 3, head_width)
    queries = (projected[:, 0] + triple_bias[0]).astype(jnp.bfloat16).reshape(shape)
    key_rows = projected[:, 1].astype(jnp.bfloat16).reshape(shape)
    value_rows = (projected[:, 2] + triple_bias[1]).astype(jnp.bfloat16).reshape(shape)
    places = jnp.arange(CELL_LEN)
    allowed = (places[None, None, :] <= places[None, :, None]) & (
        places[None, None, :] < lengths[:, None, None]
    )
    allowed = allowed[:, None]
    scores = (
        jnp.einsum("cqhd,ckhd->chqk", queries, key_rows, preferred_element_type=jnp.float32)
        * factor
    )
    masked = jnp.where(allowed, scores, -1e30)
    largest = jnp.max(masked, -1, keepdims=True)
    expo = jnp.exp(masked - largest)
    probs = expo / jnp.sum(expo, -1, keepdims=True)
    probs_low = probs.astype(jnp.bfloat16)
    context = jnp.einsum(
        "chqk,ckhd->cqhd", probs_low, value_rows, preferred_element_type=jnp.float32
    )
    context = context.reshape(row_count, head_width).astype(jnp.bfloat16)
    partial_value = jnp.dot(context, output_weight, preferred_element_type=jnp.float32)
    resid_full = (
        floats
        + sum_features(partial_value.astype(jnp.bfloat16), size).astype(jnp.float32)
        + output_bias
    )
    resid_share = lax.dynamic_slice_in_dim(resid_full, offset, share_width, 1)
    second_normed = layer_norm(resid_full, second_gain, second_shift).astype(jnp.bfloat16)
    hidden_pre = jnp.dot(second_normed, up_weight, preferred_element_type=jnp.float32) + up_bias
    hidden = smooth_gate(hidden_pre).astype(jnp.bfloat16)
    down_part = jnp.dot(hidden, down_weight, preferred_element_type=jnp.float32)
    down_total = scatter_features(down_part.astype(jnp.bfloat16), size)
    layer_out = (
        resid_share + down_total + lax.dynamic_slice_in_dim(down_bias, offset, share_width)
    ).astype(jnp.bfloat16)
    grad_float = grad_rows.astype(jnp.float32)
    down_bias_grad = jnp.sum(grad_float, 0)
    down_grad = jnp.einsum("rf,rd->fd", hidden, grad_rows, preferred_element_type=jnp.float32)
    hidden_grad = jnp.einsum(
        "rd,fd->rf", grad_rows, down_weight, preferred_element_type=jnp.float32
    )
    gate_value, gate_back = jax.vjp(smooth_gate, hidden_pre)
    pre_grad = gate_back(hidden_grad)[0]
    up_bias_grad = jnp.sum(pre_grad, 0)
    pre_low = pre_grad.astype(jnp.bfloat16)
    up_grad = jnp.einsum("rd,rf->df", second_normed, pre_low, preferred_element_type=jnp.float32)
    normed_part = jnp.einsum("rf,df->rd", pre_low, up_weight, preferred_element_type=jnp.float32)
    normed_grad = sum_features(normed_part.astype(jnp.bfloat16), size).astype(jnp.float32)
    norm_value, second_back = jax.vjp(layer_norm, resid_full, second_gain, second_shift)
    resid_back, second_gain_grad, second_shift_grad = second_back(normed_grad)
    resid_grad = grad_float + resid_back
    output_bias_grad = jnp.sum(resid_grad, 0)
    resid_low = resid_grad.astype(jnp.bfloat16)
    output_grad = jnp.einsum("rh,rd->hd", context, resid_low, preferred_element_type=jnp.float32)
    context_grad = jnp.einsum(
        "rd,hd->rh", resid_low, output_weight, preferred_element_type=jnp.float32
    )
    context_grad = context_grad.astype(jnp.bfloat16).reshape(shape)
    prob_grad = jnp.einsum(
        "cqhd,ckhd->chqk", context_grad, value_rows, preferred_element_type=jnp.float32
    )
    value_grad = jnp.einsum(
        "chqk,cqhd->ckhd", probs_low, context_grad, preferred_element_type=jnp.float32
    )
    score_grad = probs * (prob_grad - jnp.sum(prob_grad * probs, -1, keepdims=True))
    score_low = (score_grad * factor).astype(jnp.bfloat16)
    query_grad = jnp.einsum(
        "chqk,ckhd->cqhd", score_low, key_rows, preferred_element_type=jnp.float32
    )
    key_grad = jnp.einsum("chqk,cqhd->ckhd", score_low, queries, preferred_element_type=jnp.float32)
    query_grad = query_grad.reshape(row_count, head_width)
    key_grad = key_grad.reshape(row_count, head_width)
    value_grad = value_grad.reshape(row_count, head_width)
    triple_bias_grad = jnp.stack([jnp.sum(query_grad, 0), jnp.sum(value_grad, 0)], 0)
    triple_low = jnp.stack([query_grad, key_grad, value_grad], 1).astype(jnp.bfloat16)
    triple_low = triple_low.reshape(row_count, 3 * head_width)
    triple_grad = jnp.einsum(
        "rd,rc->dc", first_normed, triple_low, preferred_element_type=jnp.float32
    )
    triple_grad = triple_grad.reshape(width, 3, head_width)
    first_part = jnp.einsum(
        "rc,dc->rd", triple_low, triple_flat, preferred_element_type=jnp.float32
    )
    first_grad = sum_features(first_part.astype(jnp.bfloat16), size).astype(jnp.float32)
    first_value, first_back = jax.vjp(layer_norm, floats, first_gain, first_shift)
    input_back, first_gain_grad, first_shift_grad = first_back(first_grad)
    input_full = resid_grad + input_back
    input_grad = lax.dynamic_slice_in_dim(input_full, offset, share_width, 1).astype(jnp.bfloat16)
    down_grad = sum_cells(down_grad, groups)
    up_grad = sum_cells(up_grad, groups)
    output_grad = sum_cells(output_grad, groups)
    triple_grad = sum_cells(triple_grad.reshape(width, 3 * head_width), groups)
    triple_grad = triple_grad.reshape(width, 3, head_width)
    middle = jnp.stack(
        [down_bias_grad, up_bias_grad, second_gain_grad, second_shift_grad, output_bias_grad], 0
    )
    middle = sum_small(middle, groups)
    final = jnp.stack([first_gain_grad, first_shift_grad], 0)
    final = sum_small(final, groups)
    triple_bias_grad = sum_small(triple_bias_grad, groups)
    return (
        layer_out,
        input_grad,
        final[0],
        final[1],
        triple_grad,
        triple_bias_grad,
        output_grad,
        middle[4],
        middle[2],
        middle[3],
        up_grad,
        middle[1],
        down_grad,
        middle[0],
    )


def solution(mesh):
    placed = (
        P("dp", "tensor"),
        P(),
        P(),
        P(None, None, "tensor"),
        P(None, "tensor"),
        P("tensor", None),
        P(),
        P(),
        P(),
        P(None, "tensor"),
        P("tensor"),
        P("tensor", None),
        P(),
        P("dp", "tensor"),
        P("dp"),
    )
    return jax.shard_map(
        functools.partial(body, mesh.shape["dp"], mesh.shape["tensor"]),
        mesh=mesh,
        in_specs=placed,
        out_specs=(
            P("dp", "tensor"),
            P("dp", "tensor"),
            P(),
            P(),
            P(None, None, "tensor"),
            P(None, "tensor"),
            P("tensor", None),
            P(),
            P(),
            P(),
            P(None, "tensor"),
            P("tensor"),
            P("tensor", None),
            P(),
        ),
        check_vma=False,
    )
```

```python
import functools

import jax
import jax.numpy as jnp
from jax import lax
from jax.experimental import pallas as pl
from jax.experimental.pallas import tpu as pltpu
from jax.sharding import PartitionSpec as P

HEAD_DIM = 56
CELL_LEN = 384
LANES = 128
WIDE = 256
epsilon = 1e-05
CURVE = 0.7978845608028654
CUBIC = 0.044715
bf16 = jnp.bfloat16
f32 = jnp.float32
MIB = 1024 * 1024


def dot_nn(left, right):
    return lax.dot_general(left, right, (((1,), (0,)), ((), ())), preferred_element_type=f32)


def dot_nt(left, right):
    return lax.dot_general(left, right, (((1,), (1,)), ((), ())), preferred_element_type=f32)


def dot_tn(left, right):
    return lax.dot_general(left, right, (((0,), (0,)), ((), ())), preferred_element_type=f32)


def struct(shape, dtype=bf16):
    return jax.ShapeDtypeStruct(shape, dtype)


CHAIN = []


def in_turn(arguments, first):
    if CHAIN:
        held = lax.optimization_barrier((arguments[first], CHAIN[0]))[0]
        arguments = (*arguments[:first], held, *arguments[first + 1 :])
    return arguments


def call(kernel, name, out_shape, flops, *arguments, scratch=(), scalars=0, limit=14, transcendentals=0):
    results = pl.pallas_call(
        kernel,
        in_specs=[pl.BlockSpec(memory_space=pltpu.SMEM)] * scalars
        + [pl.BlockSpec(memory_space=pltpu.VMEM)] * (len(arguments) - scalars),
        out_specs=[pl.BlockSpec(memory_space=pltpu.VMEM)] * len(out_shape),
        out_shape=out_shape,
        scratch_shapes=scratch,
        compiler_params=pltpu.CompilerParams(vmem_limit_bytes=limit * MIB),

        name=name,
    )(*in_turn(arguments, scalars))
    CHAIN[:] = results[:1]
    return results


def loop(count, step):
    def wrapped(index, carry):
        step(index)
        return carry

    lax.fori_loop(0, count, wrapped, 0)


def lanes_at(index, size):
    return pl.ds(pl.multiple_of(index * size, size), size)


def place_pieces(place, refs, target):
    share = refs[0].shape[0]
    for offset, ref in enumerate(refs):
        slot = lax.bitwise_xor(place, offset)
        target[pl.ds(pl.multiple_of(slot * share, 8), share), :] = ref[...].astype(target.dtype)


def norm_columns(field, gain, shift):
    center = field - jnp.mean(field, 0, keepdims=True)
    spread = jnp.mean(center * center, 0, keepdims=True)
    return center * lax.rsqrt(spread + epsilon) * gain + shift


def front_kernel(
    place_ref, length_ref, own, near, far, both, columns, weight, bias,
    rows_out, normed_out, triple_out, probs_out, context_out, field,
):
    share = context_out.shape[0]
    heads = share // HEAD_DIM
    tokens = rows_out.shape[1]
    place_pieces(place_ref[0], (own, near, far, both), field)

    def norm_step(index):
        lanes = lanes_at(index, LANES)
        value = field[:, lanes]
        rows_out[:, lanes] = value.astype(bf16)
        normed_out[:, lanes] = norm_columns(value, columns[:, 0:1], columns[:, 1:2]).astype(bf16)

    loop(tokens // LANES, norm_step)

    def project_step(index):
        lanes = lanes_at(index, WIDE)
        triple_out[:, lanes] = (dot_nn(weight[...], normed_out[:, lanes]) + bias[...]).astype(bf16)

    loop(tokens // WIDE, project_step)
    factor = HEAD_DIM ** (-0.5)

    def cell_step(cell):
        length = length_ref[cell]
        for head in range(heads):
            start = HEAD_DIM * head
            for block in range(CELL_LEN // LANES):
                span = LANES * (block + 1)
                base = pl.multiple_of(cell * CELL_LEN, LANES)
                here = pl.ds(pl.multiple_of(base + LANES * block, LANES), LANES)
                queries = triple_out[start : start + HEAD_DIM, here]
                keys = triple_out[share + start : share + start + HEAD_DIM, pl.ds(base, span)]
                values = triple_out[2 * share + start : 2 * share + start + HEAD_DIM, pl.ds(base, span)]
                scores = dot_tn(keys, queries) * factor
                key_place = lax.broadcasted_iota(jnp.int32, (span, LANES), 0)
                query_place = lax.broadcasted_iota(jnp.int32, (span, LANES), 1) + LANES * block
                allowed = (key_place <= query_place) & (key_place < length)
                masked = jnp.where(allowed, scores, -1e30)
                expo = jnp.exp(masked - jnp.max(masked, 0, keepdims=True))
                probs = (expo / jnp.sum(expo, 0, keepdims=True)).astype(bf16)
                probs_out[cell, head, :span, LANES * block : span] = probs
                context_out[start : start + HEAD_DIM, here] = dot_nn(values, probs).astype(bf16)

    loop(tokens // CELL_LEN, cell_step)


def front_call(place, lengths, pieces, columns, weight, bias):
    share, tokens = pieces[0].shape
    width = weight.shape[1]
    heads = share // HEAD_DIM
    cells = tokens // CELL_LEN
    pairs = cells * heads * CELL_LEN * CELL_LEN
    return call(
        front_kernel,
        "front",
        [
            struct((width, tokens)),
            struct((width, tokens)),
            struct((3 * share, tokens)),
            struct((cells, heads, CELL_LEN, CELL_LEN)),
            struct((share, tokens)),
        ],
        tokens * width * share * 6 + pairs * HEAD_DIM * 4,
        place, lengths, *pieces, columns, weight, bias,
        scratch=[pltpu.VMEM((width, tokens), f32)],
        scalars=2,
        transcendentals=pairs,
    )


def gate_parts(value):
    square = value * value
    bend = jnp.tanh(CURVE * (value + CUBIC * square * value))
    upper = 0.5 * (1.0 + bend)
    slope = upper + 0.5 * value * (1.0 - bend * bend) * CURVE * (1.0 + 3.0 * CUBIC * square)
    return value * upper, slope


def middle_kernel(
    own, near, far, both, rows_ref, weight, columns, up,
    resid_out, normed_out, hidden_out, slope_out, field,
):
    tokens = resid_out.shape[1]
    share = own.shape[0]
    for place, piece in enumerate((own, near, far, both)):
        field[share * place : share * (place + 1), :] = piece[...].astype(f32)

    def step(index):
        lanes = lanes_at(index, WIDE)
        added = dot_nn(weight[...], field[:, lanes].astype(bf16))
        resid = rows_ref[:, lanes].astype(f32) + added + columns[:, 2:3]
        resid_out[:, lanes] = resid
        normed = norm_columns(resid, columns[:, 3:4], columns[:, 4:5]).astype(bf16)
        normed_out[:, lanes] = normed
        hidden, slope = gate_parts(dot_nn(up[...], normed) + columns[:, 5:6])
        hidden_out[:, lanes] = hidden.astype(bf16)
        slope_out[:, lanes] = slope

    loop(tokens // WIDE, step)


def middle_call(pieces, rows_all, weight, columns, up):
    width, tokens = rows_all.shape
    hidden = up.shape[0]
    return call(
        middle_kernel,
        "middle",
        [
            struct((width, tokens), f32),
            struct((width, tokens)),
            struct((hidden, tokens)),
            struct((hidden, tokens), f32),
        ],
        tokens * width * (width + hidden) * 2,
        *pieces, rows_all, weight, columns, up,
        scratch=[pltpu.VMEM((width, tokens), f32)],
        transcendentals=tokens * hidden,
    )


def spread_kernel(place_ref, own, near, far, both, rows_out, sums_out, field):
    place_pieces(place_ref[0], (own, near, far, both), field)
    rows_out[...] = field[...].astype(bf16)
    sums_out[...] = jnp.sum(field[...], 1, keepdims=True)


def spread_call(place, pieces):
    share, tokens = pieces[0].shape
    return call(
        spread_kernel,
        "spread",
        [struct((4 * share, tokens)), struct((4 * share, 1), f32)],
        4 * share * tokens,
        place, *pieces,
        scratch=[pltpu.VMEM((4 * share, tokens), f32)],
        scalars=1,
    )


def store_halves(bit, value, lanes, keep_out, send_out):
    half = keep_out.shape[0]

    @pl.when(bit == 0)
    def _():
        keep_out[:, lanes] = value[:half]
        send_out[:, lanes] = value[half:]

    @pl.when(bit != 0)
    def _():
        keep_out[:, lanes] = value[half:]
        send_out[:, lanes] = value[:half]


def turn_kernel(
    place_ref, cotangent, slope, down, up, pre_out, keep_out, send_out, sums_out,
):
    tokens = cotangent.shape[1]
    core = lax.rem(place_ref[0], 2)
    sums_out[...] = jnp.zeros_like(sums_out)

    def step(index):
        lanes = lanes_at(index, WIDE)
        pre = dot_nn(down[...], cotangent[:, lanes]) * slope[:, lanes]
        sums_out[...] += jnp.sum(pre, 1, keepdims=True)
        low = pre.astype(bf16)
        pre_out[:, lanes] = low
        store_halves(core, dot_nn(up[...], low).astype(bf16), lanes, keep_out, send_out)

    loop(tokens // WIDE, step)


def turn_call(place, cotangent, slope, down, up):
    width, tokens = cotangent.shape
    hidden = up.shape[1]
    return call(
        turn_kernel,
        "turn",
        [
            struct((hidden, tokens)),
            struct((width // 2, tokens)),
            struct((width // 2, tokens)),
            struct((hidden, 1), f32),
        ],
        tokens * width * hidden * 4,
        place, cotangent, slope, down, up,
        scalars=1,
    )


def norm_back(field, grad, gain):
    center = field - jnp.mean(field, 0, keepdims=True)
    inverse = lax.rsqrt(jnp.mean(center * center, 0, keepdims=True) + epsilon)
    normed = center * inverse
    scaled = grad * gain
    inner = jnp.mean(scaled * normed, 0, keepdims=True)
    back = inverse * (scaled - jnp.mean(scaled, 0, keepdims=True) - normed * inner)
    return normed, back


def add_parts(left, right):
    return (left.astype(f32) + right.astype(f32)).astype(bf16)


def back_kernel(
    place_ref, mine, other, resid, cotangent, columns, out_weight, triple, probs_ref, weight,
    dh_out, low_out, triple_out, keep_out, send_out, sums_out, bias_out,
    grad, context_grad, gain_sum, shift_sum, total_sum,
):
    share = out_weight.shape[0]
    width, tokens = resid.shape
    half = width // 2
    heads = share // HEAD_DIM
    factor = HEAD_DIM ** (-0.5)
    core = lax.rem(place_ref[0], 2)
    grad[pl.ds(pl.multiple_of(core * half, 8), half), :] = mine[...].astype(f32)
    grad[pl.ds(pl.multiple_of((1 - core) * half, 8), half), :] = other[...].astype(f32)
    for item in (gain_sum, shift_sum, total_sum, bias_out):
        item[...] = jnp.zeros_like(item)

    def norm_step(index):
        lanes = lanes_at(index, LANES)
        upper = grad[:, lanes]
        normed, back = norm_back(resid[:, lanes], upper, columns[:, 3:4])
        total = cotangent[:, lanes].astype(f32) + back
        dh_out[:, lanes] = total
        low_out[:, lanes] = total.astype(bf16)
        gain_sum[...] += upper * normed
        shift_sum[...] += upper
        total_sum[...] += total

    loop(tokens // LANES, norm_step)
    sums_out[:, 0:1] = jnp.sum(gain_sum[...], 1, keepdims=True)
    sums_out[:, 1:2] = jnp.sum(shift_sum[...], 1, keepdims=True)
    sums_out[:, 2:3] = jnp.sum(total_sum[...], 1, keepdims=True)

    def context_step(index):
        lanes = lanes_at(index, WIDE)
        context_grad[:, lanes] = dot_nn(out_weight[...], low_out[:, lanes]).astype(bf16)

    loop(tokens // WIDE, context_step)
    blocks = CELL_LEN // LANES

    def cell_step(cell):
        base = pl.multiple_of(cell * CELL_LEN, LANES)
        for head in range(heads):
            start = HEAD_DIM * head
            query_rows = slice(start, start + HEAD_DIM)
            key_rows = slice(share + start, share + start + HEAD_DIM)
            value_rows = slice(2 * share + start, 2 * share + start + HEAD_DIM)
            key_grads = [None] * blocks
            value_grads = [None] * blocks
            query_sum = jnp.zeros((HEAD_DIM, 1), f32)
            value_sum = jnp.zeros((HEAD_DIM, 1), f32)
            for block in range(blocks):
                span = LANES * (block + 1)
                here = pl.ds(pl.multiple_of(base + LANES * block, LANES), LANES)
                queries = triple[query_rows, here]
                keys = triple[key_rows, pl.ds(base, span)]
                values = triple[value_rows, pl.ds(base, span)]
                low = context_grad[query_rows, here]
                probs_low = probs_ref[cell, head, :span, LANES * block : span]
                probs = probs_low.astype(f32)
                prob_grad = dot_tn(values, low)
                inner = jnp.sum(prob_grad * probs, 0, keepdims=True)
                score = (probs * (prob_grad - inner) * factor).astype(bf16)
                query_grad = dot_nn(keys, score)
                query_sum += jnp.sum(query_grad, 1, keepdims=True)
                triple_out[query_rows, here] = query_grad.astype(bf16)
                key_part = dot_nt(queries, score)
                value_part = dot_nt(low, probs_low)
                for place in range(block + 1):
                    lanes = slice(LANES * place, LANES * (place + 1))
                    if key_grads[place] is None:
                        key_grads[place] = key_part[:, lanes]
                        value_grads[place] = value_part[:, lanes]
                    else:
                        key_grads[place] += key_part[:, lanes]
                        value_grads[place] += value_part[:, lanes]
            for block in range(blocks):
                here = pl.ds(pl.multiple_of(base + LANES * block, LANES), LANES)
                triple_out[key_rows, here] = key_grads[block].astype(bf16)
                triple_out[value_rows, here] = value_grads[block].astype(bf16)
                value_sum += jnp.sum(value_grads[block], 1, keepdims=True)
            bias_out[query_rows, 0:1] += query_sum
            bias_out[query_rows, 1:2] += value_sum

    loop(tokens // CELL_LEN, cell_step)

    def part_step(index):
        lanes = lanes_at(index, WIDE)
        part = dot_nn(weight[...], triple_out[:, lanes]).astype(bf16)
        store_halves(core, part, lanes, keep_out, send_out)

    loop(tokens // WIDE, part_step)


def back_call(place, mine, other, resid, cotangent, columns, out_weight, triple, probs, weight):
    width, tokens = resid.shape
    share = out_weight.shape[0]
    cells, heads = probs.shape[:2]
    pairs = cells * heads * CELL_LEN * CELL_LEN
    return call(
        back_kernel,
        "back",
        [
            struct((width, tokens), f32),
            struct((width, tokens)),
            struct((3 * share, tokens)),
            struct((width // 2, tokens)),
            struct((width // 2, tokens)),
            struct((width, 8), f32),
            struct((share, 8), f32),
        ],
        tokens * width * share * 8 + pairs * HEAD_DIM * 8,
        place, mine, other, resid, cotangent, columns, out_weight, triple, probs, weight,
        scratch=[pltpu.VMEM((width, tokens), f32), pltpu.VMEM((share, tokens), bf16)]
        + [pltpu.VMEM((width, LANES), f32)] * 3,
        scalars=1,
    )


def last_kernel(
    place_ref, mine, other, rows_ref, dh, columns, cotangent_sums, pre_sums, back_sums, bias_sums,
    out, sums_out, grad, gain_sum, shift_sum, field,
):
    share, tokens = out.shape
    width = rows_ref.shape[0]
    half = width // 2
    place = place_ref[0]
    core = lax.rem(place, 2)
    grad[pl.ds(pl.multiple_of(core * half, 8), half), :] = mine[...].astype(f32)
    grad[pl.ds(pl.multiple_of((1 - core) * half, 8), half), :] = other[...].astype(f32)
    gain_sum[...] = jnp.zeros_like(gain_sum)
    shift_sum[...] = jnp.zeros_like(shift_sum)

    def norm_step(index):
        lanes = lanes_at(index, LANES)
        upper = grad[:, lanes]
        normed, back = norm_back(rows_ref[:, lanes].astype(f32), upper, columns[:, 0:1])
        field[...] = dh[:, lanes] + back
        out[:, lanes] = field[pl.ds(pl.multiple_of(place * share, 8), share), :].astype(bf16)
        gain_sum[...] += upper * normed
        shift_sum[...] += upper

    loop(tokens // LANES, norm_step)
    field[:, 0:1] = jnp.sum(gain_sum[...], 1, keepdims=True)
    field[:, 1:2] = jnp.sum(shift_sum[...], 1, keepdims=True)
    field[:, 2:3] = cotangent_sums[...]
    field[:, 3:4] = pre_sums[...]
    field[:, 4:7] = back_sums[:, 0:3]
    field[0:share, 7:9] = bias_sums[:, 0:2]
    sums_out[...] = field[...].T[0:16, :]


def last_call(place, mine, other, rows_all, dh, columns, *sums):
    width, tokens = rows_all.shape
    return call(
        last_kernel,
        "last",
        [struct((width // 4, tokens)), struct((16, width), f32)],
        width * tokens * 12,
        place, mine, other, rows_all, dh, columns, *sums,
        scratch=[pltpu.VMEM((width, tokens), f32)] + [pltpu.VMEM((width, LANES), f32)] * 3,
        scalars=1,
    )


def add_kernel(left, right, out):
    out[...] = add_parts(left[...], right[...])


def add_call(left, right):
    return call(add_kernel, "add", [struct(left.shape)], left.size, left, right)[0]


def add_wide_kernel(left, right, out):
    out[...] = left[...] + right[...]


def add_wide_call(left, right):
    return call(add_wide_kernel, "add_wide", [struct(left.shape, f32)], left.size, left, right)[0]


def down_kernel(place_ref, hidden, down, keep_out, send_out):
    tokens = hidden.shape[1]
    share = keep_out.shape[0] // 2
    core = lax.rem(place_ref[0], 2)

    def step(index):
        lanes = lanes_at(index, WIDE)
        part = dot_nn(down[...], hidden[:, lanes]).astype(bf16)
        for chip in range(2):
            rows = slice(share * chip, share * (chip + 1))
            low = part[2 * share * chip : 2 * share * chip + share]
            high = part[2 * share * chip + share : 2 * share * (chip + 1)]

            @pl.when(core == 0)
            def _():
                keep_out[rows, lanes] = low
                send_out[rows, lanes] = high

            @pl.when(core != 0)
            def _():
                keep_out[rows, lanes] = high
                send_out[rows, lanes] = low

    loop(tokens // WIDE, step)


def down_call(place, hidden, down):
    width, inner = down.shape
    tokens = hidden.shape[1]
    return call(
        down_kernel,
        "down",
        [struct((width // 2, tokens))] * 2,
        tokens * width * inner * 2,
        place, hidden, down,
        scalars=1,
    )


def down_add_kernel(place_ref, keep, got, keep_out, send_out, field):
    share = keep_out.shape[0]
    chip = lax.div(place_ref[0], 2)
    field[...] = keep[...].astype(f32) + got[...].astype(f32)
    keep_out[...] = field[pl.ds(pl.multiple_of(chip * share, 8), share), :].astype(bf16)
    send_out[...] = field[pl.ds(pl.multiple_of((1 - chip) * share, 8), share), :].astype(bf16)


def down_add_call(place, keep, got):
    rows, tokens = keep.shape
    return call(
        down_add_kernel,
        "down_add",
        [struct((rows // 2, tokens))] * 2,
        keep.size,
        place, keep, got,
        scratch=[pltpu.VMEM(keep.shape, f32)],
        scalars=1,
    )


def layer_out_kernel(place_ref, keep, got, resid, columns, out):
    share = out.shape[0]
    rows = pl.ds(pl.multiple_of(place_ref[0] * share, 8), share)
    total = keep[...].astype(f32) + got[...].astype(f32)
    out[...] = (resid[rows, :] + total + columns[rows, 6:7]).astype(bf16)


def layer_out_call(place, keep, got, resid, columns):
    return call(
        layer_out_kernel,
        "layer_out",
        [struct(keep.shape)],
        keep.size,
        place, keep, got, resid, columns,
        scalars=1,
    )[0]


def grad_kernel(place_ref, *refs):
    pairs, (keep_out, send_out, line_out) = refs[:-3], refs[-3:]
    side = lax.rem(place_ref[0], 2)
    quarter = keep_out.shape[0]
    width = keep_out.shape[1]
    for begin in range(0, width, 384):
        lanes = slice(begin, min(begin + 384, width))
        parts = []
        for left, right in zip(pairs[0::2], pairs[1::2]):
            parts.append(dot_nt(left[...], right[lanes, :]).astype(bf16))
        value = parts[0] if len(parts) == 1 else jnp.concatenate(parts, 0)
        store_halves(side, value[: 2 * quarter], lanes, keep_out, send_out)
        line_out[:, lanes] = value[2 * quarter :]


def grad_call(dp_place, *pairs):
    rows = sum(item.shape[0] for item in pairs[0::2])
    tokens = pairs[0].shape[1]
    width = pairs[1].shape[0]
    return call(
        grad_kernel,
        "grad",
        [struct((rows // 4, width)), struct((rows // 4, width)), struct((rows // 2, width))],
        2 * rows * tokens * width,
        dp_place, *pairs,
        scalars=1,
    )


def first_hop_kernel(dp_ref, keep, got, line, line_got, out, line_keep, line_send):
    upper = lax.div(dp_ref[0], dp_ref[1])
    out[...] = add_parts(keep[...], got[...])
    value = add_parts(line[...], line_got[...])
    store_halves(upper, value, slice(None), line_keep, line_send)


def first_hop_call(dp, keep, got, line, line_got):
    return call(
        first_hop_kernel,
        "first_hop",
        [struct(keep.shape)] * 3,
        keep.size * 3,
        dp, keep, got, line, line_got,
        scalars=1,
    )


def next_hop_kernel(left, left_got, right, right_got, left_out, right_out):
    left_out[...] = add_parts(left[...], left_got[...])
    right_out[...] = add_parts(right[...], right_got[...])


def next_hop_call(left, left_got, right, right_got):
    return call(
        next_hop_kernel,
        "next_hop",
        [struct(left.shape)] * 2,
        left.size * 2,
        left, left_got, right, right_got,
    )


def fourth_hop_kernel(dp_ref, left, left_got, right, right_got, left_out, right_out):
    half = right.shape[0]
    low, high = slice(0, half), slice(half, 2 * half)
    end = dp_ref[2]
    upper = lax.div(dp_ref[0], dp_ref[1])

    @pl.when(end == 1)
    def _():
        left_out[...] = left_got[...]

    @pl.when(end == 0)
    def _():
        left_out[...] = left[...]

    @pl.when(upper == 0)
    def _():
        right_out[low, :] = right[...]
        right_out[high, :] = right_got[...]

    @pl.when(upper != 0)
    def _():
        right_out[low, :] = right_got[...]
        right_out[high, :] = right[...]


def fourth_hop_call(dp, left, left_got, right, right_got):
    rows, width = left.shape
    return call(
        fourth_hop_kernel,
        "fourth_hop",
        [struct((rows, width)), struct((2 * rows, width))],
        left.size,
        dp, left, left_got, right, right_got,
        scalars=1,
    )


def final_kernel(dp_ref, left, left_got, right, right_got, *outs):
    side = lax.rem(dp_ref[0], 2)
    end = dp_ref[2]
    quarter = left.shape[0]

    def put(start, ref):
        done = 0
        rows = ref.shape[0]
        for out in outs:
            size = out.shape[0]
            low, high = max(start, done), min(start + rows, done + size)
            if low < high:
                out[low - done : high - done, :] = ref[low - start : high - start, :].astype(f32)
            done += size

    @pl.when(side == 0)
    def _():
        put(0, left)
        put(quarter, left_got)

    @pl.when(side != 0)
    def _():
        put(0, left_got)
        put(quarter, left)

    @pl.when(end == 1)
    def _():
        put(2 * quarter, right_got)

    @pl.when(end == 0)
    def _():
        put(2 * quarter, right)


def final_call(dp, left, left_got, right, right_got, sizes):
    width = left.shape[1]
    return call(
        final_kernel,
        "final",
        [struct((size, width), f32) for size in sizes],
        left.size,
        dp, left, left_got, right, right_got,
        scalars=1,
    )


def swap_core(value):
    return lax.ppermute(value, "tensor", [(place, place ^ 1) for place in range(4)])


def swap_chip(value):
    return lax.ppermute(value, "tensor", [(place, place ^ 2) for place in range(4)])


def after(value, *others):
    return lax.optimization_barrier((value, *others))[0]


def all_pieces(share):
    far = swap_chip(share)
    return share, swap_core(share), far, swap_core(far)


def ordered(bit, mine, other, axis):
    low = jnp.where(bit == 0, mine, other)
    high = jnp.where(bit == 0, other, mine)
    return jnp.concatenate([low, high], axis)


def line_pairs(pairs):
    return [(2 * source + side, 2 * target + side) for source, target in pairs for side in (0, 1)]


INWARD = line_pairs([(0, 1), (3, 2)])
MIDDLE = line_pairs([(1, 2), (2, 1)])
OUTWARD = line_pairs([(1, 0), (2, 3)])
ACROSS = [(place, place ^ 1) for place in range(8)]
ACROSS_MIDDLE = [(2, 3), (3, 2), (4, 5), (5, 4)]


def hop(value, pairs):
    return lax.ppermute(value, "dp", pairs)


class CellSum:
    def __init__(self, groups, dp, parts, sizes):
        self.groups, self.dp, self.parts, self.sizes = groups, dp, parts, sizes
        self.stage = 0
        self.send()

    def send(self):
        if self.groups != 8:
            return
        if self.stage == 0:
            keep, send, line = self.parts
            self.got = hop(send, ACROSS), hop(line, INWARD)
        elif self.stage == 1:
            self.got = hop(self.parts[0], INWARD), hop(self.parts[2], MIDDLE)
        elif self.stage == 2:
            self.got = hop(self.parts[0], MIDDLE), hop(self.parts[1], ACROSS_MIDDLE)
        elif self.stage == 3:
            self.got = hop(self.parts[0], OUTWARD), hop(self.parts[1], MIDDLE)
        else:
            self.got = hop(self.parts[0], ACROSS), hop(self.parts[1], OUTWARD)

    def step(self):
        self.stage += 1
        if self.groups != 8:
            return self.plain() if self.stage == 5 else None
        if self.stage == 5:
            left, right = self.parts
            return final_call(self.dp, left, self.got[0], right, self.got[1], self.sizes)
        if self.stage == 1:
            keep, _, line = self.parts
            self.parts = first_hop_call(self.dp, keep, self.got[0], line, self.got[1])
        elif self.stage == 4:
            left, right = self.parts
            self.parts = fourth_hop_call(self.dp, left, self.got[0], right, self.got[1])
        else:
            left, right = self.parts[:2]
            self.parts = next_hop_call(left, self.got[0], right, self.got[1])
        self.send()

    def plain(self):
        keep, send, line = self.parts
        value = jnp.concatenate([ordered(self.dp[0] % 2, keep, send, 0), line], 0)
        value = lax.psum(value, "dp").astype(f32)
        ends = [sum(self.sizes[: place + 1]) for place in range(len(self.sizes))]
        return [value[end - size : end] for end, size in zip(ends, self.sizes)]


def body(
    groups,
    tokens,
    first_gain,
    first_shift,
    triple_weight,
    triple_bias,
    output_weight,
    output_bias,
    second_gain,
    second_shift,
    up_weight,
    up_bias,
    down_weight,
    down_bias,
    cotangent,
    lengths,
):
    share = tokens.shape[1]
    width = triple_weight.shape[0]
    index = lax.axis_index("tensor").astype(jnp.int32)
    core, chip = index % 2, index // 2
    place = index.reshape(1)
    row = lax.axis_index("dp").astype(jnp.int32)
    at_end = ((row < 2) | (row >= groups - 2)).astype(jnp.int32)
    dp = jnp.stack([row, jnp.int32(groups // 2), at_end])
    CHAIN.clear()
    token_pieces = all_pieces(tokens.T)
    triple_t = triple_weight.transpose(1, 2, 0).reshape(3 * share, width)
    bias_flat = jnp.concatenate([triple_bias[0], jnp.zeros((share,), f32), triple_bias[1]])
    columns = jnp.stack(
        [first_gain, first_shift, output_bias, second_gain, second_shift, up_bias, down_bias], 1
    )
    up_t, triple_plain = up_weight.T, triple_t.T
    own = lax.optimization_barrier((token_pieces[0], up_t, triple_plain, columns))
    up_t, triple_plain, columns = own[1:]
    token_pieces = (own[0], *token_pieces[1:])
    weight_near = swap_core(output_weight)
    weight_far = swap_chip(after(output_weight, token_pieces[2]))
    rows_all, first_normed, triple, probs, context = front_call(
        place, lengths, token_pieces, columns, triple_t, bias_flat[:, None]
    )
    context_far = swap_chip(context)
    context_near = swap_core(context)
    weight_both = swap_core(weight_far)
    weight_full = jnp.concatenate([output_weight, weight_near, weight_far, weight_both], 0)
    weight_full = after(weight_full, context).T
    down_t = after(down_weight, context).T
    context_far, weight_full, down_t = lax.optimization_barrier((context_far, weight_full, down_t))
    cotangent_pieces = all_pieces(after(cotangent.T, context_far))
    resid, second_normed, hidden, slope = middle_call(
        (context, context_near, context_far, swap_core(context_far)), rows_all, weight_full, columns, up_t
    )
    grad_rows, cotangent_sums = spread_call(place, cotangent_pieces)
    down_sum = CellSum(groups, dp, grad_call(dp, hidden, grad_rows), [width])
    pre_low, keep, send, pre_sums = turn_call(place, grad_rows, slope, down_weight, up_weight)
    near = swap_core(send)
    down_keep, down_send = down_call(place, hidden, down_t)
    down_got = swap_core(down_send)
    near = add_call(keep, near)
    far = swap_chip(near)
    up_parts = grad_call(dp, second_normed, pre_low)
    down_sum.step()
    up_sum = CellSum(groups, dp, up_parts, [width])
    mine = add_call(near, far)
    other = swap_core(mine)
    dh, low, triple_low, keep, send, back_sums, bias_sums = back_call(
        place, mine, other, resid, grad_rows, columns, output_weight, triple, probs, triple_plain
    )
    near = swap_core(send)
    down_sum.step()
    near = add_call(keep, near)
    far = swap_chip(near)
    rest_parts = grad_call(dp, triple_low, first_normed, context, low)
    down_sum.step()
    rest_sum = CellSum(groups, dp, rest_parts, [3 * share, share])
    up_sum.step()
    mine = add_call(near, far)
    other = swap_core(mine)
    down_keep, down_send = down_add_call(place, down_keep, down_got)
    down_got = swap_chip(down_send)
    input_grad, small = last_call(
        place, mine, other, rows_all, dh, columns, cotangent_sums, pre_sums, back_sums, bias_sums
    )
    if groups == 8:
        got = hop(small, ACROSS)
        down_sum.step()
        small = add_wide_call(small, got)
        got = hop(small, [(spot, spot ^ 4) for spot in range(8)])
        up_sum.step()
        layer_out = layer_out_call(place, down_keep, down_got, resid, columns)
        small = add_wide_call(small, got)
        got = hop(small, [(spot, spot ^ 2) for spot in range(8)])
        rest_sum.step()
        small = add_wide_call(small, got)
    else:
        layer_out = layer_out_call(place, down_keep, down_got, resid, columns)
        small = lax.psum(small, "dp")
        down_sum.step()
        up_sum.step()
        rest_sum.step()
    up_sum.step()
    rest_sum.step()
    down_grad = down_sum.step()[0]
    up_sum.step()
    rest_sum.step()
    up_grad = up_sum.step()[0]
    rest_sum.step()
    triple_grad, output_grad = rest_sum.step()
    triple_grad = triple_grad.reshape(3, share, width).transpose(2, 0, 1)
    return (
        layer_out.T,
        input_grad.T,
        small[0],
        small[1],
        triple_grad,
        small[7:9, :share],
        output_grad,
        small[6],
        small[4],
        small[5],
        up_grad,
        small[3],
        down_grad,
        small[2],
    )


def solution(mesh):
    placed = (
        P("dp", "tensor"),
        P(),
        P(),
        P(None, None, "tensor"),
        P(None, "tensor"),
        P("tensor", None),
        P(),
        P(),
        P(),
        P(None, "tensor"),
        P("tensor"),
        P("tensor", None),
        P(),
        P("dp", "tensor"),
        P("dp"),
    )
    return jax.shard_map(
        functools.partial(body, mesh.shape["dp"]),
        mesh=mesh,
        in_specs=placed,
        out_specs=(
            P("dp", "tensor"),
            P("dp", "tensor"),
            P(),
            P(),
            P(None, None, "tensor"),
            P(None, "tensor"),
            P("tensor", None),
            P(),
            P(),
            P(),
            P(None, "tensor"),
            P("tensor"),
            P("tensor", None),
            P(),
        ),
        check_vma=False,
    )
```

```python
import functools

import jax
import jax.numpy as jnp
from jax import lax
from jax.experimental import pallas as pl
from jax.experimental.pallas import tpu as pltpu
from jax.sharding import PartitionSpec as P

HEAD_DIM = 56
CELL_LEN = 384
LANES = 128
WIDE = 256
epsilon = 1e-05
CURVE = 0.7978845608028654
CUBIC = 0.044715
bf16 = jnp.bfloat16
f32 = jnp.float32
MIB = 1024 * 1024
SMALL = 6


def dot_nn(left, right):
    return lax.dot_general(left, right, (((1,), (0,)), ((), ())), preferred_element_type=f32)


def dot_nt(left, right):
    return lax.dot_general(left, right, (((1,), (1,)), ((), ())), preferred_element_type=f32)


def dot_tn(left, right):
    return lax.dot_general(left, right, (((0,), (0,)), ((), ())), preferred_element_type=f32)


def struct(shape, dtype=bf16):
    return jax.ShapeDtypeStruct(shape, dtype)


CHAIN = []


def in_turn(arguments, first):
    if CHAIN:
        held = lax.optimization_barrier((arguments[first], CHAIN[0]))[0]
        arguments = (*arguments[:first], held, *arguments[first + 1 :])
    return arguments


def call(kernel, name, out_shape, flops, *arguments, scratch=(), scalars=0, limit=12, transcendentals=0):
    results = pl.pallas_call(
        kernel,
        in_specs=[pl.BlockSpec(memory_space=pltpu.SMEM)] * scalars
        + [pl.BlockSpec(memory_space=pltpu.VMEM)] * (len(arguments) - scalars),
        out_specs=[pl.BlockSpec(memory_space=pltpu.VMEM)] * len(out_shape),
        out_shape=out_shape,
        scratch_shapes=scratch,
        compiler_params=pltpu.CompilerParams(vmem_limit_bytes=limit * MIB),
        name=name,
    )(*in_turn(arguments, scalars))
    CHAIN[:] = results[:1]
    return results


def loop(count, step):
    def wrapped(index, carry):
        step(index)
        return carry

    lax.fori_loop(0, count, wrapped, 0)


def lanes_at(index, size):
    return pl.ds(pl.multiple_of(index * size, size), size)


def place_pieces(place, refs, target):
    share = refs[0].shape[0]
    for offset, ref in enumerate(refs):
        slot = lax.bitwise_xor(place, offset)
        target[pl.ds(pl.multiple_of(slot * share, 8), share), :] = ref[...].astype(target.dtype)


def norm_columns(field, gain, shift):
    center = field - jnp.mean(field, 0, keepdims=True)
    spread = jnp.mean(center * center, 0, keepdims=True)
    return center * lax.rsqrt(spread + epsilon) * gain + shift


def front_kernel(
    place_ref, length_ref, own, near, far, both, columns, weight, bias,
    rows_out, normed_out, triple_out, probs_out, context_out, field,
):
    share = context_out.shape[0]
    heads = share // HEAD_DIM
    tokens = rows_out.shape[1]
    place_pieces(place_ref[0], (own, near, far, both), field)

    def norm_step(index):
        lanes = lanes_at(index, LANES)
        value = field[:, lanes]
        rows_out[:, lanes] = value.astype(bf16)
        normed_out[:, lanes] = norm_columns(value, columns[:, 0:1], columns[:, 1:2]).astype(bf16)

    loop(tokens // LANES, norm_step)

    def project_step(index):
        lanes = lanes_at(index, WIDE)
        triple_out[:, lanes] = (dot_nn(weight[...], normed_out[:, lanes]) + bias[...]).astype(bf16)

    loop(tokens // WIDE, project_step)
    factor = HEAD_DIM ** (-0.5)

    def cell_step(cell):
        length = length_ref[cell]
        for head in range(heads):
            start = HEAD_DIM * head
            for block in range(CELL_LEN // LANES):
                span = LANES * (block + 1)
                base = pl.multiple_of(cell * CELL_LEN, LANES)
                here = pl.ds(pl.multiple_of(base + LANES * block, LANES), LANES)
                queries = triple_out[start : start + HEAD_DIM, here]
                keys = triple_out[share + start : share + start + HEAD_DIM, pl.ds(base, span)]
                values = triple_out[2 * share + start : 2 * share + start + HEAD_DIM, pl.ds(base, span)]
                scores = dot_tn(keys, queries) * factor
                key_place = lax.broadcasted_iota(jnp.int32, (span, LANES), 0)
                query_place = lax.broadcasted_iota(jnp.int32, (span, LANES), 1) + LANES * block
                allowed = (key_place <= query_place) & (key_place < length)
                masked = jnp.where(allowed, scores, -1e30)
                expo = jnp.exp(masked - jnp.max(masked, 0, keepdims=True))
                probs = (expo / jnp.sum(expo, 0, keepdims=True)).astype(bf16)
                probs_out[cell, head, :span, LANES * block : span] = probs
                context_out[start : start + HEAD_DIM, here] = dot_nn(values, probs).astype(bf16)

    loop(tokens // CELL_LEN, cell_step)


def front_call(place, lengths, pieces, columns, weight, bias):
    share, tokens = pieces[0].shape
    width = weight.shape[1]
    heads = share // HEAD_DIM
    cells = tokens // CELL_LEN
    pairs = cells * heads * CELL_LEN * CELL_LEN
    return call(
        front_kernel,
        "front",
        [
            struct((width, tokens)),
            struct((width, tokens)),
            struct((3 * share, tokens)),
            struct((cells, heads, CELL_LEN, CELL_LEN)),
            struct((share, tokens)),
        ],
        tokens * width * share * 6 + pairs * HEAD_DIM * 4,
        place, lengths, *pieces, columns, weight, bias,
        scratch=[pltpu.VMEM((width, tokens), f32)],
        scalars=2,
        transcendentals=pairs,
    )


def gate_parts(value):
    square = value * value
    bend = jnp.tanh(CURVE * (value + CUBIC * square * value))
    upper = 0.5 * (1.0 + bend)
    slope = upper + 0.5 * value * (1.0 - bend * bend) * CURVE * (1.0 + 3.0 * CUBIC * square)
    return value * upper, slope


def middle_kernel(
    own, near, far, both, own_weight, near_weight, far_weight, both_weight, rows_ref, columns, up,
    resid_out, normed_out, hidden_out, slope_out, field, weight,
):
    tokens = resid_out.shape[1]
    share = own.shape[0]
    for place, piece in enumerate((own, near, far, both)):
        field[share * place : share * (place + 1), :] = piece[...].astype(f32)
    for place, piece in enumerate((own_weight, near_weight, far_weight, both_weight)):
        weight[:, share * place : share * (place + 1)] = piece[...]

    def step(index):
        lanes = lanes_at(index, WIDE)
        added = dot_nn(weight[...], field[:, lanes].astype(bf16))
        resid = rows_ref[:, lanes].astype(f32) + added + columns[:, 2:3]
        resid_out[:, lanes] = resid
        normed = norm_columns(resid, columns[:, 3:4], columns[:, 4:5]).astype(bf16)
        normed_out[:, lanes] = normed
        hidden, slope = gate_parts(dot_nn(up[...], normed) + columns[:, 5:6])
        hidden_out[:, lanes] = hidden.astype(bf16)
        slope_out[:, lanes] = slope

    loop(tokens // WIDE, step)


def middle_call(pieces, weights, rows_all, columns, up):
    width, tokens = rows_all.shape
    hidden = up.shape[0]
    return call(
        middle_kernel,
        "middle",
        [
            struct((width, tokens), f32),
            struct((width, tokens)),
            struct((hidden, tokens)),
            struct((hidden, tokens), f32),
        ],
        tokens * width * (width + hidden) * 2,
        *pieces, *weights, rows_all, columns, up,
        scratch=[pltpu.VMEM((width, tokens), f32), pltpu.VMEM((width, width), bf16)],
        transcendentals=tokens * hidden,
    )


def spread_kernel(place_ref, own, near, far, both, rows_out, sums_out, field):
    place_pieces(place_ref[0], (own, near, far, both), field)
    rows_out[...] = field[...].astype(bf16)
    sums_out[...] = jnp.sum(field[...], 1, keepdims=True)


def spread_call(place, pieces):
    share, tokens = pieces[0].shape
    return call(
        spread_kernel,
        "spread",
        [struct((4 * share, tokens)), struct((4 * share, 1), f32)],
        4 * share * tokens,
        place, *pieces,
        scratch=[pltpu.VMEM((4 * share, tokens), f32)],
        scalars=1,
    )


def store_halves(bit, value, lanes, keep_out, send_out):
    half = keep_out.shape[0]

    @pl.when(bit == 0)
    def _():
        keep_out[:, lanes] = value[:half]
        send_out[:, lanes] = value[half:]

    @pl.when(bit != 0)
    def _():
        keep_out[:, lanes] = value[half:]
        send_out[:, lanes] = value[:half]


def turn_kernel(
    place_ref, cotangent, slope, down, up, pre_out, keep_out, send_out, sums_out,
):
    tokens = cotangent.shape[1]
    core = lax.rem(place_ref[0], 2)
    sums_out[...] = jnp.zeros_like(sums_out)

    def step(index):
        lanes = lanes_at(index, WIDE)
        pre = dot_nn(down[...], cotangent[:, lanes]) * slope[:, lanes]
        sums_out[...] += jnp.sum(pre, 1, keepdims=True)
        low = pre.astype(bf16)
        pre_out[:, lanes] = low
        store_halves(core, dot_nn(up[...], low).astype(bf16), lanes, keep_out, send_out)

    loop(tokens // WIDE, step)


def turn_call(place, cotangent, slope, down, up):
    width, tokens = cotangent.shape
    hidden = up.shape[1]
    return call(
        turn_kernel,
        "turn",
        [
            struct((hidden, tokens)),
            struct((width // 2, tokens)),
            struct((width // 2, tokens)),
            struct((hidden, 1), f32),
        ],
        tokens * width * hidden * 4,
        place, cotangent, slope, down, up,
        scalars=1,
    )


def norm_back(field, grad, gain):
    center = field - jnp.mean(field, 0, keepdims=True)
    inverse = lax.rsqrt(jnp.mean(center * center, 0, keepdims=True) + epsilon)
    normed = center * inverse
    scaled = grad * gain
    inner = jnp.mean(scaled * normed, 0, keepdims=True)
    back = inverse * (scaled - jnp.mean(scaled, 0, keepdims=True) - normed * inner)
    return normed, back


def add_parts(left, right):
    return (left.astype(f32) + right.astype(f32)).astype(bf16)


def back_kernel(
    place_ref, mine, other, resid, cotangent, columns, out_weight, triple, probs_ref, weight,
    dh_out, low_out, triple_out, keep_out, send_out, sums_out, bias_out,
    grad, context_grad, gain_sum, shift_sum, total_sum,
):
    share = out_weight.shape[0]
    width, tokens = resid.shape
    half = width // 2
    heads = share // HEAD_DIM
    factor = HEAD_DIM ** (-0.5)
    core = lax.rem(place_ref[0], 2)
    grad[pl.ds(pl.multiple_of(core * half, 8), half), :] = mine[...].astype(f32)
    grad[pl.ds(pl.multiple_of((1 - core) * half, 8), half), :] = other[...].astype(f32)
    for item in (gain_sum, shift_sum, total_sum, bias_out):
        item[...] = jnp.zeros_like(item)

    def norm_step(index):
        lanes = lanes_at(index, LANES)
        upper = grad[:, lanes]
        normed, back = norm_back(resid[:, lanes], upper, columns[:, 3:4])
        total = cotangent[:, lanes].astype(f32) + back
        dh_out[:, lanes] = total
        low_out[:, lanes] = total.astype(bf16)
        gain_sum[...] += upper * normed
        shift_sum[...] += upper
        total_sum[...] += total

    loop(tokens // LANES, norm_step)
    sums_out[:, 0:1] = jnp.sum(gain_sum[...], 1, keepdims=True)
    sums_out[:, 1:2] = jnp.sum(shift_sum[...], 1, keepdims=True)
    sums_out[:, 2:3] = jnp.sum(total_sum[...], 1, keepdims=True)

    def context_step(index):
        lanes = lanes_at(index, WIDE)
        context_grad[:, lanes] = dot_nn(out_weight[...], low_out[:, lanes]).astype(bf16)

    loop(tokens // WIDE, context_step)
    blocks = CELL_LEN // LANES

    def cell_step(cell):
        base = pl.multiple_of(cell * CELL_LEN, LANES)
        for head in range(heads):
            start = HEAD_DIM * head
            query_rows = slice(start, start + HEAD_DIM)
            key_rows = slice(share + start, share + start + HEAD_DIM)
            value_rows = slice(2 * share + start, 2 * share + start + HEAD_DIM)
            key_grads = [None] * blocks
            value_grads = [None] * blocks
            query_sum = jnp.zeros((HEAD_DIM, 1), f32)
            value_sum = jnp.zeros((HEAD_DIM, 1), f32)
            for block in range(blocks):
                span = LANES * (block + 1)
                here = pl.ds(pl.multiple_of(base + LANES * block, LANES), LANES)
                queries = triple[query_rows, here]
                keys = triple[key_rows, pl.ds(base, span)]
                values = triple[value_rows, pl.ds(base, span)]
                low = context_grad[query_rows, here]
                probs_low = probs_ref[cell, head, :span, LANES * block : span]
                probs = probs_low.astype(f32)
                prob_grad = dot_tn(values, low)
                inner = jnp.sum(prob_grad * probs, 0, keepdims=True)
                score = (probs * (prob_grad - inner) * factor).astype(bf16)
                query_grad = dot_nn(keys, score)
                query_sum += jnp.sum(query_grad, 1, keepdims=True)
                triple_out[query_rows, here] = query_grad.astype(bf16)
                key_part = dot_nt(queries, score)
                value_part = dot_nt(low, probs_low)
                for place in range(block + 1):
                    lanes = slice(LANES * place, LANES * (place + 1))
                    if key_grads[place] is None:
                        key_grads[place] = key_part[:, lanes]
                        value_grads[place] = value_part[:, lanes]
                    else:
                        key_grads[place] += key_part[:, lanes]
                        value_grads[place] += value_part[:, lanes]
            for block in range(blocks):
                here = pl.ds(pl.multiple_of(base + LANES * block, LANES), LANES)
                triple_out[key_rows, here] = key_grads[block].astype(bf16)
                triple_out[value_rows, here] = value_grads[block].astype(bf16)
                value_sum += jnp.sum(value_grads[block], 1, keepdims=True)
            bias_out[query_rows, 0:1] += query_sum
            bias_out[query_rows, 1:2] += value_sum

    loop(tokens // CELL_LEN, cell_step)

    def part_step(index):
        lanes = lanes_at(index, WIDE)
        part = dot_nn(weight[...], triple_out[:, lanes]).astype(bf16)
        store_halves(core, part, lanes, keep_out, send_out)

    loop(tokens // WIDE, part_step)


def back_call(place, mine, other, resid, cotangent, columns, out_weight, triple, probs, weight):
    width, tokens = resid.shape
    share = out_weight.shape[0]
    cells, heads = probs.shape[:2]
    pairs = cells * heads * CELL_LEN * CELL_LEN
    return call(
        back_kernel,
        "back",
        [
            struct((width, tokens), f32),
            struct((width, tokens)),
            struct((3 * share, tokens)),
            struct((width // 2, tokens)),
            struct((width // 2, tokens)),
            struct((width, 8), f32),
            struct((share, 8), f32),
        ],
        tokens * width * share * 8 + pairs * HEAD_DIM * 8,
        place, mine, other, resid, cotangent, columns, out_weight, triple, probs, weight,
        scratch=[pltpu.VMEM((width, tokens), f32), pltpu.VMEM((share, tokens), bf16)]
        + [pltpu.VMEM((width, LANES), f32)] * 3,
        scalars=1,
    )


def last_kernel(
    place_ref, mine, other, rows_ref, dh, columns, cotangent_sums, pre_sums, back_sums, bias_sums,
    out, sums_out, grad, gain_sum, shift_sum, field,
):
    share, tokens = out.shape
    width = rows_ref.shape[0]
    half = width // 2
    place = place_ref[0]
    core = lax.rem(place, 2)
    grad[pl.ds(pl.multiple_of(core * half, 8), half), :] = mine[...].astype(f32)
    grad[pl.ds(pl.multiple_of((1 - core) * half, 8), half), :] = other[...].astype(f32)
    gain_sum[...] = jnp.zeros_like(gain_sum)
    shift_sum[...] = jnp.zeros_like(shift_sum)

    def norm_step(index):
        lanes = lanes_at(index, LANES)
        upper = grad[:, lanes]
        normed, back = norm_back(rows_ref[:, lanes].astype(f32), upper, columns[:, 0:1])
        field[...] = dh[:, lanes] + back
        out[:, lanes] = field[pl.ds(pl.multiple_of(place * share, 8), share), :].astype(bf16)
        gain_sum[...] += upper * normed
        shift_sum[...] += upper

    loop(tokens // LANES, norm_step)
    field[:, 0:1] = jnp.sum(gain_sum[...], 1, keepdims=True)
    field[:, 1:2] = jnp.sum(shift_sum[...], 1, keepdims=True)
    field[:, 2:3] = cotangent_sums[...]
    field[:, 3:4] = pre_sums[...]
    field[:, 4:7] = back_sums[:, 0:3]
    field[0:share, 7:9] = bias_sums[:, 0:2]
    sums_out[...] = field[...].T[0:16, :]


def last_call(place, mine, other, rows_all, dh, columns, *sums):
    width, tokens = rows_all.shape
    return call(
        last_kernel,
        "last",
        [struct((width // 4, tokens)), struct((16, width), f32)],
        width * tokens * 12,
        place, mine, other, rows_all, dh, columns, *sums,
        scratch=[pltpu.VMEM((width, tokens), f32)] + [pltpu.VMEM((width, LANES), f32)] * 3,
        scalars=1,
    )


def add_kernel(left, right, out):
    out[...] = add_parts(left[...], right[...])


def add_call(left, right):
    return call(add_kernel, "add", [struct(left.shape)], left.size, left, right, limit=SMALL)[0]


def add_wide_kernel(left, right, out):
    out[...] = left[...] + right[...]


def add_wide_call(left, right):
    return call(add_wide_kernel, "add_wide", [struct(left.shape, f32)], left.size, left, right, limit=SMALL)[0]


def down_kernel(place_ref, hidden, down, keep_out, send_out):
    tokens = hidden.shape[1]
    share = keep_out.shape[0] // 2
    core = lax.rem(place_ref[0], 2)

    def step(index):
        lanes = lanes_at(index, WIDE)
        part = dot_nn(down[...], hidden[:, lanes]).astype(bf16)
        for chip in range(2):
            rows = slice(share * chip, share * (chip + 1))
            low = part[2 * share * chip : 2 * share * chip + share]
            high = part[2 * share * chip + share : 2 * share * (chip + 1)]

            @pl.when(core == 0)
            def _():
                keep_out[rows, lanes] = low
                send_out[rows, lanes] = high

            @pl.when(core != 0)
            def _():
                keep_out[rows, lanes] = high
                send_out[rows, lanes] = low

    loop(tokens // WIDE, step)


def down_call(place, hidden, down):
    width, inner = down.shape
    tokens = hidden.shape[1]
    return call(
        down_kernel,
        "down",
        [struct((width // 2, tokens))] * 2,
        tokens * width * inner * 2,
        place, hidden, down,
        scalars=1,
    )


def down_add_kernel(place_ref, keep, got, keep_out, send_out, field):
    share = keep_out.shape[0]
    chip = lax.div(place_ref[0], 2)
    field[...] = keep[...].astype(f32) + got[...].astype(f32)
    keep_out[...] = field[pl.ds(pl.multiple_of(chip * share, 8), share), :].astype(bf16)
    send_out[...] = field[pl.ds(pl.multiple_of((1 - chip) * share, 8), share), :].astype(bf16)


def down_add_call(place, keep, got):
    rows, tokens = keep.shape
    return call(
        down_add_kernel,
        "down_add",
        [struct((rows // 2, tokens))] * 2,
        keep.size,
        place, keep, got,
        scratch=[pltpu.VMEM(keep.shape, f32)],
        scalars=1,
    )


def layer_out_kernel(place_ref, keep, got, resid, columns, out):
    share = out.shape[0]
    rows = pl.ds(pl.multiple_of(place_ref[0] * share, 8), share)
    total = keep[...].astype(f32) + got[...].astype(f32)
    out[...] = (resid[rows, :] + total + columns[rows, 6:7]).astype(bf16)


def layer_out_call(place, keep, got, resid, columns):
    return call(
        layer_out_kernel,
        "layer_out",
        [struct(keep.shape)],
        keep.size,
        place, keep, got, resid, columns,
        scalars=1,
    )[0]


def grad_kernel(ranges, place_ref, *refs):
    pairs, (keep_out, send_out) = refs[:-2], refs[-2:]
    side = lax.rem(place_ref[0], 2)
    width = keep_out.shape[1]
    for begin in range(0, width, 384):
        lanes = slice(begin, min(begin + 384, width))
        parts = []
        for left, right, (low, high) in zip(pairs[0::2], pairs[1::2], ranges):
            parts.append(dot_nt(left[low:high, :], right[lanes, :]).astype(bf16))
        value = parts[0] if len(parts) == 1 else jnp.concatenate(parts, 0)
        store_halves(side, value, lanes, keep_out, send_out)


def grad_call(dp_place, ranges, *pairs):
    rows = sum(high - low for low, high in ranges)
    tokens = pairs[0].shape[1]
    width = pairs[1].shape[0]
    return call(
        functools.partial(grad_kernel, ranges),
        "grad",
        [struct((rows // 2, width)), struct((rows // 2, width))],
        2 * rows * tokens * width,
        dp_place, *pairs,
        scalars=1,
    )


def settle_kernel(dp_ref, mine, got, out):
    @pl.when(dp_ref[2] == 1)
    def _():
        out[...] = got[...]

    @pl.when(dp_ref[2] == 0)
    def _():
        out[...] = mine[...]


def settle_call(dp, mine, got):
    return call(settle_kernel, "settle", [struct(mine.shape)], mine.size, dp, mine, got, scalars=1, limit=SMALL)[0]


def final_kernel(count, dp_ref, *refs):
    side = lax.rem(dp_ref[0], 2)
    outs = refs[2 * count :]

    def put(start, ref):
        done = 0
        rows = ref.shape[0]
        for out in outs:
            size = out.shape[0]
            low, high = max(start, done), min(start + rows, done + size)
            if low < high:
                out[low - done : high - done, :] = ref[low - start : high - start, :].astype(f32)
            done += size

    base = 0
    for place in range(count):
        mine, got = refs[2 * place : 2 * place + 2]
        half = mine.shape[0]

        @pl.when(side == 0)
        def _():
            put(base, mine)
            put(base + half, got)

        @pl.when(side != 0)
        def _():
            put(base, got)
            put(base + half, mine)

        base += 2 * half


def final_call(dp, parts, sizes):
    width = parts[0].shape[1]
    return call(
        functools.partial(final_kernel, len(parts) // 2),
        "final",
        [struct((size, width), f32) for size in sizes],
        sum(sizes) * width,
        dp, *parts,
        scalars=1,
        limit=SMALL,
    )


def swap_core(value):
    return lax.ppermute(value, "tensor", [(place, place ^ 1) for place in range(4)])


def swap_chip(value):
    return lax.ppermute(value, "tensor", [(place, place ^ 2) for place in range(4)])


def after(value, *others):
    return lax.optimization_barrier((value, *others))[0]


def all_pieces(share):
    far = swap_chip(share)
    return share, swap_core(share), far, swap_core(far)


def ordered(bit, mine, other, axis):
    low = jnp.where(bit == 0, mine, other)
    high = jnp.where(bit == 0, other, mine)
    return jnp.concatenate([low, high], axis)


def line_pairs(pairs):
    return [(2 * source + side, 2 * target + side) for source, target in pairs for side in (0, 1)]


INWARD = line_pairs([(0, 1), (3, 2)])
MIDDLE = line_pairs([(1, 2), (2, 1)])
OUTWARD = line_pairs([(1, 0), (2, 3)])
ACROSS = [(place, place ^ 1) for place in range(8)]
ACROSS_MIDDLE = [(2, 3), (3, 2), (4, 5), (5, 4)]


def hop(value, pairs):
    return lax.ppermute(value, "dp", pairs)


STAGES = (ACROSS, INWARD, MIDDLE, OUTWARD, ACROSS)


class CellSum:
    def __init__(self, groups, dp, parts):
        self.groups, self.dp = groups, dp
        self.mine, self.got = parts
        self.stage = -1

    def step(self):
        self.stage += 1
        if self.groups != 8:
            return
        send = self.got
        if self.stage == 4:
            send = self.mine = settle_call(self.dp, self.mine, self.got)
        elif self.stage > 0:
            send = self.mine = add_call(self.mine, self.got)
        self.got = hop(send, STAGES[self.stage])

    def plain(self):
        value = ordered(self.dp[0] % 2, self.mine, self.got, 0)
        return lax.psum(value, "dp").astype(f32)


def finish(sums, sizes):
    if sums[0].groups == 8:
        return final_call(sums[0].dp, [piece for item in sums for piece in (item.mine, item.got)], sizes)
    value = jnp.concatenate([item.plain() for item in sums], 0)
    ends = [sum(sizes[: place + 1]) for place in range(len(sizes))]
    return [value[end - size : end] for end, size in zip(ends, sizes)]


def end_round(sums, *values):
    held = lax.optimization_barrier((*[item.got for item in sums], *values))
    for item, got in zip(sums, held):
        item.got = got
    return held[len(sums) :]


def body(
    groups,
    tokens,
    first_gain,
    first_shift,
    triple_weight,
    triple_bias,
    output_weight,
    output_bias,
    second_gain,
    second_shift,
    up_weight,
    up_bias,
    down_weight,
    down_bias,
    cotangent,
    lengths,
):
    share = tokens.shape[1]
    width = triple_weight.shape[0]
    index = lax.axis_index("tensor").astype(jnp.int32)
    core, chip = index % 2, index // 2
    place = index.reshape(1)
    row = lax.axis_index("dp").astype(jnp.int32)
    at_end = ((row < 2) | (row >= groups - 2)).astype(jnp.int32)
    dp = jnp.stack([row, jnp.int32(groups // 2), at_end])
    CHAIN.clear()
    fence = lambda *values: lax.optimization_barrier(values)
    token_own, grad_own = tokens.T, cotangent.T
    token_far, token_near = swap_chip(token_own), swap_core(token_own)
    grad_near, weight_near = swap_core(grad_own), swap_core(output_weight)
    triple_t = triple_weight.transpose(1, 2, 0).reshape(3 * share, width)
    bias_flat = jnp.concatenate([triple_bias[0], jnp.zeros((share,), f32), triple_bias[1]])[:, None]
    columns = jnp.stack(
        [first_gain, first_shift, output_bias, second_gain, second_shift, up_bias, down_bias], 1
    )
    up_t, triple_plain = up_weight.T, triple_t.T
    token_far, token_near, up_t, triple_plain, columns, bias_flat, out_weight = fence(
        token_far, token_near, up_t, triple_plain, columns, bias_flat, output_weight
    )
    token_both = swap_core(token_far)
    weight_far = swap_chip(out_weight)
    own_t = out_weight.T
    token_both, own_t = fence(token_both, own_t)
    rows_all, first_normed, triple, probs, context = front_call(
        place, lengths, (token_own, token_near, token_far, token_both), columns, triple_t, bias_flat
    )
    context_far, context_near = swap_chip(context), swap_core(context)
    weight_far, weight_near, down_plain, _ = fence(weight_far, weight_near, down_weight, context)
    weight_both = swap_core(weight_far)
    weights = own_t, weight_near.T, weight_far.T, weight_both.T
    down_t = down_plain.T
    context_far, context_near, down_t, grad_own, *weights = fence(
        context_far, context_near, down_t, grad_own, *weights
    )
    context_both = swap_core(context_far)
    grad_far = swap_chip(grad_own)
    resid, second_normed, hidden, slope = middle_call(
        (context, context_near, context_far, context_both), weights, rows_all, columns, up_t
    )
    grad_far, _ = fence(grad_far, second_normed)
    grad_both = swap_core(grad_far)
    grad_rows, cotangent_sums = spread_call(place, (grad_own, grad_near, grad_far, grad_both))
    half = width // 2

    def cell_sum(ranges, *pairs):
        return CellSum(groups, dp, grad_call(dp, ranges, *pairs))

    down_low = cell_sum([(0, half)], hidden, grad_rows)
    down_low.step()
    down_high = cell_sum([(half, width)], hidden, grad_rows)
    pre_low, keep, send, pre_sums = turn_call(place, grad_rows, slope, down_weight, up_weight)
    near = swap_core(send)
    down_keep, down_send = down_call(place, hidden, down_t)
    near, down_keep, down_send = end_round([down_low], near, down_keep, down_send)
    near = add_call(keep, near)
    far = swap_chip(near)
    down_low.step()
    down_high.step()
    down_got = swap_core(down_send)
    up_low = cell_sum([(0, half)], second_normed, pre_low)
    up_high = cell_sum([(half, width)], second_normed, pre_low)
    far, down_got, near, _ = end_round([down_low, down_high], far, down_got, near, up_high.mine)
    mine = add_call(near, far)
    other = swap_core(mine)
    for item in (down_low, down_high, up_low):
        item.step()
    dh, low, triple_low, keep, send, back_sums, bias_sums = back_call(
        place, mine, other, resid, grad_rows, columns, output_weight, triple, probs, triple_plain
    )
    keep, send = end_round([down_low, down_high, up_low], keep, send)
    near = swap_core(send)
    for item in (down_low, down_high, up_low, up_high):
        item.step()
    near = add_call(keep, near)
    far = swap_chip(near)
    early = cell_sum([(0, 2 * share)], triple_low, first_normed)
    late = cell_sum([(2 * share, 3 * share), (0, share)], triple_low, first_normed, context, low)
    far, near, _ = end_round([down_low, down_high, up_low, up_high], far, near, late.mine)
    mine = add_call(near, far)
    other = swap_core(mine)
    for item in (early, down_low, down_high, up_low, up_high):
        item.step()
    down_keep, down_send = down_add_call(place, down_keep, down_got)
    down_got = swap_chip(down_send)
    input_grad, small = last_call(
        place, mine, other, rows_all, dh, columns, cotangent_sums, pre_sums, back_sums, bias_sums
    )
    small, down_got = end_round([down_low, down_high, up_low, up_high, early], small, down_got)
    shifts = (1, 4, 2)
    if groups != 8:
        small = lax.psum(small, "dp")
    rounds = [
        (early, up_low, up_high, late),
        (early, late, up_high, down_high),
        (early, late, up_low),
        (early, late, up_high),
        (late,),
    ]
    for place_in, items in enumerate(rounds):
        if groups == 8 and place_in < 3:
            got = hop(small, [(spot, spot ^ shifts[place_in]) for spot in range(8)])
        for item in items:
            item.step()
        if place_in == 0:
            layer_out = layer_out_call(place, down_keep, down_got, resid, columns)
        if groups == 8 and place_in < 3:
            (got,) = end_round(list(items), got)
            small = add_wide_call(small, got)
        else:
            end_round(list(items))
        if place_in == 2:
            down_grad = finish([down_low, down_high], [width])[0]
        if place_in == 3:
            up_grad = finish([up_low, up_high], [width])[0]
    triple_grad, output_grad = finish([early, late], [3 * share, share])
    triple_grad = triple_grad.reshape(3, share, width).transpose(2, 0, 1)
    return (
        layer_out.T,
        input_grad.T,
        small[0],
        small[1],
        triple_grad,
        small[7:9, :share],
        output_grad,
        small[6],
        small[4],
        small[5],
        up_grad,
        small[3],
        down_grad,
        small[2],
    )


def solution(mesh):
    placed = (
        P("dp", "tensor"),
        P(),
        P(),
        P(None, None, "tensor"),
        P(None, "tensor"),
        P("tensor", None),
        P(),
        P(),
        P(),
        P(None, "tensor"),
        P("tensor"),
        P("tensor", None),
        P(),
        P("dp", "tensor"),
        P("dp"),
    )
    return jax.shard_map(
        functools.partial(body, mesh.shape["dp"]),
        mesh=mesh,
        in_specs=placed,
        out_specs=(
            P("dp", "tensor"),
            P("dp", "tensor"),
            P(),
            P(),
            P(None, None, "tensor"),
            P(None, "tensor"),
            P("tensor", None),
            P(),
            P(),
            P(),
            P(None, "tensor"),
            P("tensor"),
            P("tensor", None),
            P(),
        ),
        check_vma=False,
    )
```

```python
import functools

import jax
import jax.numpy as jnp
from jax import lax
from jax.experimental import pallas as pl
from jax.experimental.pallas import tpu as pltpu
from jax.sharding import PartitionSpec as P

HEAD_DIM = 56
CELL_LEN = 384
LANES = 128
WIDE = 256
epsilon = 1e-05
CURVE = 0.7978845608028654
CUBIC = 0.044715
bf16 = jnp.bfloat16
f32 = jnp.float32
MIB = 1024 * 1024
SMALL = 6


def dot_nn(left, right):
    return lax.dot_general(left, right, (((1,), (0,)), ((), ())), preferred_element_type=f32)


def dot_nt(left, right):
    return lax.dot_general(left, right, (((1,), (1,)), ((), ())), preferred_element_type=f32)


def dot_tn(left, right):
    return lax.dot_general(left, right, (((0,), (0,)), ((), ())), preferred_element_type=f32)


def struct(shape, dtype=bf16):
    return jax.ShapeDtypeStruct(shape, dtype)


CHAIN = []


def in_turn(arguments, first):
    if CHAIN:
        held = lax.optimization_barrier((arguments[first], CHAIN[0]))[0]
        arguments = (*arguments[:first], held, *arguments[first + 1 :])
    return arguments


def call(kernel, name, out_shape, flops, *arguments, scratch=(), scalars=0, limit=12, transcendentals=0, far_in=(), far_out=()):
    inputs = [pl.ANY if place in far_in else pltpu.VMEM for place in range(len(arguments) - scalars)]
    outputs = [pl.ANY if place in far_out else pltpu.VMEM for place in range(len(out_shape))]
    results = pl.pallas_call(
        kernel,
        in_specs=[pl.BlockSpec(memory_space=space) for space in [pltpu.SMEM] * scalars + inputs],
        out_specs=[pl.BlockSpec(memory_space=space) for space in outputs],
        out_shape=out_shape,
        scratch_shapes=scratch,
        compiler_params=pltpu.CompilerParams(vmem_limit_bytes=limit * MIB),
        name=name,
    )(*in_turn(arguments, scalars))
    CHAIN[:] = results[:1]
    return results


def loop(count, step):
    def wrapped(index, carry):
        step(index)
        return carry

    lax.fori_loop(0, count, wrapped, 0)


def by_rows(rows, step):
    whole = rows // 64

    def block(index):
        step(pl.multiple_of(index * 64, 64), 64)

    loop(whole, block)
    if rows % 64:
        step(64 * whole, rows % 64)


def lanes_at(index, size):
    return pl.ds(pl.multiple_of(index * size, size), size)


def start_copies(pairs, sems, first=0):
    copies = [
        pltpu.make_async_copy(source, target, sems.at[first + place])
        for place, (source, target) in enumerate(pairs)
    ]
    for copy in copies:
        copy.start()
    return copies


def wait_for(copies):
    for copy in copies:
        copy.wait()


def place_pieces(place, refs, target):
    share = refs[0].shape[0]
    for offset, ref in enumerate(refs):
        slot = lax.bitwise_xor(place, offset)
        target[pl.ds(pl.multiple_of(slot * share, 8), share), :] = ref[...].astype(target.dtype)


def norm_columns(field, gain, shift):
    center = field - jnp.mean(field, 0, keepdims=True)
    spread = jnp.mean(center * center, 0, keepdims=True)
    return center * lax.rsqrt(spread + epsilon) * gain + shift


def front_kernel(
    place_ref, length_ref, own, near, far, both, weight_far, columns, bias,
    rows_far, normed_far, triple_far, probs_far, context_out,
    field, pieces, weight, rows_out, normed_out, triple_out, probs_out, sems,
):
    share = context_out.shape[0]
    heads = share // HEAD_DIM
    tokens = rows_out.shape[1]
    arrived = [pieces.at[offset] for offset in range(4)]
    copies = start_copies([*zip((own, near, far, both), arrived), (weight_far, weight)], sems)
    wait_for(copies[:4])
    place_pieces(place_ref[0], arrived, field)

    def norm_step(index):
        lanes = lanes_at(index, LANES)
        value = field[:, lanes]
        rows_out[:, lanes] = value.astype(bf16)
        normed_out[:, lanes] = norm_columns(value, columns[:, 0:1], columns[:, 1:2]).astype(bf16)

    loop(tokens // LANES, norm_step)
    copies[4].wait()
    leaving = start_copies([(rows_out, rows_far), (normed_out, normed_far)], sems, 5)

    def project_step(index):
        lanes = lanes_at(index, WIDE)
        triple_out[:, lanes] = (dot_nn(weight[...], normed_out[:, lanes]) + bias[...]).astype(bf16)

    loop(tokens // WIDE, project_step)
    leaving += start_copies([(triple_out, triple_far)], sems, 7)
    factor = HEAD_DIM ** (-0.5)

    def cell_step(cell):
        length = length_ref[cell]
        for head in range(heads):
            start = HEAD_DIM * head
            for block in range(CELL_LEN // LANES):
                span = LANES * (block + 1)
                base = pl.multiple_of(cell * CELL_LEN, LANES)
                here = pl.ds(pl.multiple_of(base + LANES * block, LANES), LANES)
                queries = triple_out[start : start + HEAD_DIM, here]
                keys = triple_out[share + start : share + start + HEAD_DIM, pl.ds(base, span)]
                values = triple_out[2 * share + start : 2 * share + start + HEAD_DIM, pl.ds(base, span)]
                scores = dot_tn(keys, queries) * factor
                key_place = lax.broadcasted_iota(jnp.int32, (span, LANES), 0)
                query_place = lax.broadcasted_iota(jnp.int32, (span, LANES), 1) + LANES * block
                allowed = (key_place <= query_place) & (key_place < length)
                masked = jnp.where(allowed, scores, -1e30)
                expo = jnp.exp(masked - jnp.max(masked, 0, keepdims=True))
                probs = (expo / jnp.sum(expo, 0, keepdims=True)).astype(bf16)
                probs_out[cell, head, :span, LANES * block : span] = probs
                context_out[start : start + HEAD_DIM, here] = dot_nn(values, probs).astype(bf16)
        pltpu.make_async_copy(probs_out.at[cell], probs_far.at[cell], sems.at[8 + cell]).start()

    loop(tokens // CELL_LEN, cell_step)
    for cell in range(tokens // CELL_LEN):
        pltpu.make_async_copy(probs_out.at[cell], probs_far.at[cell], sems.at[8 + cell]).wait()
    wait_for(leaving)


def front_call(place, lengths, pieces, columns, weight, bias):
    share, tokens = pieces[0].shape
    width = weight.shape[1]
    heads = share // HEAD_DIM
    cells = tokens // CELL_LEN
    pairs = cells * heads * CELL_LEN * CELL_LEN
    return call(
        front_kernel,
        "front",
        [
            struct((width, tokens)),
            struct((width, tokens)),
            struct((3 * share, tokens)),
            struct((cells, heads, CELL_LEN, CELL_LEN)),
            struct((share, tokens)),
        ],
        tokens * width * share * 6 + pairs * HEAD_DIM * 4,
        place, lengths, *pieces, weight, columns, bias,
        scratch=[
            pltpu.VMEM((width, tokens), f32),
            pltpu.VMEM((4, share, tokens), bf16),
            pltpu.VMEM(weight.shape, bf16),
            pltpu.VMEM((width, tokens), bf16),
            pltpu.VMEM((width, tokens), bf16),
            pltpu.VMEM((3 * share, tokens), bf16),
            pltpu.VMEM((cells, heads, CELL_LEN, CELL_LEN), bf16),
            pltpu.SemaphoreType.DMA((8 + cells,)),
        ],
        scalars=2,
        limit=60,
        far_in=range(5),
        far_out=range(4),
        transcendentals=pairs,
    )


def gate_parts(value):
    square = value * value
    bend = jnp.tanh(CURVE * (value + CUBIC * square * value))
    upper = 0.5 * (1.0 + bend)
    slope = upper + 0.5 * value * (1.0 - bend * bend) * CURVE * (1.0 + 3.0 * CUBIC * square)
    return value * upper, slope


def middle_kernel(
    own, near, far, both, own_weight, near_weight, far_weight, both_weight, rows_far, up_far, columns,
    resid_far, normed_far, hidden_out, slope_out,
    field, weight, pieces, weights, rows_ref, up, resid_out, normed_out, sems,
):
    tokens = resid_out.shape[1]
    share = own.shape[0]
    sources = own, near, far, both, own_weight, near_weight, far_weight, both_weight
    targets = [pieces.at[place] for place in range(4)] + [weights.at[place] for place in range(4)]
    copies = start_copies([*zip(sources, targets), (rows_far, rows_ref), (up_far, up)], sems)
    wait_for(copies[:8])
    for place in range(4):
        field[share * place : share * (place + 1), :] = pieces[place].astype(f32)
        weight[:, share * place : share * (place + 1)] = weights[place]
    wait_for(copies[8:])

    def leaving(index):
        lanes = lanes_at(index, WIDE)
        resid_copy = pltpu.make_async_copy(
            resid_out.at[:, lanes], resid_far.at[:, lanes], sems.at[10 + 2 * index]
        )
        normed_copy = pltpu.make_async_copy(
            normed_out.at[:, lanes], normed_far.at[:, lanes], sems.at[11 + 2 * index]
        )
        return resid_copy, normed_copy

    def step(index):
        lanes = lanes_at(index, WIDE)
        added = dot_nn(weight[...], field[:, lanes].astype(bf16))
        resid = rows_ref[:, lanes].astype(f32) + added + columns[:, 2:3]
        resid_out[:, lanes] = resid
        normed = norm_columns(resid, columns[:, 3:4], columns[:, 4:5]).astype(bf16)
        normed_out[:, lanes] = normed
        hidden, slope = gate_parts(dot_nn(up[...], normed) + columns[:, 5:6])
        hidden_out[:, lanes] = hidden.astype(bf16)
        slope_out[:, lanes] = slope
        for copy in leaving(index):
            copy.start()

    loop(tokens // WIDE, step)
    for index in range(tokens // WIDE):
        wait_for(leaving(index))


def middle_call(pieces, weights, rows_all, columns, up):
    width, tokens = rows_all.shape
    hidden = up.shape[0]
    return call(
        middle_kernel,
        "middle",
        [
            struct((width, tokens), f32),
            struct((width, tokens)),
            struct((hidden, tokens)),
            struct((hidden, tokens), f32),
        ],
        tokens * width * (width + hidden) * 2,
        *pieces, *weights, rows_all, up, columns,
        scratch=[
            pltpu.VMEM((width, tokens), f32),
            pltpu.VMEM((width, width), bf16),
            pltpu.VMEM((4, *pieces[0].shape), bf16),
            pltpu.VMEM((4, *weights[0].shape), bf16),
            pltpu.VMEM((width, tokens), bf16),
            pltpu.VMEM(up.shape, bf16),
            pltpu.VMEM((width, tokens), f32),
            pltpu.VMEM((width, tokens), bf16),
            pltpu.SemaphoreType.DMA((10 + 2 * (tokens // WIDE),)),
        ],
        limit=53,
        far_in=range(10),
        far_out=range(2),
        transcendentals=tokens * hidden,
    )


def spread_kernel(place_ref, own, near, far, both, rows_out, sums_out, field):
    place_pieces(place_ref[0], (own, near, far, both), field)
    rows_out[...] = field[...].astype(bf16)
    sums_out[...] = jnp.sum(field[...], 1, keepdims=True)


def spread_call(place, pieces):
    share, tokens = pieces[0].shape
    return call(
        spread_kernel,
        "spread",
        [struct((4 * share, tokens)), struct((4 * share, 1), f32)],
        4 * share * tokens,
        place, *pieces,
        scratch=[pltpu.VMEM((4 * share, tokens), f32)],
        scalars=1,
    )


def store_halves(bit, value, lanes, keep_out, send_out):
    half = keep_out.shape[0]

    @pl.when(bit == 0)
    def _():
        keep_out[:, lanes] = value[:half]
        send_out[:, lanes] = value[half:]

    @pl.when(bit != 0)
    def _():
        keep_out[:, lanes] = value[half:]
        send_out[:, lanes] = value[:half]


def turn_kernel(
    place_ref, cotangent, slope, down, up, pre_out, keep_out, send_out, sums_out,
):
    tokens = cotangent.shape[1]
    core = lax.rem(place_ref[0], 2)
    sums_out[...] = jnp.zeros_like(sums_out)

    def step(index):
        lanes = lanes_at(index, WIDE)
        pre = dot_nn(down[...], cotangent[:, lanes]) * slope[:, lanes]
        sums_out[...] += jnp.sum(pre, 1, keepdims=True)
        low = pre.astype(bf16)
        pre_out[:, lanes] = low
        store_halves(core, dot_nn(up[...], low).astype(bf16), lanes, keep_out, send_out)

    loop(tokens // WIDE, step)


def turn_call(place, cotangent, slope, down, up):
    width, tokens = cotangent.shape
    hidden = up.shape[1]
    return call(
        turn_kernel,
        "turn",
        [
            struct((hidden, tokens)),
            struct((width // 2, tokens)),
            struct((width // 2, tokens)),
            struct((hidden, 1), f32),
        ],
        tokens * width * hidden * 4,
        place, cotangent, slope, down, up,
        scalars=1,
    )


def norm_back(field, grad, gain):
    center = field - jnp.mean(field, 0, keepdims=True)
    inverse = lax.rsqrt(jnp.mean(center * center, 0, keepdims=True) + epsilon)
    normed = center * inverse
    scaled = grad * gain
    inner = jnp.mean(scaled * normed, 0, keepdims=True)
    back = inverse * (scaled - jnp.mean(scaled, 0, keepdims=True) - normed * inner)
    return normed, back


def add_parts(left, right):
    return (left.astype(f32) + right.astype(f32)).astype(bf16)


def back_kernel(
    place_ref, mine, other, resid, cotangent, columns, out_weight, triple, probs_ref, weight,
    dh_out, low_out, triple_out, keep_out, send_out, sums_out, bias_out,
    grad, context_grad, gain_sum, shift_sum, total_sum,
):
    share = out_weight.shape[0]
    width, tokens = resid.shape
    half = width // 2
    heads = share // HEAD_DIM
    factor = HEAD_DIM ** (-0.5)
    core = lax.rem(place_ref[0], 2)
    grad[pl.ds(pl.multiple_of(core * half, 8), half), :] = mine[...].astype(f32)
    grad[pl.ds(pl.multiple_of((1 - core) * half, 8), half), :] = other[...].astype(f32)
    for item in (gain_sum, shift_sum, total_sum, bias_out):
        item[...] = jnp.zeros_like(item)

    def norm_step(index):
        lanes = lanes_at(index, LANES)
        upper = grad[:, lanes]
        normed, back = norm_back(resid[:, lanes], upper, columns[:, 3:4])
        total = cotangent[:, lanes].astype(f32) + back
        dh_out[:, lanes] = total
        low_out[:, lanes] = total.astype(bf16)
        gain_sum[...] += upper * normed
        shift_sum[...] += upper
        total_sum[...] += total

    loop(tokens // LANES, norm_step)
    sums_out[:, 0:1] = jnp.sum(gain_sum[...], 1, keepdims=True)
    sums_out[:, 1:2] = jnp.sum(shift_sum[...], 1, keepdims=True)
    sums_out[:, 2:3] = jnp.sum(total_sum[...], 1, keepdims=True)

    def context_step(index):
        lanes = lanes_at(index, WIDE)
        context_grad[:, lanes] = dot_nn(out_weight[...], low_out[:, lanes]).astype(bf16)

    loop(tokens // WIDE, context_step)
    blocks = CELL_LEN // LANES

    def cell_step(cell):
        base = pl.multiple_of(cell * CELL_LEN, LANES)
        for head in range(heads):
            start = HEAD_DIM * head
            query_rows = slice(start, start + HEAD_DIM)
            key_rows = slice(share + start, share + start + HEAD_DIM)
            value_rows = slice(2 * share + start, 2 * share + start + HEAD_DIM)
            key_grads = [None] * blocks
            value_grads = [None] * blocks
            query_sum = jnp.zeros((HEAD_DIM, 1), f32)
            value_sum = jnp.zeros((HEAD_DIM, 1), f32)
            for block in range(blocks):
                span = LANES * (block + 1)
                here = pl.ds(pl.multiple_of(base + LANES * block, LANES), LANES)
                queries = triple[query_rows, here]
                keys = triple[key_rows, pl.ds(base, span)]
                values = triple[value_rows, pl.ds(base, span)]
                low = context_grad[query_rows, here]
                probs_low = probs_ref[cell, head, :span, LANES * block : span]
                probs = probs_low.astype(f32)
                prob_grad = dot_tn(values, low)
                inner = jnp.sum(prob_grad * probs, 0, keepdims=True)
                score = (probs * (prob_grad - inner) * factor).astype(bf16)
                query_grad = dot_nn(keys, score)
                query_sum += jnp.sum(query_grad, 1, keepdims=True)
                triple_out[query_rows, here] = query_grad.astype(bf16)
                key_part = dot_nt(queries, score)
                value_part = dot_nt(low, probs_low)
                for place in range(block + 1):
                    lanes = slice(LANES * place, LANES * (place + 1))
                    if key_grads[place] is None:
                        key_grads[place] = key_part[:, lanes]
                        value_grads[place] = value_part[:, lanes]
                    else:
                        key_grads[place] += key_part[:, lanes]
                        value_grads[place] += value_part[:, lanes]
            for block in range(blocks):
                here = pl.ds(pl.multiple_of(base + LANES * block, LANES), LANES)
                triple_out[key_rows, here] = key_grads[block].astype(bf16)
                triple_out[value_rows, here] = value_grads[block].astype(bf16)
                value_sum += jnp.sum(value_grads[block], 1, keepdims=True)
            bias_out[query_rows, 0:1] += query_sum
            bias_out[query_rows, 1:2] += value_sum

    loop(tokens // CELL_LEN, cell_step)

    def part_step(index):
        lanes = lanes_at(index, WIDE)
        part = dot_nn(weight[...], triple_out[:, lanes]).astype(bf16)
        store_halves(core, part, lanes, keep_out, send_out)

    loop(tokens // WIDE, part_step)


def back_call(place, mine, other, resid, cotangent, columns, out_weight, triple, probs, weight):
    width, tokens = resid.shape
    share = out_weight.shape[0]
    cells, heads = probs.shape[:2]
    pairs = cells * heads * CELL_LEN * CELL_LEN
    return call(
        back_kernel,
        "back",
        [
            struct((width, tokens), f32),
            struct((width, tokens)),
            struct((3 * share, tokens)),
            struct((width // 2, tokens)),
            struct((width // 2, tokens)),
            struct((width, 8), f32),
            struct((share, 8), f32),
        ],
        tokens * width * share * 8 + pairs * HEAD_DIM * 8,
        place, mine, other, resid, cotangent, columns, out_weight, triple, probs, weight,
        scratch=[pltpu.VMEM((width, tokens), f32), pltpu.VMEM((share, tokens), bf16)]
        + [pltpu.VMEM((width, LANES), f32)] * 3,
        scalars=1,
    )


def last_kernel(
    place_ref, mine, other, rows_ref, dh, columns, cotangent_sums, pre_sums, back_sums, bias_sums,
    out, sums_out, grad, gain_sum, shift_sum, field,
):
    share, tokens = out.shape
    width = rows_ref.shape[0]
    half = width // 2
    place = place_ref[0]
    core = lax.rem(place, 2)
    grad[pl.ds(pl.multiple_of(core * half, 8), half), :] = mine[...].astype(f32)
    grad[pl.ds(pl.multiple_of((1 - core) * half, 8), half), :] = other[...].astype(f32)
    gain_sum[...] = jnp.zeros_like(gain_sum)
    shift_sum[...] = jnp.zeros_like(shift_sum)

    def norm_step(index):
        lanes = lanes_at(index, LANES)
        upper = grad[:, lanes]
        normed, back = norm_back(rows_ref[:, lanes].astype(f32), upper, columns[:, 0:1])
        field[...] = dh[:, lanes] + back
        out[:, lanes] = field[pl.ds(pl.multiple_of(place * share, 8), share), :].astype(bf16)
        gain_sum[...] += upper * normed
        shift_sum[...] += upper

    loop(tokens // LANES, norm_step)
    field[:, 0:1] = jnp.sum(gain_sum[...], 1, keepdims=True)
    field[:, 1:2] = jnp.sum(shift_sum[...], 1, keepdims=True)
    field[:, 2:3] = cotangent_sums[...]
    field[:, 3:4] = pre_sums[...]
    field[:, 4:7] = back_sums[:, 0:3]
    field[0:share, 7:9] = bias_sums[:, 0:2]
    sums_out[...] = field[...].T[0:16, :]


def last_call(place, mine, other, rows_all, dh, columns, *sums):
    width, tokens = rows_all.shape
    return call(
        last_kernel,
        "last",
        [struct((width // 4, tokens)), struct((16, width), f32)],
        width * tokens * 12,
        place, mine, other, rows_all, dh, columns, *sums,
        scratch=[pltpu.VMEM((width, tokens), f32)] + [pltpu.VMEM((width, LANES), f32)] * 3,
        scalars=1,
    )


def add_kernel(left, right, out):
    def step(start, size):
        rows = pl.ds(start, size)
        out[rows, :] = add_parts(left[rows, :], right[rows, :])

    by_rows(out.shape[0], step)


def add_call(left, right):
    return call(add_kernel, "add", [struct(left.shape)], left.size, left, right, limit=SMALL)[0]


def add_wide_kernel(left, right, out):
    out[...] = left[...] + right[...]


def add_wide_call(left, right):
    return call(add_wide_kernel, "add_wide", [struct(left.shape, f32)], left.size, left, right, limit=SMALL)[0]


def down_kernel(place_ref, hidden, down, keep_out, send_out):
    tokens = hidden.shape[1]
    share = keep_out.shape[0] // 2
    core = lax.rem(place_ref[0], 2)

    def step(index):
        lanes = lanes_at(index, WIDE)
        part = dot_nn(down[...], hidden[:, lanes]).astype(bf16)
        for chip in range(2):
            rows = slice(share * chip, share * (chip + 1))
            low = part[2 * share * chip : 2 * share * chip + share]
            high = part[2 * share * chip + share : 2 * share * (chip + 1)]

            @pl.when(core == 0)
            def _():
                keep_out[rows, lanes] = low
                send_out[rows, lanes] = high

            @pl.when(core != 0)
            def _():
                keep_out[rows, lanes] = high
                send_out[rows, lanes] = low

    loop(tokens // WIDE, step)


def down_call(place, hidden, down):
    width, inner = down.shape
    tokens = hidden.shape[1]
    return call(
        down_kernel,
        "down",
        [struct((width // 2, tokens))] * 2,
        tokens * width * inner * 2,
        place, hidden, down,
        scalars=1,
    )


def down_add_kernel(place_ref, keep, got, keep_out, send_out, field):
    share = keep_out.shape[0]
    chip = lax.div(place_ref[0], 2)
    field[...] = keep[...].astype(f32) + got[...].astype(f32)
    keep_out[...] = field[pl.ds(pl.multiple_of(chip * share, 8), share), :].astype(bf16)
    send_out[...] = field[pl.ds(pl.multiple_of((1 - chip) * share, 8), share), :].astype(bf16)


def down_add_call(place, keep, got):
    rows, tokens = keep.shape
    return call(
        down_add_kernel,
        "down_add",
        [struct((rows // 2, tokens))] * 2,
        keep.size,
        place, keep, got,
        scratch=[pltpu.VMEM(keep.shape, f32)],
        scalars=1,
    )


def layer_out_kernel(place_ref, keep, got, resid, columns, out):
    share = out.shape[0]
    rows = pl.ds(pl.multiple_of(place_ref[0] * share, 8), share)
    total = keep[...].astype(f32) + got[...].astype(f32)
    out[...] = (resid[rows, :] + total + columns[rows, 6:7]).astype(bf16)


def layer_out_call(place, keep, got, resid, columns):
    return call(
        layer_out_kernel,
        "layer_out",
        [struct(keep.shape)],
        keep.size,
        place, keep, got, resid, columns,
        scalars=1,
    )[0]


def grad_kernel(ranges, place_ref, *refs):
    pairs, (keep_out, send_out) = refs[:-2], refs[-2:]
    side = lax.rem(place_ref[0], 2)
    width = keep_out.shape[1]
    for begin in range(0, width, 384):
        lanes = slice(begin, min(begin + 384, width))
        parts = []
        for left, right, (low, high) in zip(pairs[0::2], pairs[1::2], ranges):
            parts.append(dot_nt(left[low:high, :], right[lanes, :]).astype(bf16))
        value = parts[0] if len(parts) == 1 else jnp.concatenate(parts, 0)
        store_halves(side, value, lanes, keep_out, send_out)


def grad_call(dp_place, ranges, *pairs):
    rows = sum(high - low for low, high in ranges)
    tokens = pairs[0].shape[1]
    width = pairs[1].shape[0]
    return call(
        functools.partial(grad_kernel, ranges),
        "grad",
        [struct((rows // 2, width)), struct((rows // 2, width))],
        2 * rows * tokens * width,
        dp_place, *pairs,
        scalars=1,
    )


def settle_kernel(dp_ref, mine, got, out):
    def copy_from(ref):
        def step(start, size):
            rows = pl.ds(start, size)
            out[rows, :] = ref[rows, :]

        by_rows(out.shape[0], step)

    pl.when(dp_ref[2] == 1)(lambda: copy_from(got))
    pl.when(dp_ref[2] == 0)(lambda: copy_from(mine))


def settle_call(dp, mine, got):
    return call(settle_kernel, "settle", [struct(mine.shape)], mine.size, dp, mine, got, scalars=1, limit=SMALL)[0]


def final_kernel(count, dp_ref, *refs):
    side = lax.rem(dp_ref[0], 2)
    outs = refs[2 * count :]

    def put(start, ref):
        done = 0
        rows = ref.shape[0]
        for out in outs:
            size = out.shape[0]
            low, high = max(start, done), min(start + rows, done + size)
            if low < high:

                def step(begin, count):
                    value = ref[pl.ds(low - start + begin, count), :].astype(f32)
                    out[pl.ds(low - done + begin, count), :] = value

                by_rows(high - low, step)
            done += size

    base = 0
    for place in range(count):
        mine, got = refs[2 * place : 2 * place + 2]
        half = mine.shape[0]

        @pl.when(side == 0)
        def _():
            put(base, mine)
            put(base + half, got)

        @pl.when(side != 0)
        def _():
            put(base, got)
            put(base + half, mine)

        base += 2 * half


def final_call(dp, parts, sizes):
    width = parts[0].shape[1]
    return call(
        functools.partial(final_kernel, len(parts) // 2),
        "final",
        [struct((size, width), f32) for size in sizes],
        sum(sizes) * width,
        dp, *parts,
        scalars=1,
        limit=SMALL,
    )


def swap_core(value):
    return lax.ppermute(value, "tensor", [(place, place ^ 1) for place in range(4)])


def swap_chip(value):
    return lax.ppermute(value, "tensor", [(place, place ^ 2) for place in range(4)])


def after(value, *others):
    return lax.optimization_barrier((value, *others))[0]


def all_pieces(share):
    far = swap_chip(share)
    return share, swap_core(share), far, swap_core(far)


def ordered(bit, mine, other, axis):
    low = jnp.where(bit == 0, mine, other)
    high = jnp.where(bit == 0, other, mine)
    return jnp.concatenate([low, high], axis)


def line_pairs(pairs):
    return [(2 * source + side, 2 * target + side) for source, target in pairs for side in (0, 1)]


INWARD = line_pairs([(0, 1), (3, 2)])
MIDDLE = line_pairs([(1, 2), (2, 1)])
OUTWARD = line_pairs([(1, 0), (2, 3)])
ACROSS = [(place, place ^ 1) for place in range(8)]
ACROSS_MIDDLE = [(2, 3), (3, 2), (4, 5), (5, 4)]


def hop(value, pairs):
    return lax.ppermute(value, "dp", pairs)


STAGES = (ACROSS, INWARD, MIDDLE, OUTWARD, ACROSS)


class CellSum:
    def __init__(self, groups, dp, parts):
        self.groups, self.dp = groups, dp
        self.mine, self.got = parts
        self.stage = -1

    def step(self):
        self.stage += 1
        if self.groups != 8:
            return
        send = self.got
        if self.stage == 4:
            send = self.mine = settle_call(self.dp, self.mine, self.got)
        elif self.stage > 0:
            send = self.mine = add_call(self.mine, self.got)
        self.got = hop(send, STAGES[self.stage])

    def plain(self):
        value = ordered(self.dp[0] % 2, self.mine, self.got, 0)
        return lax.psum(value, "dp").astype(f32)


def finish(sums, sizes):
    if sums[0].groups == 8:
        return final_call(sums[0].dp, [piece for item in sums for piece in (item.mine, item.got)], sizes)
    value = jnp.concatenate([item.plain() for item in sums], 0)
    ends = [sum(sizes[: place + 1]) for place in range(len(sizes))]
    return [value[end - size : end] for end, size in zip(ends, sizes)]


def end_round(sums, *values):
    held = lax.optimization_barrier((*[item.got for item in sums], *values))
    for item, got in zip(sums, held):
        item.got = got
    return held[len(sums) :]


def body(
    groups,
    tokens,
    first_gain,
    first_shift,
    triple_weight,
    triple_bias,
    output_weight,
    output_bias,
    second_gain,
    second_shift,
    up_weight,
    up_bias,
    down_weight,
    down_bias,
    cotangent,
    lengths,
):
    share = tokens.shape[1]
    width = triple_weight.shape[0]
    index = lax.axis_index("tensor").astype(jnp.int32)
    core, chip = index % 2, index // 2
    place = index.reshape(1)
    row = lax.axis_index("dp").astype(jnp.int32)
    at_end = ((row < 2) | (row >= groups - 2)).astype(jnp.int32)
    dp = jnp.stack([row, jnp.int32(groups // 2), at_end])
    CHAIN.clear()
    fence = lambda *values: lax.optimization_barrier(values)
    token_own, grad_own = tokens.T, cotangent.T
    token_far, token_near = swap_chip(token_own), swap_core(token_own)
    grad_near, weight_near = swap_core(grad_own), swap_core(output_weight)
    triple_t = triple_weight.transpose(1, 2, 0).reshape(3 * share, width)
    bias_flat = jnp.concatenate([triple_bias[0], jnp.zeros((share,), f32), triple_bias[1]])[:, None]
    columns = jnp.stack(
        [first_gain, first_shift, output_bias, second_gain, second_shift, up_bias, down_bias], 1
    )
    up_t, triple_plain = up_weight.T, triple_t.T
    token_far, token_near, up_t, triple_plain, columns, bias_flat, out_weight = fence(
        token_far, token_near, up_t, triple_plain, columns, bias_flat, output_weight
    )
    token_both = swap_core(token_far)
    weight_far = swap_chip(out_weight)
    own_t = out_weight.T
    token_both, own_t = fence(token_both, own_t)
    rows_all, first_normed, triple, probs, context = front_call(
        place, lengths, (token_own, token_near, token_far, token_both), columns, triple_t, bias_flat
    )
    context_far, context_near = swap_chip(context), swap_core(context)
    weight_far, weight_near, down_plain, _ = fence(weight_far, weight_near, down_weight, context)
    weight_both = swap_core(weight_far)
    weights = own_t, weight_near.T, weight_far.T, weight_both.T
    down_t = down_plain.T
    context_far, context_near, down_t, grad_own, *weights = fence(
        context_far, context_near, down_t, grad_own, *weights
    )
    context_both = swap_core(context_far)
    grad_far = swap_chip(grad_own)
    resid, second_normed, hidden, slope = middle_call(
        (context, context_near, context_far, context_both), weights, rows_all, columns, up_t
    )
    grad_far, _ = fence(grad_far, second_normed)
    grad_both = swap_core(grad_far)
    grad_rows, cotangent_sums = spread_call(place, (grad_own, grad_near, grad_far, grad_both))
    half = width // 2

    def cell_sum(ranges, *pairs):
        return CellSum(groups, dp, grad_call(dp, ranges, *pairs))

    down_low = cell_sum([(0, half)], hidden, grad_rows)
    down_low.step()
    down_high = cell_sum([(half, width)], hidden, grad_rows)
    pre_low, keep, send, pre_sums = turn_call(place, grad_rows, slope, down_weight, up_weight)
    keep, send = end_round([down_low], keep, send)
    near = swap_core(send)
    down_low.step()
    down_high.step()
    down_keep, down_send = down_call(place, hidden, down_t)
    near = add_call(keep, near)
    far = swap_chip(near)
    down_got = swap_core(down_send)
    up_low = cell_sum([(0, half)], second_normed, pre_low)
    up_high = cell_sum([(half, width)], second_normed, pre_low)
    far, down_got, near, _ = end_round([down_low, down_high], far, down_got, near, up_high.mine)
    mine = add_call(near, far)
    other = swap_core(mine)
    for item in (up_low, down_low, down_high, up_high):
        item.step()
    dh, low, triple_low, keep, send, back_sums, bias_sums = back_call(
        place, mine, other, resid, grad_rows, columns, output_weight, triple, probs, triple_plain
    )
    keep, send = end_round([down_low, down_high, up_low, up_high], keep, send)
    near = swap_core(send)
    early = cell_sum([(0, 2 * share)], triple_low, first_normed)
    for item in (early, up_low, down_high, down_low):
        item.step()
    near = add_call(keep, near)
    far = swap_chip(near)
    late = cell_sum([(2 * share, 3 * share), (0, share)], triple_low, first_normed, context, low)
    far, near, _ = end_round([early, down_low, down_high, up_low, up_high], far, near, late.mine)
    mine = add_call(near, far)
    other = swap_core(mine)
    for item in (late, early, up_low, down_high):
        item.step()
    down_keep, down_send = down_add_call(place, down_keep, down_got)
    down_got = swap_chip(down_send)
    input_grad, small = last_call(
        place, mine, other, rows_all, dh, columns, cotangent_sums, pre_sums, back_sums, bias_sums
    )
    small, down_got = end_round([down_low, down_high, up_low, up_high, early, late], small, down_got)
    shifts = (1, 4, 2)
    if groups != 8:
        small = lax.psum(small, "dp")
    rounds = [
        (down_low, late, early, up_low),
        (down_high, late, early, up_high),
        (up_low, late, up_high),
        (early, up_high),
        (late, up_high),
    ]
    for place_in, items in enumerate(rounds):
        if groups == 8 and place_in < 3:
            got = hop(small, [(spot, spot ^ shifts[place_in]) for spot in range(8)])
        for item in items:
            item.step()
        if place_in == 2:
            down_grad = finish([down_low, down_high], [width])[0]
        if place_in == 0:
            layer_out = layer_out_call(place, down_keep, down_got, resid, columns)
        if groups == 8 and place_in < 3:
            (got,) = end_round(list(items), got)
            small = add_wide_call(small, got)
        else:
            end_round(list(items))
    up_grad = finish([up_low, up_high], [width])[0]
    triple_grad, output_grad = finish([early, late], [3 * share, share])
    triple_grad = triple_grad.reshape(3, share, width).transpose(2, 0, 1)
    return (
        layer_out.T,
        input_grad.T,
        small[0],
        small[1],
        triple_grad,
        small[7:9, :share],
        output_grad,
        small[6],
        small[4],
        small[5],
        up_grad,
        small[3],
        down_grad,
        small[2],
    )


def solution(mesh):
    placed = (
        P("dp", "tensor"),
        P(),
        P(),
        P(None, None, "tensor"),
        P(None, "tensor"),
        P("tensor", None),
        P(),
        P(),
        P(),
        P(None, "tensor"),
        P("tensor"),
        P("tensor", None),
        P(),
        P("dp", "tensor"),
        P("dp"),
    )
    return jax.shard_map(
        functools.partial(body, mesh.shape["dp"]),
        mesh=mesh,
        in_specs=placed,
        out_specs=(
            P("dp", "tensor"),
            P("dp", "tensor"),
            P(),
            P(),
            P(None, None, "tensor"),
            P(None, "tensor"),
            P("tensor", None),
            P(),
            P(),
            P(),
            P(None, "tensor"),
            P("tensor"),
            P("tensor", None),
            P(),
        ),
        check_vma=False,
    )
```

```python
import functools

import jax
import jax.numpy as jnp
from jax import lax
from jax.experimental import pallas as pl
from jax.experimental.pallas import tpu as pltpu
from jax.sharding import PartitionSpec as P

HEAD_DIM = 56
CELL_LEN = 384
LANES = 128
WIDE = 256
epsilon = 1e-05
CURVE = 0.7978845608028654
CUBIC = 0.044715
bf16 = jnp.bfloat16
f32 = jnp.float32
MIB = 1024 * 1024
SMALL = 6


def dot_nn(left, right):
    return lax.dot_general(left, right, (((1,), (0,)), ((), ())), preferred_element_type=f32)


def dot_nt(left, right):
    return lax.dot_general(left, right, (((1,), (1,)), ((), ())), preferred_element_type=f32)


def dot_tn(left, right):
    return lax.dot_general(left, right, (((0,), (0,)), ((), ())), preferred_element_type=f32)


def struct(shape, dtype=bf16):
    return jax.ShapeDtypeStruct(shape, dtype)


CHAIN = []


def in_turn(arguments, first):
    if CHAIN:
        held = lax.optimization_barrier((arguments[first], CHAIN[0]))[0]
        arguments = (*arguments[:first], held, *arguments[first + 1 :])
    return arguments


def call(kernel, name, out_shape, flops, *arguments, scratch=(), scalars=0, limit=12, transcendentals=0, far_in=(), far_out=()):
    inputs = [pl.ANY if place in far_in else pltpu.VMEM for place in range(len(arguments) - scalars)]
    outputs = [pl.ANY if place in far_out else pltpu.VMEM for place in range(len(out_shape))]
    results = pl.pallas_call(
        kernel,
        in_specs=[pl.BlockSpec(memory_space=space) for space in [pltpu.SMEM] * scalars + inputs],
        out_specs=[pl.BlockSpec(memory_space=space) for space in outputs],
        out_shape=out_shape,
        scratch_shapes=scratch,
        compiler_params=pltpu.CompilerParams(vmem_limit_bytes=limit * MIB),
        name=name,
    )(*in_turn(arguments, scalars))
    CHAIN[:] = results[:1]
    return results


def loop(count, step):
    def wrapped(index, carry):
        step(index)
        return carry

    lax.fori_loop(0, count, wrapped, 0)


def by_rows(rows, step):
    whole = rows // 64

    def block(index):
        step(pl.multiple_of(index * 64, 64), 64)

    loop(whole, block)
    if rows % 64:
        step(64 * whole, rows % 64)


def lanes_at(index, size):
    return pl.ds(pl.multiple_of(index * size, size), size)


def start_copies(pairs, sems, first=0):
    copies = [
        pltpu.make_async_copy(source, target, sems.at[first + place])
        for place, (source, target) in enumerate(pairs)
    ]
    for copy in copies:
        copy.start()
    return copies


def wait_for(copies):
    for copy in copies:
        copy.wait()


def place_pieces(place, refs, target):
    share = refs[0].shape[0]
    for offset, ref in enumerate(refs):
        base = lax.bitwise_xor(place, offset) * share

        def step(start, size):
            value = ref[pl.ds(start, size), :].astype(target.dtype)
            target[pl.ds(pl.multiple_of(base + start, 8), size), :] = value

        by_rows(share, step)


def norm_columns(field, gain, shift):
    center = field - jnp.mean(field, 0, keepdims=True)
    spread = jnp.mean(center * center, 0, keepdims=True)
    return center * lax.rsqrt(spread + epsilon) * gain + shift


def front_kernel(
    place_ref, length_ref, own, near, far, both, weight_far, columns, bias,
    rows_far, normed_far, triple_far, probs_far, context_out,
    field, pieces, weight, rows_out, normed_out, triple_out, probs_out, sems,
):
    share = context_out.shape[0]
    heads = share // HEAD_DIM
    tokens = rows_out.shape[1]
    arrived = [pieces.at[offset] for offset in range(4)]
    copies = start_copies([*zip((own, near, far, both), arrived), (weight_far, weight)], sems)
    wait_for(copies[:4])
    place_pieces(place_ref[0], arrived, field)

    def norm_step(index):
        lanes = lanes_at(index, LANES)
        value = field[:, lanes]
        rows_out[:, lanes] = value.astype(bf16)
        normed_out[:, lanes] = norm_columns(value, columns[:, 0:1], columns[:, 1:2]).astype(bf16)

    loop(tokens // LANES, norm_step)
    copies[4].wait()
    leaving = start_copies([(rows_out, rows_far), (normed_out, normed_far)], sems, 5)

    def project_step(index):
        lanes = lanes_at(index, WIDE)
        triple_out[:, lanes] = (dot_nn(weight[...], normed_out[:, lanes]) + bias[...]).astype(bf16)

    loop(tokens // WIDE, project_step)
    leaving += start_copies([(triple_out, triple_far)], sems, 7)
    factor = HEAD_DIM ** (-0.5)

    def cell_step(cell):
        length = length_ref[cell]
        for head in range(heads):
            start = HEAD_DIM * head
            for block in range(CELL_LEN // LANES):
                span = LANES * (block + 1)
                base = pl.multiple_of(cell * CELL_LEN, LANES)
                here = pl.ds(pl.multiple_of(base + LANES * block, LANES), LANES)
                queries = triple_out[start : start + HEAD_DIM, here]
                keys = triple_out[share + start : share + start + HEAD_DIM, pl.ds(base, span)]
                values = triple_out[2 * share + start : 2 * share + start + HEAD_DIM, pl.ds(base, span)]
                scores = dot_tn(keys, queries) * factor
                key_place = lax.broadcasted_iota(jnp.int32, (span, LANES), 0)
                query_place = lax.broadcasted_iota(jnp.int32, (span, LANES), 1) + LANES * block
                allowed = (key_place <= query_place) & (key_place < length)
                masked = jnp.where(allowed, scores, -1e30)
                expo = jnp.exp(masked - jnp.max(masked, 0, keepdims=True))
                probs = (expo / jnp.sum(expo, 0, keepdims=True)).astype(bf16)
                probs_out[cell, head, :span, LANES * block : span] = probs
                context_out[start : start + HEAD_DIM, here] = dot_nn(values, probs).astype(bf16)
        pltpu.make_async_copy(probs_out.at[cell], probs_far.at[cell], sems.at[8 + cell]).start()

    loop(tokens // CELL_LEN, cell_step)
    for cell in range(tokens // CELL_LEN):
        pltpu.make_async_copy(probs_out.at[cell], probs_far.at[cell], sems.at[8 + cell]).wait()
    wait_for(leaving)


def front_call(place, lengths, pieces, columns, weight, bias):
    share, tokens = pieces[0].shape
    width = weight.shape[1]
    heads = share // HEAD_DIM
    cells = tokens // CELL_LEN
    pairs = cells * heads * CELL_LEN * CELL_LEN
    return call(
        front_kernel,
        "front",
        [
            struct((width, tokens)),
            struct((width, tokens)),
            struct((3 * share, tokens)),
            struct((cells, heads, CELL_LEN, CELL_LEN)),
            struct((share, tokens)),
        ],
        tokens * width * share * 6 + pairs * HEAD_DIM * 4,
        place, lengths, *pieces, weight, columns, bias,
        scratch=[
            pltpu.VMEM((width, tokens), f32),
            pltpu.VMEM((4, share, tokens), bf16),
            pltpu.VMEM(weight.shape, bf16),
            pltpu.VMEM((width, tokens), bf16),
            pltpu.VMEM((width, tokens), bf16),
            pltpu.VMEM((3 * share, tokens), bf16),
            pltpu.VMEM((cells, heads, CELL_LEN, CELL_LEN), bf16),
            pltpu.SemaphoreType.DMA((8 + cells,)),
        ],
        scalars=2,
        limit=60,
        far_in=range(5),
        far_out=range(4),
        transcendentals=pairs,
    )


def gate_parts(value):
    square = value * value
    bend = jnp.tanh(CURVE * (value + CUBIC * square * value))
    upper = 0.5 * (1.0 + bend)
    slope = upper + 0.5 * value * (1.0 - bend * bend) * CURVE * (1.0 + 3.0 * CUBIC * square)
    return value * upper, slope


def middle_kernel(
    own, near, far, both, own_weight, near_weight, far_weight, both_weight, rows_far, up_far, columns,
    resid_far, normed_far, hidden_out, slope_out,
    field, weight, pieces, weights, rows_ref, up, resid_out, normed_out, sems,
):
    tokens = resid_out.shape[1]
    share = own.shape[0]
    sources = own, near, far, both, own_weight, near_weight, far_weight, both_weight
    targets = [pieces.at[place] for place in range(4)] + [weights.at[place] for place in range(4)]
    copies = start_copies([*zip(sources, targets), (rows_far, rows_ref), (up_far, up)], sems)
    wait_for(copies[:8])
    place_pieces(0, [pieces.at[place] for place in range(4)], field)
    for place in range(4):
        weight[:, share * place : share * (place + 1)] = weights[place]
    wait_for(copies[8:])

    def leaving(index):
        lanes = lanes_at(index, WIDE)
        resid_copy = pltpu.make_async_copy(
            resid_out.at[:, lanes], resid_far.at[:, lanes], sems.at[10 + 2 * index]
        )
        normed_copy = pltpu.make_async_copy(
            normed_out.at[:, lanes], normed_far.at[:, lanes], sems.at[11 + 2 * index]
        )
        return resid_copy, normed_copy

    def step(index):
        lanes = lanes_at(index, WIDE)
        added = dot_nn(weight[...], field[:, lanes].astype(bf16))
        resid = rows_ref[:, lanes].astype(f32) + added + columns[:, 2:3]
        resid_out[:, lanes] = resid
        normed = norm_columns(resid, columns[:, 3:4], columns[:, 4:5]).astype(bf16)
        normed_out[:, lanes] = normed
        hidden, slope = gate_parts(dot_nn(up[...], normed) + columns[:, 5:6])
        hidden_out[:, lanes] = hidden.astype(bf16)
        slope_out[:, lanes] = slope
        for copy in leaving(index):
            copy.start()

    loop(tokens // WIDE, step)
    for index in range(tokens // WIDE):
        wait_for(leaving(index))


def middle_call(pieces, weights, rows_all, columns, up):
    width, tokens = rows_all.shape
    hidden = up.shape[0]
    return call(
        middle_kernel,
        "middle",
        [
            struct((width, tokens), f32),
            struct((width, tokens)),
            struct((hidden, tokens)),
            struct((hidden, tokens), f32),
        ],
        tokens * width * (width + hidden) * 2,
        *pieces, *weights, rows_all, up, columns,
        scratch=[
            pltpu.VMEM((width, tokens), f32),
            pltpu.VMEM((width, width), bf16),
            pltpu.VMEM((4, *pieces[0].shape), bf16),
            pltpu.VMEM((4, *weights[0].shape), bf16),
            pltpu.VMEM((width, tokens), bf16),
            pltpu.VMEM(up.shape, bf16),
            pltpu.VMEM((width, tokens), f32),
            pltpu.VMEM((width, tokens), bf16),
            pltpu.SemaphoreType.DMA((10 + 2 * (tokens // WIDE),)),
        ],
        limit=53,
        far_in=range(10),
        far_out=range(2),
        transcendentals=tokens * hidden,
    )


def spread_kernel(place_ref, own, near, far, both, rows_out, sums_out, field):
    place_pieces(place_ref[0], (own, near, far, both), field)
    rows_out[...] = field[...].astype(bf16)
    sums_out[...] = jnp.sum(field[...], 1, keepdims=True)


def spread_call(place, pieces):
    share, tokens = pieces[0].shape
    return call(
        spread_kernel,
        "spread",
        [struct((4 * share, tokens)), struct((4 * share, 1), f32)],
        4 * share * tokens,
        place, *pieces,
        scratch=[pltpu.VMEM((4 * share, tokens), f32)],
        scalars=1,
    )


def store_halves(bit, value, lanes, keep_out, send_out):
    half = keep_out.shape[0]

    @pl.when(bit == 0)
    def _():
        keep_out[:, lanes] = value[:half]
        send_out[:, lanes] = value[half:]

    @pl.when(bit != 0)
    def _():
        keep_out[:, lanes] = value[half:]
        send_out[:, lanes] = value[:half]


def turn_kernel(
    place_ref, cotangent, slope, down, up, pre_out, keep_out, send_out, sums_out,
):
    tokens = cotangent.shape[1]
    core = lax.rem(place_ref[0], 2)
    sums_out[...] = jnp.zeros_like(sums_out)

    def step(index):
        lanes = lanes_at(index, WIDE)
        pre = dot_nn(down[...], cotangent[:, lanes]) * slope[:, lanes]
        sums_out[...] += jnp.sum(pre, 1, keepdims=True)
        low = pre.astype(bf16)
        pre_out[:, lanes] = low
        store_halves(core, dot_nn(up[...], low).astype(bf16), lanes, keep_out, send_out)

    loop(tokens // WIDE, step)


def turn_call(place, cotangent, slope, down, up):
    width, tokens = cotangent.shape
    hidden = up.shape[1]
    return call(
        turn_kernel,
        "turn",
        [
            struct((hidden, tokens)),
            struct((width // 2, tokens)),
            struct((width // 2, tokens)),
            struct((hidden, 1), f32),
        ],
        tokens * width * hidden * 4,
        place, cotangent, slope, down, up,
        scalars=1,
    )


def norm_back(field, grad, gain):
    center = field - jnp.mean(field, 0, keepdims=True)
    inverse = lax.rsqrt(jnp.mean(center * center, 0, keepdims=True) + epsilon)
    normed = center * inverse
    scaled = grad * gain
    inner = jnp.mean(scaled * normed, 0, keepdims=True)
    back = inverse * (scaled - jnp.mean(scaled, 0, keepdims=True) - normed * inner)
    return normed, back


def add_parts(left, right):
    return (left.astype(f32) + right.astype(f32)).astype(bf16)


def back_kernel(
    place_ref, mine, other, resid, cotangent, columns, out_weight, triple, probs_ref, weight,
    dh_out, low_out, triple_out, keep_out, send_out, sums_out, bias_out,
    grad, context_grad, gain_sum, shift_sum, total_sum,
):
    share = out_weight.shape[0]
    width, tokens = resid.shape
    half = width // 2
    heads = share // HEAD_DIM
    factor = HEAD_DIM ** (-0.5)
    core = lax.rem(place_ref[0], 2)
    place_pieces(core, (mine, other), grad)
    for item in (gain_sum, shift_sum, total_sum, bias_out):
        item[...] = jnp.zeros_like(item)

    def norm_step(index):
        lanes = lanes_at(index, LANES)
        upper = grad[:, lanes]
        normed, back = norm_back(resid[:, lanes], upper, columns[:, 3:4])
        total = cotangent[:, lanes].astype(f32) + back
        dh_out[:, lanes] = total
        low_out[:, lanes] = total.astype(bf16)
        gain_sum[...] += upper * normed
        shift_sum[...] += upper
        total_sum[...] += total

    loop(tokens // LANES, norm_step)
    sums_out[:, 0:1] = jnp.sum(gain_sum[...], 1, keepdims=True)
    sums_out[:, 1:2] = jnp.sum(shift_sum[...], 1, keepdims=True)
    sums_out[:, 2:3] = jnp.sum(total_sum[...], 1, keepdims=True)

    def context_step(index):
        lanes = lanes_at(index, WIDE)
        context_grad[:, lanes] = dot_nn(out_weight[...], low_out[:, lanes]).astype(bf16)

    loop(tokens // WIDE, context_step)
    blocks = CELL_LEN // LANES

    def cell_step(cell):
        base = pl.multiple_of(cell * CELL_LEN, LANES)
        for head in range(heads):
            start = HEAD_DIM * head
            query_rows = slice(start, start + HEAD_DIM)
            key_rows = slice(share + start, share + start + HEAD_DIM)
            value_rows = slice(2 * share + start, 2 * share + start + HEAD_DIM)
            key_grads = [None] * blocks
            value_grads = [None] * blocks
            query_sum = jnp.zeros((HEAD_DIM, 1), f32)
            value_sum = jnp.zeros((HEAD_DIM, 1), f32)
            for block in range(blocks):
                span = LANES * (block + 1)
                here = pl.ds(pl.multiple_of(base + LANES * block, LANES), LANES)
                queries = triple[query_rows, here]
                keys = triple[key_rows, pl.ds(base, span)]
                values = triple[value_rows, pl.ds(base, span)]
                low = context_grad[query_rows, here]
                probs_low = probs_ref[cell, head, :span, LANES * block : span]
                probs = probs_low.astype(f32)
                prob_grad = dot_tn(values, low)
                inner = jnp.sum(prob_grad * probs, 0, keepdims=True)
                score = (probs * (prob_grad - inner) * factor).astype(bf16)
                query_grad = dot_nn(keys, score)
                query_sum += jnp.sum(query_grad, 1, keepdims=True)
                triple_out[query_rows, here] = query_grad.astype(bf16)
                key_part = dot_nt(queries, score)
                value_part = dot_nt(low, probs_low)
                for place in range(block + 1):
                    lanes = slice(LANES * place, LANES * (place + 1))
                    if key_grads[place] is None:
                        key_grads[place] = key_part[:, lanes]
                        value_grads[place] = value_part[:, lanes]
                    else:
                        key_grads[place] += key_part[:, lanes]
                        value_grads[place] += value_part[:, lanes]
            for block in range(blocks):
                here = pl.ds(pl.multiple_of(base + LANES * block, LANES), LANES)
                triple_out[key_rows, here] = key_grads[block].astype(bf16)
                triple_out[value_rows, here] = value_grads[block].astype(bf16)
                value_sum += jnp.sum(value_grads[block], 1, keepdims=True)
            bias_out[query_rows, 0:1] += query_sum
            bias_out[query_rows, 1:2] += value_sum

    loop(tokens // CELL_LEN, cell_step)

    def part_step(index):
        lanes = lanes_at(index, WIDE)
        part = dot_nn(weight[...], triple_out[:, lanes]).astype(bf16)
        store_halves(core, part, lanes, keep_out, send_out)

    loop(tokens // WIDE, part_step)


def back_call(place, mine, other, resid, cotangent, columns, out_weight, triple, probs, weight):
    width, tokens = resid.shape
    share = out_weight.shape[0]
    cells, heads = probs.shape[:2]
    pairs = cells * heads * CELL_LEN * CELL_LEN
    return call(
        back_kernel,
        "back",
        [
            struct((width, tokens), f32),
            struct((width, tokens)),
            struct((3 * share, tokens)),
            struct((width // 2, tokens)),
            struct((width // 2, tokens)),
            struct((width, 8), f32),
            struct((share, 8), f32),
        ],
        tokens * width * share * 8 + pairs * HEAD_DIM * 8,
        place, mine, other, resid, cotangent, columns, out_weight, triple, probs, weight,
        scratch=[pltpu.VMEM((width, tokens), f32), pltpu.VMEM((share, tokens), bf16)]
        + [pltpu.VMEM((width, LANES), f32)] * 3,
        scalars=1,
    )


def last_kernel(
    place_ref, mine, other, rows_ref, dh, columns, cotangent_sums, pre_sums, back_sums, bias_sums,
    out, sums_out, grad, gain_sum, shift_sum, field,
):
    share, tokens = out.shape
    width = rows_ref.shape[0]
    half = width // 2
    place = place_ref[0]
    core = lax.rem(place, 2)
    place_pieces(core, (mine, other), grad)
    gain_sum[...] = jnp.zeros_like(gain_sum)
    shift_sum[...] = jnp.zeros_like(shift_sum)

    def norm_step(index):
        lanes = lanes_at(index, LANES)
        upper = grad[:, lanes]
        normed, back = norm_back(rows_ref[:, lanes].astype(f32), upper, columns[:, 0:1])
        field[...] = dh[:, lanes] + back
        out[:, lanes] = field[pl.ds(pl.multiple_of(place * share, 8), share), :].astype(bf16)
        gain_sum[...] += upper * normed
        shift_sum[...] += upper

    loop(tokens // LANES, norm_step)
    field[:, 0:1] = jnp.sum(gain_sum[...], 1, keepdims=True)
    field[:, 1:2] = jnp.sum(shift_sum[...], 1, keepdims=True)
    field[:, 2:3] = cotangent_sums[...]
    field[:, 3:4] = pre_sums[...]
    field[:, 4:7] = back_sums[:, 0:3]
    field[0:share, 7:9] = bias_sums[:, 0:2]
    sums_out[...] = field[...].T[0:16, :]


def last_call(place, mine, other, rows_all, dh, columns, *sums):
    width, tokens = rows_all.shape
    return call(
        last_kernel,
        "last",
        [struct((width // 4, tokens)), struct((16, width), f32)],
        width * tokens * 12,
        place, mine, other, rows_all, dh, columns, *sums,
        scratch=[pltpu.VMEM((width, tokens), f32)] + [pltpu.VMEM((width, LANES), f32)] * 3,
        scalars=1,
    )


def add_kernel(left, right, out):
    def step(start, size):
        rows = pl.ds(start, size)
        out[rows, :] = add_parts(left[rows, :], right[rows, :])

    by_rows(out.shape[0], step)


def add_call(left, right):
    return call(add_kernel, "add", [struct(left.shape)], left.size, left, right, limit=SMALL)[0]


def add_wide_kernel(left, right, out):
    out[...] = left[...] + right[...]


def add_wide_call(left, right):
    return call(add_wide_kernel, "add_wide", [struct(left.shape, f32)], left.size, left, right, limit=SMALL)[0]


def down_kernel(place_ref, hidden, down, keep_out, send_out):
    tokens = hidden.shape[1]
    share = keep_out.shape[0] // 2
    core = lax.rem(place_ref[0], 2)

    def step(index):
        lanes = lanes_at(index, WIDE)
        part = dot_nn(down[...], hidden[:, lanes]).astype(bf16)
        for chip in range(2):
            rows = slice(share * chip, share * (chip + 1))
            low = part[2 * share * chip : 2 * share * chip + share]
            high = part[2 * share * chip + share : 2 * share * (chip + 1)]

            @pl.when(core == 0)
            def _():
                keep_out[rows, lanes] = low
                send_out[rows, lanes] = high

            @pl.when(core != 0)
            def _():
                keep_out[rows, lanes] = high
                send_out[rows, lanes] = low

    loop(tokens // WIDE, step)


def down_call(place, hidden, down):
    width, inner = down.shape
    tokens = hidden.shape[1]
    return call(
        down_kernel,
        "down",
        [struct((width // 2, tokens))] * 2,
        tokens * width * inner * 2,
        place, hidden, down,
        scalars=1,
    )


def down_add_kernel(place_ref, keep, got, keep_out, send_out, field):
    share = keep_out.shape[0]
    chip = lax.div(place_ref[0], 2)
    field[...] = keep[...].astype(f32) + got[...].astype(f32)
    keep_out[...] = field[pl.ds(pl.multiple_of(chip * share, 8), share), :].astype(bf16)
    send_out[...] = field[pl.ds(pl.multiple_of((1 - chip) * share, 8), share), :].astype(bf16)


def down_add_call(place, keep, got):
    rows, tokens = keep.shape
    return call(
        down_add_kernel,
        "down_add",
        [struct((rows // 2, tokens))] * 2,
        keep.size,
        place, keep, got,
        scratch=[pltpu.VMEM(keep.shape, f32)],
        scalars=1,
    )


def layer_out_kernel(place_ref, keep, got, resid, columns, out):
    share = out.shape[0]
    rows = pl.ds(pl.multiple_of(place_ref[0] * share, 8), share)
    total = keep[...].astype(f32) + got[...].astype(f32)
    out[...] = (resid[rows, :] + total + columns[rows, 6:7]).astype(bf16)


def layer_out_call(place, keep, got, resid, columns):
    return call(
        layer_out_kernel,
        "layer_out",
        [struct(keep.shape)],
        keep.size,
        place, keep, got, resid, columns,
        scalars=1,
    )[0]


def grad_kernel(ranges, place_ref, *refs):
    pairs, (keep_out, send_out) = refs[:-2], refs[-2:]
    side = lax.rem(place_ref[0], 2)
    width = keep_out.shape[1]

    def step(lanes):
        parts = []
        for left, right, (low, high) in zip(pairs[0::2], pairs[1::2], ranges):
            parts.append(dot_nt(left[low:high, :], right[lanes, :]).astype(bf16))
        value = parts[0] if len(parts) == 1 else jnp.concatenate(parts, 0)
        store_halves(side, value, lanes, keep_out, send_out)

    loop(width // WIDE, lambda index: step(lanes_at(index, WIDE)))
    if width % WIDE:
        step(slice(width - width % WIDE, width))


def grad_call(dp_place, ranges, *pairs):
    rows = sum(high - low for low, high in ranges)
    tokens = pairs[0].shape[1]
    width = pairs[1].shape[0]
    return call(
        functools.partial(grad_kernel, ranges),
        "grad",
        [struct((rows // 2, width)), struct((rows // 2, width))],
        2 * rows * tokens * width,
        dp_place, *pairs,
        scalars=1,
    )


def settle_kernel(dp_ref, mine, got, out):
    def copy_from(ref):
        def step(start, size):
            rows = pl.ds(start, size)
            out[rows, :] = ref[rows, :]

        by_rows(out.shape[0], step)

    pl.when(dp_ref[2] == 1)(lambda: copy_from(got))
    pl.when(dp_ref[2] == 0)(lambda: copy_from(mine))


def settle_call(dp, mine, got):
    return call(settle_kernel, "settle", [struct(mine.shape)], mine.size, dp, mine, got, scalars=1, limit=SMALL)[0]


def final_kernel(count, dp_ref, *refs):
    side = lax.rem(dp_ref[0], 2)
    outs = refs[2 * count :]

    def put(start, ref):
        done = 0
        rows = ref.shape[0]
        for out in outs:
            size = out.shape[0]
            low, high = max(start, done), min(start + rows, done + size)
            if low < high:

                def step(begin, count):
                    value = ref[pl.ds(low - start + begin, count), :].astype(f32)
                    out[pl.ds(low - done + begin, count), :] = value

                by_rows(high - low, step)
            done += size

    base = 0
    for place in range(count):
        mine, got = refs[2 * place : 2 * place + 2]
        half = mine.shape[0]

        @pl.when(side == 0)
        def _():
            put(base, mine)
            put(base + half, got)

        @pl.when(side != 0)
        def _():
            put(base, got)
            put(base + half, mine)

        base += 2 * half


def final_call(dp, parts, sizes):
    width = parts[0].shape[1]
    return call(
        functools.partial(final_kernel, len(parts) // 2),
        "final",
        [struct((size, width), f32) for size in sizes],
        sum(sizes) * width,
        dp, *parts,
        scalars=1,
        limit=SMALL,
    )


def swap_core(value):
    return lax.ppermute(value, "tensor", [(place, place ^ 1) for place in range(4)])


def swap_chip(value):
    return lax.ppermute(value, "tensor", [(place, place ^ 2) for place in range(4)])


def after(value, *others):
    return lax.optimization_barrier((value, *others))[0]


def all_pieces(share):
    far = swap_chip(share)
    return share, swap_core(share), far, swap_core(far)


def ordered(bit, mine, other, axis):
    low = jnp.where(bit == 0, mine, other)
    high = jnp.where(bit == 0, other, mine)
    return jnp.concatenate([low, high], axis)


def line_pairs(pairs):
    return [(2 * source + side, 2 * target + side) for source, target in pairs for side in (0, 1)]


INWARD = line_pairs([(0, 1), (3, 2)])
MIDDLE = line_pairs([(1, 2), (2, 1)])
OUTWARD = line_pairs([(1, 0), (2, 3)])
ACROSS = [(place, place ^ 1) for place in range(8)]
ACROSS_MIDDLE = [(2, 3), (3, 2), (4, 5), (5, 4)]


def hop(value, pairs):
    return lax.ppermute(value, "dp", pairs)


STAGES = (ACROSS, INWARD, MIDDLE, OUTWARD, ACROSS)


class CellSum:
    def __init__(self, groups, dp, parts):
        self.groups, self.dp = groups, dp
        self.mine, self.got = parts
        self.stage = -1

    def step(self):
        self.stage += 1
        if self.groups != 8:
            return
        send = self.got
        if self.stage == 4:
            send = self.mine = settle_call(self.dp, self.mine, self.got)
        elif self.stage > 0:
            send = self.mine = add_call(self.mine, self.got)
        self.got = hop(send, STAGES[self.stage])

    def plain(self):
        value = ordered(self.dp[0] % 2, self.mine, self.got, 0)
        return lax.psum(value, "dp").astype(f32)


def finish(sums, sizes):
    if sums[0].groups == 8:
        return final_call(sums[0].dp, [piece for item in sums for piece in (item.mine, item.got)], sizes)
    value = jnp.concatenate([item.plain() for item in sums], 0)
    ends = [sum(sizes[: place + 1]) for place in range(len(sizes))]
    return [value[end - size : end] for end, size in zip(ends, sizes)]


def end_round(sums, *values):
    held = lax.optimization_barrier((*[item.got for item in sums], *values))
    for item, got in zip(sums, held):
        item.got = got
    return held[len(sums) :]


def body(
    groups,
    tokens,
    first_gain,
    first_shift,
    triple_weight,
    triple_bias,
    output_weight,
    output_bias,
    second_gain,
    second_shift,
    up_weight,
    up_bias,
    down_weight,
    down_bias,
    cotangent,
    lengths,
):
    share = tokens.shape[1]
    width = triple_weight.shape[0]
    index = lax.axis_index("tensor").astype(jnp.int32)
    core, chip = index % 2, index // 2
    place = index.reshape(1)
    row = lax.axis_index("dp").astype(jnp.int32)
    at_end = ((row < 2) | (row >= groups - 2)).astype(jnp.int32)
    dp = jnp.stack([row, jnp.int32(groups // 2), at_end])
    CHAIN.clear()
    fence = lambda *values: lax.optimization_barrier(values)
    token_own, grad_own = tokens.T, cotangent.T
    token_far, token_near = swap_chip(token_own), swap_core(token_own)
    grad_near, weight_near = swap_core(grad_own), swap_core(output_weight)
    triple_t = triple_weight.transpose(1, 2, 0).reshape(3 * share, width)
    bias_flat = jnp.concatenate([triple_bias[0], jnp.zeros((share,), f32), triple_bias[1]])[:, None]
    columns = jnp.stack(
        [first_gain, first_shift, output_bias, second_gain, second_shift, up_bias, down_bias], 1
    )
    up_t, triple_plain = up_weight.T, triple_t.T
    token_far, token_near, up_t, triple_plain, columns, bias_flat, out_weight = fence(
        token_far, token_near, up_t, triple_plain, columns, bias_flat, output_weight
    )
    token_both = swap_core(token_far)
    weight_far = swap_chip(out_weight)
    own_t = out_weight.T
    token_both, own_t = fence(token_both, own_t)
    rows_all, first_normed, triple, probs, context = front_call(
        place, lengths, (token_own, token_near, token_far, token_both), columns, triple_t, bias_flat
    )
    context_far, context_near = swap_chip(context), swap_core(context)
    weight_far, weight_near, down_plain, _ = fence(weight_far, weight_near, down_weight, context)
    weight_both = swap_core(weight_far)
    weights = own_t, weight_near.T, weight_far.T, weight_both.T
    down_t = down_plain.T
    context_far, context_near, down_t, grad_own, *weights = fence(
        context_far, context_near, down_t, grad_own, *weights
    )
    context_both = swap_core(context_far)
    grad_far = swap_chip(grad_own)
    resid, second_normed, hidden, slope = middle_call(
        (context, context_near, context_far, context_both), weights, rows_all, columns, up_t
    )
    grad_far, _ = fence(grad_far, second_normed)
    grad_both = swap_core(grad_far)
    grad_rows, cotangent_sums = spread_call(place, (grad_own, grad_near, grad_far, grad_both))
    half = width // 2

    def cell_sum(ranges, *pairs):
        return CellSum(groups, dp, grad_call(dp, ranges, *pairs))

    down_low = cell_sum([(0, half)], hidden, grad_rows)
    down_low.step()
    pre_low, keep, send, pre_sums = turn_call(place, grad_rows, slope, down_weight, up_weight)
    keep, send = end_round([down_low], keep, send)
    near = swap_core(send)
    down_low.step()
    down_keep, down_send = down_call(place, hidden, down_t)
    near = add_call(keep, near)
    far = swap_chip(near)
    down_high = cell_sum([(half, width)], hidden, grad_rows)
    down_high.step()
    down_got = swap_core(down_send)
    up_low = cell_sum([(0, half)], second_normed, pre_low)
    up_high = cell_sum([(half, width)], second_normed, pre_low)
    far, down_got, near, _ = end_round([down_low, down_high], far, down_got, near, up_high.mine)
    mine = add_call(near, far)
    other = swap_core(mine)
    for item in (down_high, down_low, up_low, up_high):
        item.step()
    dh, low, triple_low, keep, send, back_sums, bias_sums = back_call(
        place, mine, other, resid, grad_rows, columns, output_weight, triple, probs, triple_plain
    )
    keep, send = end_round([down_low, down_high, up_low, up_high], keep, send)
    near = swap_core(send)
    early = cell_sum([(0, 2 * share)], triple_low, first_normed)
    near = add_call(keep, near)
    far = swap_chip(near)
    for item in (up_low, down_high, down_low, early):
        item.step()
    late = cell_sum([(2 * share, 3 * share), (0, share)], triple_low, first_normed, context, low)
    far, near, _ = end_round([early, down_low, down_high, up_low, up_high], far, near, late.mine)
    mine = add_call(near, far)
    other = swap_core(mine)
    for item in (early, up_low, down_high, late):
        item.step()
    down_keep, down_send = down_add_call(place, down_keep, down_got)
    down_got = swap_chip(down_send)
    input_grad, small = last_call(
        place, mine, other, rows_all, dh, columns, cotangent_sums, pre_sums, back_sums, bias_sums
    )
    small, down_got = end_round([down_low, down_high, up_low, up_high, early, late], small, down_got)
    shifts = (1, 4, 2)
    if groups != 8:
        small = lax.psum(small, "dp")
    rounds = [
        (late, early, up_low, down_low),
        (up_high, late, early, down_high),
        (up_high, late, up_low),
        (early, up_high),
        (late, up_high),
    ]
    for place_in, items in enumerate(rounds):
        if groups == 8 and place_in < 3:
            got = hop(small, [(spot, spot ^ shifts[place_in]) for spot in range(8)])
        for item in items:
            item.step()
        if place_in == 2:
            down_grad = finish([down_low, down_high], [width])[0]
        if place_in == 0:
            layer_out = layer_out_call(place, down_keep, down_got, resid, columns)
        if groups == 8 and place_in < 3:
            (got,) = end_round(list(items), got)
            small = add_wide_call(small, got)
        else:
            end_round(list(items))
    up_grad = finish([up_low, up_high], [width])[0]
    triple_grad, output_grad = finish([early, late], [3 * share, share])
    triple_grad = triple_grad.reshape(3, share, width).transpose(2, 0, 1)
    return (
        layer_out.T,
        input_grad.T,
        small[0],
        small[1],
        triple_grad,
        small[7:9, :share],
        output_grad,
        small[6],
        small[4],
        small[5],
        up_grad,
        small[3],
        down_grad,
        small[2],
    )


def solution(mesh):
    placed = (
        P("dp", "tensor"),
        P(),
        P(),
        P(None, None, "tensor"),
        P(None, "tensor"),
        P("tensor", None),
        P(),
        P(),
        P(),
        P(None, "tensor"),
        P("tensor"),
        P("tensor", None),
        P(),
        P("dp", "tensor"),
        P("dp"),
    )
    return jax.shard_map(
        functools.partial(body, mesh.shape["dp"]),
        mesh=mesh,
        in_specs=placed,
        out_specs=(
            P("dp", "tensor"),
            P("dp", "tensor"),
            P(),
            P(),
            P(None, None, "tensor"),
            P(None, "tensor"),
            P("tensor", None),
            P(),
            P(),
            P(),
            P(None, "tensor"),
            P("tensor"),
            P("tensor", None),
            P(),
        ),
        check_vma=False,
    )
```

```python
import functools

import jax
import jax.numpy as jnp
from jax import lax
from jax.experimental import pallas as pl
from jax.experimental.pallas import tpu as pltpu
from jax.sharding import PartitionSpec as P

HEAD_DIM = 56
CELL_LEN = 384
LANES = 128
WIDE = 256
epsilon = 1e-05
CURVE = 0.7978845608028654
CUBIC = 0.044715
bf16 = jnp.bfloat16
f32 = jnp.float32
MIB = 1024 * 1024
SMALL = 6


def dot_nn(left, right):
    return lax.dot_general(left, right, (((1,), (0,)), ((), ())), preferred_element_type=f32)


def dot_nt(left, right):
    return lax.dot_general(left, right, (((1,), (1,)), ((), ())), preferred_element_type=f32)


def dot_tn(left, right):
    return lax.dot_general(left, right, (((0,), (0,)), ((), ())), preferred_element_type=f32)


def struct(shape, dtype=bf16):
    return jax.ShapeDtypeStruct(shape, dtype)


CHAIN = []


def in_turn(arguments, first):
    if CHAIN:
        held = lax.optimization_barrier((arguments[first], CHAIN[0]))[0]
        arguments = (*arguments[:first], held, *arguments[first + 1 :])
    return arguments


def call(kernel, name, out_shape, flops, *arguments, scratch=(), scalars=0, limit=12, transcendentals=0, far_in=(), far_out=()):
    inputs = [pl.ANY if place in far_in else pltpu.VMEM for place in range(len(arguments) - scalars)]
    outputs = [pl.ANY if place in far_out else pltpu.VMEM for place in range(len(out_shape))]
    results = pl.pallas_call(
        kernel,
        in_specs=[pl.BlockSpec(memory_space=space) for space in [pltpu.SMEM] * scalars + inputs],
        out_specs=[pl.BlockSpec(memory_space=space) for space in outputs],
        out_shape=out_shape,
        scratch_shapes=scratch,
        compiler_params=pltpu.CompilerParams(vmem_limit_bytes=limit * MIB),
        name=name,
    )(*in_turn(arguments, scalars))
    CHAIN[:] = results[:1]
    return results


def loop(count, step):
    def wrapped(index, carry):
        step(index)
        return carry

    lax.fori_loop(0, count, wrapped, 0)


def by_rows(rows, step):
    whole = rows // 64

    def block(index):
        step(pl.multiple_of(index * 64, 64), 64)

    loop(whole, block)
    if rows % 64:
        step(64 * whole, rows % 64)


def lanes_at(index, size):
    return pl.ds(pl.multiple_of(index * size, size), size)


def start_copies(pairs, sems, first=0):
    copies = [
        pltpu.make_async_copy(source, target, sems.at[first + place])
        for place, (source, target) in enumerate(pairs)
    ]
    for copy in copies:
        copy.start()
    return copies


def wait_for(copies):
    for copy in copies:
        copy.wait()


def place_pieces(place, refs, target):
    share = refs[0].shape[0]
    for offset, ref in enumerate(refs):
        base = lax.bitwise_xor(place, offset) * share

        def step(start, size):
            value = ref[pl.ds(start, size), :].astype(target.dtype)
            target[pl.ds(pl.multiple_of(base + start, 8), size), :] = value

        by_rows(share, step)


def norm_columns(field, gain, shift):
    center = field - jnp.mean(field, 0, keepdims=True)
    spread = jnp.mean(center * center, 0, keepdims=True)
    return center * lax.rsqrt(spread + epsilon) * gain + shift


def front_kernel(
    place_ref, length_ref, own, near, far, both, weight_far, columns, bias,
    rows_far, normed_far, triple_far, probs_far, context_out,
    field, pieces, weight, rows_out, normed_out, triple_out, probs_out, sems,
):
    share = context_out.shape[0]
    heads = share // HEAD_DIM
    tokens = rows_out.shape[1]
    arrived = [pieces.at[offset] for offset in range(4)]
    copies = start_copies([*zip((own, near, far, both), arrived), (weight_far, weight)], sems)
    wait_for(copies[:4])
    place_pieces(place_ref[0], arrived, field)

    def norm_step(index):
        lanes = lanes_at(index, LANES)
        value = field[:, lanes]
        rows_out[:, lanes] = value.astype(bf16)
        normed_out[:, lanes] = norm_columns(value, columns[:, 0:1], columns[:, 1:2]).astype(bf16)

    loop(tokens // LANES, norm_step)
    copies[4].wait()
    leaving = start_copies([(rows_out, rows_far), (normed_out, normed_far)], sems, 5)

    def project_step(index):
        lanes = lanes_at(index, WIDE)
        triple_out[:, lanes] = (dot_nn(weight[...], normed_out[:, lanes]) + bias[...]).astype(bf16)

    loop(tokens // WIDE, project_step)
    leaving += start_copies([(triple_out, triple_far)], sems, 7)
    factor = HEAD_DIM ** (-0.5)

    def cell_step(cell):
        length = length_ref[cell]
        for head in range(heads):
            start = HEAD_DIM * head
            for block in range(CELL_LEN // LANES):
                span = LANES * (block + 1)
                base = pl.multiple_of(cell * CELL_LEN, LANES)
                here = pl.ds(pl.multiple_of(base + LANES * block, LANES), LANES)
                queries = triple_out[start : start + HEAD_DIM, here]
                keys = triple_out[share + start : share + start + HEAD_DIM, pl.ds(base, span)]
                values = triple_out[2 * share + start : 2 * share + start + HEAD_DIM, pl.ds(base, span)]
                scores = dot_tn(keys, queries) * factor
                key_place = lax.broadcasted_iota(jnp.int32, (span, LANES), 0)
                query_place = lax.broadcasted_iota(jnp.int32, (span, LANES), 1) + LANES * block
                allowed = (key_place <= query_place) & (key_place < length)
                masked = jnp.where(allowed, scores, -1e30)
                expo = jnp.exp(masked - jnp.max(masked, 0, keepdims=True))
                probs = (expo / jnp.sum(expo, 0, keepdims=True)).astype(bf16)
                probs_out[cell, head, :span, LANES * block : span] = probs
                context_out[start : start + HEAD_DIM, here] = dot_nn(values, probs).astype(bf16)
        pltpu.make_async_copy(probs_out.at[cell], probs_far.at[cell], sems.at[8 + cell]).start()

    loop(tokens // CELL_LEN, cell_step)
    for cell in range(tokens // CELL_LEN):
        pltpu.make_async_copy(probs_out.at[cell], probs_far.at[cell], sems.at[8 + cell]).wait()
    wait_for(leaving)


def front_call(place, lengths, pieces, columns, weight, bias):
    share, tokens = pieces[0].shape
    width = weight.shape[1]
    heads = share // HEAD_DIM
    cells = tokens // CELL_LEN
    pairs = cells * heads * CELL_LEN * CELL_LEN
    return call(
        front_kernel,
        "front",
        [
            struct((width, tokens)),
            struct((width, tokens)),
            struct((3 * share, tokens)),
            struct((cells, heads, CELL_LEN, CELL_LEN)),
            struct((share, tokens)),
        ],
        tokens * width * share * 6 + pairs * HEAD_DIM * 4,
        place, lengths, *pieces, weight, columns, bias,
        scratch=[
            pltpu.VMEM((width, tokens), f32),
            pltpu.VMEM((4, share, tokens), bf16),
            pltpu.VMEM(weight.shape, bf16),
            pltpu.VMEM((width, tokens), bf16),
            pltpu.VMEM((width, tokens), bf16),
            pltpu.VMEM((3 * share, tokens), bf16),
            pltpu.VMEM((cells, heads, CELL_LEN, CELL_LEN), bf16),
            pltpu.SemaphoreType.DMA((8 + cells,)),
        ],
        scalars=2,
        limit=60,
        far_in=range(5),
        far_out=range(4),
        transcendentals=pairs,
    )


def gate_parts(value):
    square = value * value
    bend = jnp.tanh(CURVE * (value + CUBIC * square * value))
    upper = 0.5 * (1.0 + bend)
    slope = upper + 0.5 * value * (1.0 - bend * bend) * CURVE * (1.0 + 3.0 * CUBIC * square)
    return value * upper, slope


def middle_kernel(
    own, near, far, both, own_weight, near_weight, far_weight, both_weight, rows_far, up_far, columns,
    resid_far, normed_far, hidden_out, slope_out,
    field, weight, pieces, weights, rows_ref, up, resid_out, normed_out, sems,
):
    tokens = resid_out.shape[1]
    share = own.shape[0]
    sources = own, near, far, both, own_weight, near_weight, far_weight, both_weight
    targets = [pieces.at[place] for place in range(4)] + [weights.at[place] for place in range(4)]
    copies = start_copies([*zip(sources, targets), (rows_far, rows_ref), (up_far, up)], sems)
    wait_for(copies[:8])
    place_pieces(0, [pieces.at[place] for place in range(4)], field)
    for place in range(4):
        weight[:, share * place : share * (place + 1)] = weights[place]
    wait_for(copies[8:])

    def leaving(index):
        lanes = lanes_at(index, WIDE)
        resid_copy = pltpu.make_async_copy(
            resid_out.at[:, lanes], resid_far.at[:, lanes], sems.at[10 + 2 * index]
        )
        normed_copy = pltpu.make_async_copy(
            normed_out.at[:, lanes], normed_far.at[:, lanes], sems.at[11 + 2 * index]
        )
        return resid_copy, normed_copy

    def step(index):
        lanes = lanes_at(index, WIDE)
        added = dot_nn(weight[...], field[:, lanes].astype(bf16))
        resid = rows_ref[:, lanes].astype(f32) + added + columns[:, 2:3]
        resid_out[:, lanes] = resid
        normed = norm_columns(resid, columns[:, 3:4], columns[:, 4:5]).astype(bf16)
        normed_out[:, lanes] = normed
        hidden, slope = gate_parts(dot_nn(up[...], normed) + columns[:, 5:6])
        hidden_out[:, lanes] = hidden.astype(bf16)
        slope_out[:, lanes] = slope
        for copy in leaving(index):
            copy.start()

    loop(tokens // WIDE, step)
    for index in range(tokens // WIDE):
        wait_for(leaving(index))


def middle_call(pieces, weights, rows_all, columns, up):
    width, tokens = rows_all.shape
    hidden = up.shape[0]
    return call(
        middle_kernel,
        "middle",
        [
            struct((width, tokens), f32),
            struct((width, tokens)),
            struct((hidden, tokens)),
            struct((hidden, tokens), f32),
        ],
        tokens * width * (width + hidden) * 2,
        *pieces, *weights, rows_all, up, columns,
        scratch=[
            pltpu.VMEM((width, tokens), f32),
            pltpu.VMEM((width, width), bf16),
            pltpu.VMEM((4, *pieces[0].shape), bf16),
            pltpu.VMEM((4, *weights[0].shape), bf16),
            pltpu.VMEM((width, tokens), bf16),
            pltpu.VMEM(up.shape, bf16),
            pltpu.VMEM((width, tokens), f32),
            pltpu.VMEM((width, tokens), bf16),
            pltpu.SemaphoreType.DMA((10 + 2 * (tokens // WIDE),)),
        ],
        limit=53,
        far_in=range(10),
        far_out=range(2),
        transcendentals=tokens * hidden,
    )


def spread_kernel(place_ref, own, near, far, both, rows_out, sums_out, field):
    place_pieces(place_ref[0], (own, near, far, both), field)
    rows_out[...] = field[...].astype(bf16)
    sums_out[...] = jnp.sum(field[...], 1, keepdims=True)


def spread_call(place, pieces):
    share, tokens = pieces[0].shape
    return call(
        spread_kernel,
        "spread",
        [struct((4 * share, tokens)), struct((4 * share, 1), f32)],
        4 * share * tokens,
        place, *pieces,
        scratch=[pltpu.VMEM((4 * share, tokens), f32)],
        scalars=1,
    )


def store_halves(bit, value, lanes, keep_out, send_out):
    half = keep_out.shape[0]

    @pl.when(bit == 0)
    def _():
        keep_out[:, lanes] = value[:half]
        send_out[:, lanes] = value[half:]

    @pl.when(bit != 0)
    def _():
        keep_out[:, lanes] = value[half:]
        send_out[:, lanes] = value[:half]


def turn_kernel(
    place_ref, cotangent, slope, down, up, pre_out, keep_out, send_out, sums_out,
):
    tokens = cotangent.shape[1]
    core = lax.rem(place_ref[0], 2)
    sums_out[...] = jnp.zeros_like(sums_out)

    def step(index):
        lanes = lanes_at(index, WIDE)
        pre = dot_nn(down[...], cotangent[:, lanes]) * slope[:, lanes]
        sums_out[...] += jnp.sum(pre, 1, keepdims=True)
        low = pre.astype(bf16)
        pre_out[:, lanes] = low
        store_halves(core, dot_nn(up[...], low).astype(bf16), lanes, keep_out, send_out)

    loop(tokens // WIDE, step)


def turn_call(place, cotangent, slope, down, up):
    width, tokens = cotangent.shape
    hidden = up.shape[1]
    return call(
        turn_kernel,
        "turn",
        [
            struct((hidden, tokens)),
            struct((width // 2, tokens)),
            struct((width // 2, tokens)),
            struct((hidden, 1), f32),
        ],
        tokens * width * hidden * 4,
        place, cotangent, slope, down, up,
        scalars=1,
    )


def norm_back(field, grad, gain):
    center = field - jnp.mean(field, 0, keepdims=True)
    inverse = lax.rsqrt(jnp.mean(center * center, 0, keepdims=True) + epsilon)
    normed = center * inverse
    scaled = grad * gain
    inner = jnp.mean(scaled * normed, 0, keepdims=True)
    back = inverse * (scaled - jnp.mean(scaled, 0, keepdims=True) - normed * inner)
    return normed, back


def add_parts(left, right):
    return (left.astype(f32) + right.astype(f32)).astype(bf16)


def back_kernel(
    place_ref, mine, other, resid, cotangent, columns, out_weight, triple, probs_ref, weight,
    dh_out, low_out, triple_out, keep_out, send_out, sums_out, bias_out,
    grad, context_grad, gain_sum, shift_sum, total_sum,
):
    share = out_weight.shape[0]
    width, tokens = resid.shape
    half = width // 2
    heads = share // HEAD_DIM
    factor = HEAD_DIM ** (-0.5)
    core = lax.rem(place_ref[0], 2)
    place_pieces(core, (mine, other), grad)
    for item in (gain_sum, shift_sum, total_sum, bias_out):
        item[...] = jnp.zeros_like(item)

    def norm_step(index):
        lanes = lanes_at(index, LANES)
        upper = grad[:, lanes]
        normed, back = norm_back(resid[:, lanes], upper, columns[:, 3:4])
        total = cotangent[:, lanes].astype(f32) + back
        dh_out[:, lanes] = total
        low_out[:, lanes] = total.astype(bf16)
        gain_sum[...] += upper * normed
        shift_sum[...] += upper
        total_sum[...] += total

    loop(tokens // LANES, norm_step)
    sums_out[:, 0:1] = jnp.sum(gain_sum[...], 1, keepdims=True)
    sums_out[:, 1:2] = jnp.sum(shift_sum[...], 1, keepdims=True)
    sums_out[:, 2:3] = jnp.sum(total_sum[...], 1, keepdims=True)

    def context_step(index):
        lanes = lanes_at(index, WIDE)
        context_grad[:, lanes] = dot_nn(out_weight[...], low_out[:, lanes]).astype(bf16)

    loop(tokens // WIDE, context_step)
    blocks = CELL_LEN // LANES

    def cell_step(cell):
        base = pl.multiple_of(cell * CELL_LEN, LANES)
        for head in range(heads):
            start = HEAD_DIM * head
            query_rows = slice(start, start + HEAD_DIM)
            key_rows = slice(share + start, share + start + HEAD_DIM)
            value_rows = slice(2 * share + start, 2 * share + start + HEAD_DIM)
            key_grads = [None] * blocks
            value_grads = [None] * blocks
            query_sum = jnp.zeros((HEAD_DIM, 1), f32)
            value_sum = jnp.zeros((HEAD_DIM, 1), f32)
            for block in range(blocks):
                span = LANES * (block + 1)
                here = pl.ds(pl.multiple_of(base + LANES * block, LANES), LANES)
                queries = triple[query_rows, here]
                keys = triple[key_rows, pl.ds(base, span)]
                values = triple[value_rows, pl.ds(base, span)]
                low = context_grad[query_rows, here]
                probs_low = probs_ref[cell, head, :span, LANES * block : span]
                probs = probs_low.astype(f32)
                prob_grad = dot_tn(values, low)
                inner = jnp.sum(prob_grad * probs, 0, keepdims=True)
                score = (probs * (prob_grad - inner) * factor).astype(bf16)
                query_grad = dot_nn(keys, score)
                query_sum += jnp.sum(query_grad, 1, keepdims=True)
                triple_out[query_rows, here] = query_grad.astype(bf16)
                key_part = dot_nt(queries, score)
                value_part = dot_nt(low, probs_low)
                for place in range(block + 1):
                    lanes = slice(LANES * place, LANES * (place + 1))
                    if key_grads[place] is None:
                        key_grads[place] = key_part[:, lanes]
                        value_grads[place] = value_part[:, lanes]
                    else:
                        key_grads[place] += key_part[:, lanes]
                        value_grads[place] += value_part[:, lanes]
            for block in range(blocks):
                here = pl.ds(pl.multiple_of(base + LANES * block, LANES), LANES)
                triple_out[key_rows, here] = key_grads[block].astype(bf16)
                triple_out[value_rows, here] = value_grads[block].astype(bf16)
                value_sum += jnp.sum(value_grads[block], 1, keepdims=True)
            bias_out[query_rows, 0:1] += query_sum
            bias_out[query_rows, 1:2] += value_sum

    loop(tokens // CELL_LEN, cell_step)

    def part_step(index):
        lanes = lanes_at(index, WIDE)
        part = dot_nn(weight[...], triple_out[:, lanes]).astype(bf16)
        store_halves(core, part, lanes, keep_out, send_out)

    loop(tokens // WIDE, part_step)


def back_call(place, mine, other, resid, cotangent, columns, out_weight, triple, probs, weight):
    width, tokens = resid.shape
    share = out_weight.shape[0]
    cells, heads = probs.shape[:2]
    pairs = cells * heads * CELL_LEN * CELL_LEN
    return call(
        back_kernel,
        "back",
        [
            struct((width, tokens), f32),
            struct((width, tokens)),
            struct((3 * share, tokens)),
            struct((width // 2, tokens)),
            struct((width // 2, tokens)),
            struct((width, 8), f32),
            struct((share, 8), f32),
        ],
        tokens * width * share * 8 + pairs * HEAD_DIM * 8,
        place, mine, other, resid, cotangent, columns, out_weight, triple, probs, weight,
        scratch=[pltpu.VMEM((width, tokens), f32), pltpu.VMEM((share, tokens), bf16)]
        + [pltpu.VMEM((width, LANES), f32)] * 3,
        scalars=1,
    )


def last_kernel(
    place_ref, mine, other, rows_ref, dh, columns, cotangent_sums, pre_sums, back_sums, bias_sums,
    out, sums_out, grad, gain_sum, shift_sum, field,
):
    share, tokens = out.shape
    width = rows_ref.shape[0]
    half = width // 2
    place = place_ref[0]
    core = lax.rem(place, 2)
    place_pieces(core, (mine, other), grad)
    gain_sum[...] = jnp.zeros_like(gain_sum)
    shift_sum[...] = jnp.zeros_like(shift_sum)

    def norm_step(index):
        lanes = lanes_at(index, LANES)
        upper = grad[:, lanes]
        normed, back = norm_back(rows_ref[:, lanes].astype(f32), upper, columns[:, 0:1])
        field[...] = dh[:, lanes] + back
        out[:, lanes] = field[pl.ds(pl.multiple_of(place * share, 8), share), :].astype(bf16)
        gain_sum[...] += upper * normed
        shift_sum[...] += upper

    loop(tokens // LANES, norm_step)
    field[:, 0:1] = jnp.sum(gain_sum[...], 1, keepdims=True)
    field[:, 1:2] = jnp.sum(shift_sum[...], 1, keepdims=True)
    field[:, 2:3] = cotangent_sums[...]
    field[:, 3:4] = pre_sums[...]
    field[:, 4:7] = back_sums[:, 0:3]
    field[0:share, 7:9] = bias_sums[:, 0:2]
    sums_out[...] = field[...].T[0:16, :]


def last_call(place, mine, other, rows_all, dh, columns, *sums):
    width, tokens = rows_all.shape
    return call(
        last_kernel,
        "last",
        [struct((width // 4, tokens)), struct((16, width), f32)],
        width * tokens * 12,
        place, mine, other, rows_all, dh, columns, *sums,
        scratch=[pltpu.VMEM((width, tokens), f32)] + [pltpu.VMEM((width, LANES), f32)] * 3,
        scalars=1,
    )


def add_kernel(left, right, out):
    def step(start, size):
        rows = pl.ds(start, size)
        out[rows, :] = add_parts(left[rows, :], right[rows, :])

    by_rows(out.shape[0], step)


def add_call(left, right):
    return call(add_kernel, "add", [struct(left.shape)], left.size, left, right, limit=SMALL)[0]


def add_wide_kernel(left, right, out):
    out[...] = left[...] + right[...]


def add_wide_call(left, right):
    return call(add_wide_kernel, "add_wide", [struct(left.shape, f32)], left.size, left, right, limit=SMALL)[0]


def down_kernel(place_ref, hidden, down, keep_out, send_out):
    tokens = hidden.shape[1]
    share = keep_out.shape[0] // 2
    core = lax.rem(place_ref[0], 2)

    def step(index):
        lanes = lanes_at(index, WIDE)
        part = dot_nn(down[...], hidden[:, lanes]).astype(bf16)
        for chip in range(2):
            rows = slice(share * chip, share * (chip + 1))
            low = part[2 * share * chip : 2 * share * chip + share]
            high = part[2 * share * chip + share : 2 * share * (chip + 1)]

            @pl.when(core == 0)
            def _():
                keep_out[rows, lanes] = low
                send_out[rows, lanes] = high

            @pl.when(core != 0)
            def _():
                keep_out[rows, lanes] = high
                send_out[rows, lanes] = low

    loop(tokens // WIDE, step)


def down_call(place, hidden, down):
    width, inner = down.shape
    tokens = hidden.shape[1]
    return call(
        down_kernel,
        "down",
        [struct((width // 2, tokens))] * 2,
        tokens * width * inner * 2,
        place, hidden, down,
        scalars=1,
    )


def down_add_kernel(place_ref, keep, got, keep_out, send_out, field):
    share = keep_out.shape[0]
    chip = lax.div(place_ref[0], 2)
    field[...] = keep[...].astype(f32) + got[...].astype(f32)
    keep_out[...] = field[pl.ds(pl.multiple_of(chip * share, 8), share), :].astype(bf16)
    send_out[...] = field[pl.ds(pl.multiple_of((1 - chip) * share, 8), share), :].astype(bf16)


def down_add_call(place, keep, got):
    rows, tokens = keep.shape
    return call(
        down_add_kernel,
        "down_add",
        [struct((rows // 2, tokens))] * 2,
        keep.size,
        place, keep, got,
        scratch=[pltpu.VMEM(keep.shape, f32)],
        scalars=1,
    )


def layer_out_kernel(place_ref, keep, got, resid, columns, out):
    share = out.shape[0]
    rows = pl.ds(pl.multiple_of(place_ref[0] * share, 8), share)
    total = keep[...].astype(f32) + got[...].astype(f32)
    out[...] = (resid[rows, :] + total + columns[rows, 6:7]).astype(bf16)


def layer_out_call(place, keep, got, resid, columns):
    return call(
        layer_out_kernel,
        "layer_out",
        [struct(keep.shape)],
        keep.size,
        place, keep, got, resid, columns,
        scalars=1,
    )[0]


def grad_kernel(ranges, place_ref, *refs):
    pairs, (keep_out, send_out) = refs[:-2], refs[-2:]
    side = lax.rem(place_ref[0], 2)
    width = keep_out.shape[1]

    def step(lanes):
        parts = []
        for left, right, (low, high) in zip(pairs[0::2], pairs[1::2], ranges):
            parts.append(dot_nt(left[low:high, :], right[lanes, :]).astype(bf16))
        value = parts[0] if len(parts) == 1 else jnp.concatenate(parts, 0)
        store_halves(side, value, lanes, keep_out, send_out)

    loop(width // WIDE, lambda index: step(lanes_at(index, WIDE)))
    if width % WIDE:
        step(slice(width - width % WIDE, width))


def grad_call(dp_place, ranges, *pairs):
    rows = sum(high - low for low, high in ranges)
    tokens = pairs[0].shape[1]
    width = pairs[1].shape[0]
    return call(
        functools.partial(grad_kernel, ranges),
        "grad",
        [struct((rows // 2, width)), struct((rows // 2, width))],
        2 * rows * tokens * width,
        dp_place, *pairs,
        scalars=1,
    )


def settle_kernel(dp_ref, mine, got, out):
    def copy_from(ref):
        def step(start, size):
            rows = pl.ds(start, size)
            out[rows, :] = ref[rows, :]

        by_rows(out.shape[0], step)

    pl.when(dp_ref[2] == 1)(lambda: copy_from(got))
    pl.when(dp_ref[2] == 0)(lambda: copy_from(mine))


def settle_call(dp, mine, got):
    return call(settle_kernel, "settle", [struct(mine.shape)], mine.size, dp, mine, got, scalars=1, limit=SMALL)[0]


def final_kernel(count, dp_ref, *refs):
    side = lax.rem(dp_ref[0], 2)
    outs = refs[2 * count :]

    def put(start, ref):
        done = 0
        rows = ref.shape[0]
        for out in outs:
            size = out.shape[0]
            low, high = max(start, done), min(start + rows, done + size)
            if low < high:

                def step(begin, count):
                    value = ref[pl.ds(low - start + begin, count), :].astype(f32)
                    out[pl.ds(low - done + begin, count), :] = value

                by_rows(high - low, step)
            done += size

    base = 0
    for place in range(count):
        mine, got = refs[2 * place : 2 * place + 2]
        half = mine.shape[0]

        @pl.when(side == 0)
        def _():
            put(base, mine)
            put(base + half, got)

        @pl.when(side != 0)
        def _():
            put(base, got)
            put(base + half, mine)

        base += 2 * half


def final_call(dp, parts, sizes):
    width = parts[0].shape[1]
    return call(
        functools.partial(final_kernel, len(parts) // 2),
        "final",
        [struct((size, width), f32) for size in sizes],
        sum(sizes) * width,
        dp, *parts,
        scalars=1,
        limit=SMALL,
    )


def swap_core(value):
    return lax.ppermute(value, "tensor", [(place, place ^ 1) for place in range(4)])


def swap_chip(value):
    return lax.ppermute(value, "tensor", [(place, place ^ 2) for place in range(4)])


def after(value, *others):
    return lax.optimization_barrier((value, *others))[0]


def all_pieces(share):
    far = swap_chip(share)
    return share, swap_core(share), far, swap_core(far)


def ordered(bit, mine, other, axis):
    low = jnp.where(bit == 0, mine, other)
    high = jnp.where(bit == 0, other, mine)
    return jnp.concatenate([low, high], axis)


def line_pairs(pairs):
    return [(2 * source + side, 2 * target + side) for source, target in pairs for side in (0, 1)]


INWARD = line_pairs([(0, 1), (3, 2)])
MIDDLE = line_pairs([(1, 2), (2, 1)])
OUTWARD = line_pairs([(1, 0), (2, 3)])
ACROSS = [(place, place ^ 1) for place in range(8)]
ACROSS_MIDDLE = [(2, 3), (3, 2), (4, 5), (5, 4)]


def hop(value, pairs):
    return lax.ppermute(value, "dp", pairs)


STAGES = (ACROSS, INWARD, MIDDLE, OUTWARD, ACROSS)


class CellSum:
    def __init__(self, groups, dp, parts):
        self.groups, self.dp = groups, dp
        self.mine, self.got = parts
        self.stage = -1

    def step(self):
        self.stage += 1
        if self.groups != 8:
            return
        send = self.got
        if self.stage == 4:
            send = self.mine = settle_call(self.dp, self.mine, self.got)
        elif self.stage > 0:
            send = self.mine = add_call(self.mine, self.got)
        self.got = hop(send, STAGES[self.stage])

    def plain(self):
        value = ordered(self.dp[0] % 2, self.mine, self.got, 0)
        return lax.psum(value, "dp").astype(f32)


def finish(sums, sizes):
    if sums[0].groups == 8:
        return final_call(sums[0].dp, [piece for item in sums for piece in (item.mine, item.got)], sizes)
    value = jnp.concatenate([item.plain() for item in sums], 0)
    ends = [sum(sizes[: place + 1]) for place in range(len(sizes))]
    return [value[end - size : end] for end, size in zip(ends, sizes)]


def end_round(sums, *values):
    held = lax.optimization_barrier((*[item.got for item in sums], *values))
    for item, got in zip(sums, held):
        item.got = got
    return held[len(sums) :]


def body(
    groups,
    tokens,
    first_gain,
    first_shift,
    triple_weight,
    triple_bias,
    output_weight,
    output_bias,
    second_gain,
    second_shift,
    up_weight,
    up_bias,
    down_weight,
    down_bias,
    cotangent,
    lengths,
):
    share = tokens.shape[1]
    width = triple_weight.shape[0]
    index = lax.axis_index("tensor").astype(jnp.int32)
    core, chip = index % 2, index // 2
    place = index.reshape(1)
    row = lax.axis_index("dp").astype(jnp.int32)
    at_end = ((row < 2) | (row >= groups - 2)).astype(jnp.int32)
    dp = jnp.stack([row, jnp.int32(groups // 2), at_end])
    CHAIN.clear()
    fence = lambda *values: lax.optimization_barrier(values)
    token_own, grad_own = tokens.T, cotangent.T
    token_far, token_near = swap_chip(token_own), swap_core(token_own)
    grad_near, weight_near = swap_core(grad_own), swap_core(output_weight)
    triple_t = triple_weight.transpose(1, 2, 0).reshape(3 * share, width)
    bias_flat = jnp.concatenate([triple_bias[0], jnp.zeros((share,), f32), triple_bias[1]])[:, None]
    columns = jnp.stack(
        [first_gain, first_shift, output_bias, second_gain, second_shift, up_bias, down_bias], 1
    )
    up_t, triple_plain = up_weight.T, triple_t.T
    token_far, token_near, up_t, triple_plain, columns, bias_flat, out_weight = fence(
        token_far, token_near, up_t, triple_plain, columns, bias_flat, output_weight
    )
    token_both = swap_core(token_far)
    weight_far = swap_chip(out_weight)
    own_t = out_weight.T
    token_both, own_t = fence(token_both, own_t)
    rows_all, first_normed, triple, probs, context = front_call(
        place, lengths, (token_own, token_near, token_far, token_both), columns, triple_t, bias_flat
    )
    context_far, context_near = swap_chip(context), swap_core(context)
    weight_far, weight_near, down_plain, _ = fence(weight_far, weight_near, down_weight, context)
    weight_both = swap_core(weight_far)
    weights = own_t, weight_near.T, weight_far.T, weight_both.T
    down_t = down_plain.T
    context_far, context_near, down_t, grad_own, *weights = fence(
        context_far, context_near, down_t, grad_own, *weights
    )
    context_both = swap_core(context_far)
    grad_far = swap_chip(grad_own)
    resid, second_normed, hidden, slope = middle_call(
        (context, context_near, context_far, context_both), weights, rows_all, columns, up_t
    )
    grad_far, _ = fence(grad_far, second_normed)
    grad_both = swap_core(grad_far)
    grad_rows, cotangent_sums = spread_call(place, (grad_own, grad_near, grad_far, grad_both))
    half = width // 2

    def cell_sum(ranges, *pairs):
        return CellSum(groups, dp, grad_call(dp, ranges, *pairs))

    down_low = cell_sum([(0, half)], hidden, grad_rows)
    down_low.step()
    pre_low, keep, send, pre_sums = turn_call(place, grad_rows, slope, down_weight, up_weight)
    keep, send = end_round([down_low], keep, send)
    near = swap_core(send)
    down_low.step()
    down_keep, down_send = down_call(place, hidden, down_t)
    near = add_call(keep, near)
    far = swap_chip(near)
    down_high = cell_sum([(half, width)], hidden, grad_rows)
    down_high.step()
    down_got = swap_core(down_send)
    up_low = cell_sum([(0, half)], second_normed, pre_low)
    up_high = cell_sum([(half, width)], second_normed, pre_low)
    far, down_got, near, _ = end_round([down_low, down_high], far, down_got, near, up_high.mine)
    mine = add_call(near, far)
    other = swap_core(mine)
    for item in (down_high, down_low, up_low, up_high):
        item.step()
    down_keep, down_send = down_add_call(place, down_keep, down_got)
    down_got = swap_chip(down_send)
    dh, low, triple_low, keep, send, back_sums, bias_sums = back_call(
        place, mine, other, resid, grad_rows, columns, output_weight, triple, probs, triple_plain
    )
    keep, send, down_got = end_round([down_low, down_high, up_low, up_high], keep, send, down_got)
    near = swap_core(send)
    early = cell_sum([(0, 2 * share)], triple_low, first_normed)
    near = add_call(keep, near)
    far = swap_chip(near)
    for item in (up_low, down_high, down_low, early):
        item.step()
    late = cell_sum([(2 * share, 3 * share), (0, share)], triple_low, first_normed, context, low)
    far, near, _ = end_round([early, down_low, down_high, up_low, up_high], far, near, late.mine)
    mine = add_call(near, far)
    other = swap_core(mine)
    for item in (early, up_low, down_high, late):
        item.step()
    input_grad, small = last_call(
        place, mine, other, rows_all, dh, columns, cotangent_sums, pre_sums, back_sums, bias_sums
    )
    (small,) = end_round([down_low, down_high, up_low, up_high, early, late], small)
    shifts = (1, 4, 2)
    if groups != 8:
        small = lax.psum(small, "dp")
    rounds = [
        (late, early, up_low, down_low),
        (up_high, late, early, down_high),
        (up_high, late, up_low),
        (early, up_high),
        (up_high, late),
    ]
    for place_in, items in enumerate(rounds):
        if groups == 8 and place_in < 3:
            got = hop(small, [(spot, spot ^ shifts[place_in]) for spot in range(8)])
        for item in items:
            item.step()
        if place_in == 2:
            down_grad = finish([down_low, down_high], [width])[0]
        if place_in == 0:
            layer_out = layer_out_call(place, down_keep, down_got, resid, columns)
        if groups == 8 and place_in < 3:
            (got,) = end_round(list(items), got)
            small = add_wide_call(small, got)
        elif place_in < 4:
            end_round(list(items))
    up_grad = finish([up_low, up_high], [width])[0]
    triple_grad, output_grad = finish([early, late], [3 * share, share])
    triple_grad = triple_grad.reshape(3, share, width).transpose(2, 0, 1)
    return (
        layer_out.T,
        input_grad.T,
        small[0],
        small[1],
        triple_grad,
        small[7:9, :share],
        output_grad,
        small[6],
        small[4],
        small[5],
        up_grad,
        small[3],
        down_grad,
        small[2],
    )


def solution(mesh):
    placed = (
        P("dp", "tensor"),
        P(),
        P(),
        P(None, None, "tensor"),
        P(None, "tensor"),
        P("tensor", None),
        P(),
        P(),
        P(),
        P(None, "tensor"),
        P("tensor"),
        P("tensor", None),
        P(),
        P("dp", "tensor"),
        P("dp"),
    )
    return jax.shard_map(
        functools.partial(body, mesh.shape["dp"]),
        mesh=mesh,
        in_specs=placed,
        out_specs=(
            P("dp", "tensor"),
            P("dp", "tensor"),
            P(),
            P(),
            P(None, None, "tensor"),
            P(None, "tensor"),
            P("tensor", None),
            P(),
            P(),
            P(),
            P(None, "tensor"),
            P("tensor"),
            P("tensor", None),
            P(),
        ),
        check_vma=False,
    )
```

```python
import functools

import jax
import jax.numpy as jnp
from jax import lax
from jax.experimental import pallas as pl
from jax.experimental.pallas import tpu as pltpu
from jax.sharding import PartitionSpec as P

HEAD_DIM = 56
CELL_LEN = 384
LANES = 128
WIDE = 256
epsilon = 1e-05
CURVE = 0.7978845608028654
CUBIC = 0.044715
bf16 = jnp.bfloat16
f32 = jnp.float32
MIB = 1024 * 1024
SMALL = 6


def dot_nn(left, right):
    return lax.dot_general(left, right, (((1,), (0,)), ((), ())), preferred_element_type=f32)


def dot_nt(left, right):
    return lax.dot_general(left, right, (((1,), (1,)), ((), ())), preferred_element_type=f32)


def dot_tn(left, right):
    return lax.dot_general(left, right, (((0,), (0,)), ((), ())), preferred_element_type=f32)


def struct(shape, dtype=bf16):
    return jax.ShapeDtypeStruct(shape, dtype)


CHAIN = []


def in_turn(arguments, first):
    if CHAIN:
        held = lax.optimization_barrier((arguments[first], CHAIN[0]))[0]
        arguments = (*arguments[:first], held, *arguments[first + 1 :])
    return arguments


def call(kernel, name, out_shape, flops, *arguments, scratch=(), scalars=0, limit=12, transcendentals=0, far_in=(), far_out=()):
    inputs = [pl.ANY if place in far_in else pltpu.VMEM for place in range(len(arguments) - scalars)]
    outputs = [pl.ANY if place in far_out else pltpu.VMEM for place in range(len(out_shape))]
    results = pl.pallas_call(
        kernel,
        in_specs=[pl.BlockSpec(memory_space=space) for space in [pltpu.SMEM] * scalars + inputs],
        out_specs=[pl.BlockSpec(memory_space=space) for space in outputs],
        out_shape=out_shape,
        scratch_shapes=scratch,
        compiler_params=pltpu.CompilerParams(vmem_limit_bytes=limit * MIB),
        name=name,
    )(*in_turn(arguments, scalars))
    CHAIN[:] = results[:1]
    return results


def loop(count, step):
    def wrapped(index, carry):
        step(index)
        return carry

    lax.fori_loop(0, count, wrapped, 0)


def by_rows(rows, step):
    whole = rows // 64

    def block(index):
        step(pl.multiple_of(index * 64, 64), 64)

    loop(whole, block)
    if rows % 64:
        step(64 * whole, rows % 64)


def lanes_at(index, size):
    return pl.ds(pl.multiple_of(index * size, size), size)


def start_copies(pairs, sems, first=0):
    copies = [
        pltpu.make_async_copy(source, target, sems.at[first + place])
        for place, (source, target) in enumerate(pairs)
    ]
    for copy in copies:
        copy.start()
    return copies


def wait_for(copies):
    for copy in copies:
        copy.wait()


def place_pieces(place, refs, target):
    share = refs[0].shape[0]
    for offset, ref in enumerate(refs):
        base = lax.bitwise_xor(place, offset) * share

        def step(start, size):
            value = ref[pl.ds(start, size), :].astype(target.dtype)
            target[pl.ds(pl.multiple_of(base + start, 8), size), :] = value

        by_rows(share, step)


def norm_columns(field, gain, shift):
    center = field - jnp.mean(field, 0, keepdims=True)
    spread = jnp.mean(center * center, 0, keepdims=True)
    return center * lax.rsqrt(spread + epsilon) * gain + shift


def front_kernel(
    place_ref, length_ref, own, near, far, both, weight_far, columns, bias,
    rows_far, normed_far, triple_far, probs_far, context_out,
    field, pieces, weight, rows_out, normed_out, triple_out, probs_out, sems,
):
    share = context_out.shape[0]
    heads = share // HEAD_DIM
    tokens = rows_out.shape[1]
    arrived = [pieces.at[offset] for offset in range(4)]
    copies = start_copies([*zip((own, near, far, both), arrived), (weight_far, weight)], sems)
    wait_for(copies[:4])
    place_pieces(place_ref[0], arrived, field)

    def norm_step(index):
        lanes = lanes_at(index, LANES)
        value = field[:, lanes]
        rows_out[:, lanes] = value.astype(bf16)
        normed_out[:, lanes] = norm_columns(value, columns[:, 0:1], columns[:, 1:2]).astype(bf16)

    loop(tokens // LANES, norm_step)
    copies[4].wait()
    leaving = start_copies([(rows_out, rows_far), (normed_out, normed_far)], sems, 5)

    def project_step(index):
        lanes = lanes_at(index, WIDE)
        triple_out[:, lanes] = (dot_nn(weight[...], normed_out[:, lanes]) + bias[...]).astype(bf16)

    loop(tokens // WIDE, project_step)
    leaving += start_copies([(triple_out, triple_far)], sems, 7)
    factor = HEAD_DIM ** (-0.5)

    def cell_step(cell):
        length = length_ref[cell]
        for head in range(heads):
            start = HEAD_DIM * head
            for block in range(CELL_LEN // LANES):
                span = LANES * (block + 1)
                base = pl.multiple_of(cell * CELL_LEN, LANES)
                here = pl.ds(pl.multiple_of(base + LANES * block, LANES), LANES)
                queries = triple_out[start : start + HEAD_DIM, here]
                keys = triple_out[share + start : share + start + HEAD_DIM, pl.ds(base, span)]
                values = triple_out[2 * share + start : 2 * share + start + HEAD_DIM, pl.ds(base, span)]
                scores = dot_tn(keys, queries) * factor
                key_place = lax.broadcasted_iota(jnp.int32, (span, LANES), 0)
                query_place = lax.broadcasted_iota(jnp.int32, (span, LANES), 1) + LANES * block
                allowed = (key_place <= query_place) & (key_place < length)
                masked = jnp.where(allowed, scores, -1e30)
                expo = jnp.exp(masked - jnp.max(masked, 0, keepdims=True))
                probs = (expo / jnp.sum(expo, 0, keepdims=True)).astype(bf16)
                probs_out[cell, head, :span, LANES * block : span] = probs
                context_out[start : start + HEAD_DIM, here] = dot_nn(values, probs).astype(bf16)
        pltpu.make_async_copy(probs_out.at[cell], probs_far.at[cell], sems.at[8 + cell]).start()

    loop(tokens // CELL_LEN, cell_step)
    for cell in range(tokens // CELL_LEN):
        pltpu.make_async_copy(probs_out.at[cell], probs_far.at[cell], sems.at[8 + cell]).wait()
    wait_for(leaving)


def front_call(place, lengths, pieces, columns, weight, bias):
    share, tokens = pieces[0].shape
    width = weight.shape[1]
    heads = share // HEAD_DIM
    cells = tokens // CELL_LEN
    pairs = cells * heads * CELL_LEN * CELL_LEN
    return call(
        front_kernel,
        "front",
        [
            struct((width, tokens)),
            struct((width, tokens)),
            struct((3 * share, tokens)),
            struct((cells, heads, CELL_LEN, CELL_LEN)),
            struct((share, tokens)),
        ],
        tokens * width * share * 6 + pairs * HEAD_DIM * 4,
        place, lengths, *pieces, weight, columns, bias,
        scratch=[
            pltpu.VMEM((width, tokens), f32),
            pltpu.VMEM((4, share, tokens), bf16),
            pltpu.VMEM(weight.shape, bf16),
            pltpu.VMEM((width, tokens), bf16),
            pltpu.VMEM((width, tokens), bf16),
            pltpu.VMEM((3 * share, tokens), bf16),
            pltpu.VMEM((cells, heads, CELL_LEN, CELL_LEN), bf16),
            pltpu.SemaphoreType.DMA((8 + cells,)),
        ],
        scalars=2,
        limit=60,
        far_in=range(5),
        far_out=range(4),
        transcendentals=pairs,
    )


def gate_parts(value):
    square = value * value
    bend = jnp.tanh(CURVE * (value + CUBIC * square * value))
    upper = 0.5 * (1.0 + bend)
    slope = upper + 0.5 * value * (1.0 - bend * bend) * CURVE * (1.0 + 3.0 * CUBIC * square)
    return value * upper, slope


def middle_kernel(
    own, near, far, both, own_weight, near_weight, far_weight, both_weight, rows_far, up_far, columns,
    resid_far, normed_far, hidden_out, slope_out,
    field, weight, pieces, weights, rows_ref, up, resid_out, normed_out, sems,
):
    tokens = resid_out.shape[1]
    share = own.shape[0]
    sources = own, near, far, both, own_weight, near_weight, far_weight, both_weight
    targets = [pieces.at[place] for place in range(4)] + [weights.at[place] for place in range(4)]
    copies = start_copies([*zip(sources, targets), (rows_far, rows_ref), (up_far, up)], sems)
    wait_for(copies[:8])
    place_pieces(0, [pieces.at[place] for place in range(4)], field)
    for place in range(4):
        weight[:, share * place : share * (place + 1)] = weights[place]
    wait_for(copies[8:])

    def leaving(index):
        lanes = lanes_at(index, WIDE)
        resid_copy = pltpu.make_async_copy(
            resid_out.at[:, lanes], resid_far.at[:, lanes], sems.at[10 + 2 * index]
        )
        normed_copy = pltpu.make_async_copy(
            normed_out.at[:, lanes], normed_far.at[:, lanes], sems.at[11 + 2 * index]
        )
        return resid_copy, normed_copy

    def step(index):
        lanes = lanes_at(index, WIDE)
        added = dot_nn(weight[...], field[:, lanes].astype(bf16))
        resid = rows_ref[:, lanes].astype(f32) + added + columns[:, 2:3]
        resid_out[:, lanes] = resid
        normed = norm_columns(resid, columns[:, 3:4], columns[:, 4:5]).astype(bf16)
        normed_out[:, lanes] = normed
        hidden, slope = gate_parts(dot_nn(up[...], normed) + columns[:, 5:6])
        hidden_out[:, lanes] = hidden.astype(bf16)
        slope_out[:, lanes] = slope
        for copy in leaving(index):
            copy.start()

    loop(tokens // WIDE, step)
    for index in range(tokens // WIDE):
        wait_for(leaving(index))


def middle_call(pieces, weights, rows_all, columns, up):
    width, tokens = rows_all.shape
    hidden = up.shape[0]
    return call(
        middle_kernel,
        "middle",
        [
            struct((width, tokens), f32),
            struct((width, tokens)),
            struct((hidden, tokens)),
            struct((hidden, tokens), f32),
        ],
        tokens * width * (width + hidden) * 2,
        *pieces, *weights, rows_all, up, columns,
        scratch=[
            pltpu.VMEM((width, tokens), f32),
            pltpu.VMEM((width, width), bf16),
            pltpu.VMEM((4, *pieces[0].shape), bf16),
            pltpu.VMEM((4, *weights[0].shape), bf16),
            pltpu.VMEM((width, tokens), bf16),
            pltpu.VMEM(up.shape, bf16),
            pltpu.VMEM((width, tokens), f32),
            pltpu.VMEM((width, tokens), bf16),
            pltpu.SemaphoreType.DMA((10 + 2 * (tokens // WIDE),)),
        ],
        limit=50,
        far_in=range(10),
        far_out=range(2),
        transcendentals=tokens * hidden,
    )


def spread_kernel(place_ref, own, near, far, both, rows_out, sums_out, field):
    place_pieces(place_ref[0], (own, near, far, both), field)
    rows_out[...] = field[...].astype(bf16)
    sums_out[...] = jnp.sum(field[...], 1, keepdims=True)


def spread_call(place, pieces):
    share, tokens = pieces[0].shape
    return call(
        spread_kernel,
        "spread",
        [struct((4 * share, tokens)), struct((4 * share, 1), f32)],
        4 * share * tokens,
        place, *pieces,
        scratch=[pltpu.VMEM((4 * share, tokens), f32)],
        scalars=1,
    )


def store_halves(bit, value, lanes, keep_out, send_out):
    half = keep_out.shape[0]

    @pl.when(bit == 0)
    def _():
        keep_out[:, lanes] = value[:half]
        send_out[:, lanes] = value[half:]

    @pl.when(bit != 0)
    def _():
        keep_out[:, lanes] = value[half:]
        send_out[:, lanes] = value[:half]


def turn_kernel(
    place_ref, cotangent, slope, down, up, pre_out, keep_out, send_out, sums_out,
):
    tokens = cotangent.shape[1]
    core = lax.rem(place_ref[0], 2)
    sums_out[...] = jnp.zeros_like(sums_out)

    def step(index):
        lanes = lanes_at(index, WIDE)
        pre = dot_nn(down[...], cotangent[:, lanes]) * slope[:, lanes]
        sums_out[...] += jnp.sum(pre, 1, keepdims=True)
        low = pre.astype(bf16)
        pre_out[:, lanes] = low
        store_halves(core, dot_nn(up[...], low).astype(bf16), lanes, keep_out, send_out)

    loop(tokens // WIDE, step)


def turn_call(place, cotangent, slope, down, up):
    width, tokens = cotangent.shape
    hidden = up.shape[1]
    return call(
        turn_kernel,
        "turn",
        [
            struct((hidden, tokens)),
            struct((width // 2, tokens)),
            struct((width // 2, tokens)),
            struct((hidden, 1), f32),
        ],
        tokens * width * hidden * 4,
        place, cotangent, slope, down, up,
        scalars=1,
    )


def norm_back(field, grad, gain):
    center = field - jnp.mean(field, 0, keepdims=True)
    inverse = lax.rsqrt(jnp.mean(center * center, 0, keepdims=True) + epsilon)
    normed = center * inverse
    scaled = grad * gain
    inner = jnp.mean(scaled * normed, 0, keepdims=True)
    back = inverse * (scaled - jnp.mean(scaled, 0, keepdims=True) - normed * inner)
    return normed, back


def add_parts(left, right):
    return (left.astype(f32) + right.astype(f32)).astype(bf16)


def back_kernel(
    place_ref, mine, other, resid, cotangent, columns, out_weight, triple, probs_ref, weight,
    dh_out, low_out, triple_out, keep_out, send_out, sums_out, bias_out,
    grad, context_grad, gain_sum, shift_sum, total_sum,
):
    share = out_weight.shape[0]
    width, tokens = resid.shape
    half = width // 2
    heads = share // HEAD_DIM
    factor = HEAD_DIM ** (-0.5)
    core = lax.rem(place_ref[0], 2)
    place_pieces(core, (mine, other), grad)
    for item in (gain_sum, shift_sum, total_sum, bias_out):
        item[...] = jnp.zeros_like(item)

    def norm_step(index):
        lanes = lanes_at(index, LANES)
        upper = grad[:, lanes]
        normed, back = norm_back(resid[:, lanes], upper, columns[:, 3:4])
        total = cotangent[:, lanes].astype(f32) + back
        dh_out[:, lanes] = total
        low_out[:, lanes] = total.astype(bf16)
        gain_sum[...] += upper * normed
        shift_sum[...] += upper
        total_sum[...] += total

    loop(tokens // LANES, norm_step)
    sums_out[:, 0:1] = jnp.sum(gain_sum[...], 1, keepdims=True)
    sums_out[:, 1:2] = jnp.sum(shift_sum[...], 1, keepdims=True)
    sums_out[:, 2:3] = jnp.sum(total_sum[...], 1, keepdims=True)

    def context_step(index):
        lanes = lanes_at(index, WIDE)
        context_grad[:, lanes] = dot_nn(out_weight[...], low_out[:, lanes]).astype(bf16)

    loop(tokens // WIDE, context_step)
    blocks = CELL_LEN // LANES

    def cell_step(cell):
        base = pl.multiple_of(cell * CELL_LEN, LANES)
        for head in range(heads):
            start = HEAD_DIM * head
            query_rows = slice(start, start + HEAD_DIM)
            key_rows = slice(share + start, share + start + HEAD_DIM)
            value_rows = slice(2 * share + start, 2 * share + start + HEAD_DIM)
            key_grads = [None] * blocks
            value_grads = [None] * blocks
            query_sum = jnp.zeros((HEAD_DIM, 1), f32)
            value_sum = jnp.zeros((HEAD_DIM, 1), f32)
            for block in range(blocks):
                span = LANES * (block + 1)
                here = pl.ds(pl.multiple_of(base + LANES * block, LANES), LANES)
                queries = triple[query_rows, here]
                keys = triple[key_rows, pl.ds(base, span)]
                values = triple[value_rows, pl.ds(base, span)]
                low = context_grad[query_rows, here]
                probs_low = probs_ref[cell, head, :span, LANES * block : span]
                probs = probs_low.astype(f32)
                prob_grad = dot_tn(values, low)
                inner = jnp.sum(prob_grad * probs, 0, keepdims=True)
                score = (probs * (prob_grad - inner) * factor).astype(bf16)
                query_grad = dot_nn(keys, score)
                query_sum += jnp.sum(query_grad, 1, keepdims=True)
                triple_out[query_rows, here] = query_grad.astype(bf16)
                key_part = dot_nt(queries, score)
                value_part = dot_nt(low, probs_low)
                for place in range(block + 1):
                    lanes = slice(LANES * place, LANES * (place + 1))
                    if key_grads[place] is None:
                        key_grads[place] = key_part[:, lanes]
                        value_grads[place] = value_part[:, lanes]
                    else:
                        key_grads[place] += key_part[:, lanes]
                        value_grads[place] += value_part[:, lanes]
            for block in range(blocks):
                here = pl.ds(pl.multiple_of(base + LANES * block, LANES), LANES)
                triple_out[key_rows, here] = key_grads[block].astype(bf16)
                triple_out[value_rows, here] = value_grads[block].astype(bf16)
                value_sum += jnp.sum(value_grads[block], 1, keepdims=True)
            bias_out[query_rows, 0:1] += query_sum
            bias_out[query_rows, 1:2] += value_sum

    loop(tokens // CELL_LEN, cell_step)

    def part_step(index):
        lanes = lanes_at(index, WIDE)
        part = dot_nn(weight[...], triple_out[:, lanes]).astype(bf16)
        store_halves(core, part, lanes, keep_out, send_out)

    loop(tokens // WIDE, part_step)


def back_call(place, mine, other, resid, cotangent, columns, out_weight, triple, probs, weight):
    width, tokens = resid.shape
    share = out_weight.shape[0]
    cells, heads = probs.shape[:2]
    pairs = cells * heads * CELL_LEN * CELL_LEN
    return call(
        back_kernel,
        "back",
        [
            struct((width, tokens), f32),
            struct((width, tokens)),
            struct((3 * share, tokens)),
            struct((width // 2, tokens)),
            struct((width // 2, tokens)),
            struct((width, 8), f32),
            struct((share, 8), f32),
        ],
        tokens * width * share * 8 + pairs * HEAD_DIM * 8,
        place, mine, other, resid, cotangent, columns, out_weight, triple, probs, weight,
        scratch=[pltpu.VMEM((width, tokens), f32), pltpu.VMEM((share, tokens), bf16)]
        + [pltpu.VMEM((width, LANES), f32)] * 3,
        scalars=1,
    )


def last_kernel(
    place_ref, mine, other, rows_ref, dh, columns, cotangent_sums, pre_sums, back_sums, bias_sums,
    out, sums_out, grad, gain_sum, shift_sum, field,
):
    share, tokens = out.shape
    width = rows_ref.shape[0]
    half = width // 2
    place = place_ref[0]
    core = lax.rem(place, 2)
    place_pieces(core, (mine, other), grad)
    gain_sum[...] = jnp.zeros_like(gain_sum)
    shift_sum[...] = jnp.zeros_like(shift_sum)

    def norm_step(index):
        lanes = lanes_at(index, LANES)
        upper = grad[:, lanes]
        normed, back = norm_back(rows_ref[:, lanes].astype(f32), upper, columns[:, 0:1])
        field[...] = dh[:, lanes] + back
        out[:, lanes] = field[pl.ds(pl.multiple_of(place * share, 8), share), :].astype(bf16)
        gain_sum[...] += upper * normed
        shift_sum[...] += upper

    loop(tokens // LANES, norm_step)
    field[:, 0:1] = jnp.sum(gain_sum[...], 1, keepdims=True)
    field[:, 1:2] = jnp.sum(shift_sum[...], 1, keepdims=True)
    field[:, 2:3] = cotangent_sums[...]
    field[:, 3:4] = pre_sums[...]
    field[:, 4:7] = back_sums[:, 0:3]
    field[0:share, 7:9] = bias_sums[:, 0:2]
    sums_out[...] = field[...].T[0:16, :]


def last_call(place, mine, other, rows_all, dh, columns, *sums):
    width, tokens = rows_all.shape
    return call(
        last_kernel,
        "last",
        [struct((width // 4, tokens)), struct((16, width), f32)],
        width * tokens * 12,
        place, mine, other, rows_all, dh, columns, *sums,
        scratch=[pltpu.VMEM((width, tokens), f32)] + [pltpu.VMEM((width, LANES), f32)] * 3,
        scalars=1,
    )


def add_kernel(left, right, out):
    def step(start, size):
        rows = pl.ds(start, size)
        out[rows, :] = add_parts(left[rows, :], right[rows, :])

    by_rows(out.shape[0], step)


def add_call(left, right):
    return call(add_kernel, "add", [struct(left.shape)], left.size, left, right, limit=SMALL)[0]


def add_wide_kernel(left, right, out):
    out[...] = left[...] + right[...]


def add_wide_call(left, right):
    return call(add_wide_kernel, "add_wide", [struct(left.shape, f32)], left.size, left, right, limit=SMALL)[0]


def down_kernel(place_ref, hidden, down, keep_out, send_out):
    tokens = hidden.shape[1]
    share = keep_out.shape[0] // 2
    core = lax.rem(place_ref[0], 2)

    def step(index):
        lanes = lanes_at(index, WIDE)
        part = dot_nn(down[...], hidden[:, lanes]).astype(bf16)
        for chip in range(2):
            rows = slice(share * chip, share * (chip + 1))
            low = part[2 * share * chip : 2 * share * chip + share]
            high = part[2 * share * chip + share : 2 * share * (chip + 1)]

            @pl.when(core == 0)
            def _():
                keep_out[rows, lanes] = low
                send_out[rows, lanes] = high

            @pl.when(core != 0)
            def _():
                keep_out[rows, lanes] = high
                send_out[rows, lanes] = low

    loop(tokens // WIDE, step)


def down_call(place, hidden, down):
    width, inner = down.shape
    tokens = hidden.shape[1]
    return call(
        down_kernel,
        "down",
        [struct((width // 2, tokens))] * 2,
        tokens * width * inner * 2,
        place, hidden, down,
        scalars=1,
    )


def down_add_kernel(place_ref, keep, got, keep_out, send_out, field):
    share = keep_out.shape[0]
    chip = lax.div(place_ref[0], 2)
    field[...] = keep[...].astype(f32) + got[...].astype(f32)
    keep_out[...] = field[pl.ds(pl.multiple_of(chip * share, 8), share), :].astype(bf16)
    send_out[...] = field[pl.ds(pl.multiple_of((1 - chip) * share, 8), share), :].astype(bf16)


def down_add_call(place, keep, got):
    rows, tokens = keep.shape
    return call(
        down_add_kernel,
        "down_add",
        [struct((rows // 2, tokens))] * 2,
        keep.size,
        place, keep, got,
        scratch=[pltpu.VMEM(keep.shape, f32)],
        scalars=1,
    )


def layer_out_kernel(place_ref, keep, got, resid, columns, out):
    share = out.shape[0]
    rows = pl.ds(pl.multiple_of(place_ref[0] * share, 8), share)
    total = keep[...].astype(f32) + got[...].astype(f32)
    out[...] = (resid[rows, :] + total + columns[rows, 6:7]).astype(bf16)


def layer_out_call(place, keep, got, resid, columns):
    return call(
        layer_out_kernel,
        "layer_out",
        [struct(keep.shape)],
        keep.size,
        place, keep, got, resid, columns,
        scalars=1,
    )[0]


def grad_kernel(ranges, place_ref, *refs):
    pairs, (keep_out, send_out) = refs[:-2], refs[-2:]
    side = lax.rem(place_ref[0], 2)
    width = keep_out.shape[1]

    def step(lanes):
        parts = []
        for left, right, (low, high) in zip(pairs[0::2], pairs[1::2], ranges):
            parts.append(dot_nt(left[low:high, :], right[lanes, :]).astype(bf16))
        value = parts[0] if len(parts) == 1 else jnp.concatenate(parts, 0)
        store_halves(side, value, lanes, keep_out, send_out)

    loop(width // WIDE, lambda index: step(lanes_at(index, WIDE)))
    if width % WIDE:
        step(slice(width - width % WIDE, width))


def grad_call(dp_place, ranges, *pairs):
    rows = sum(high - low for low, high in ranges)
    tokens = pairs[0].shape[1]
    width = pairs[1].shape[0]
    return call(
        functools.partial(grad_kernel, ranges),
        "grad",
        [struct((rows // 2, width)), struct((rows // 2, width))],
        2 * rows * tokens * width,
        dp_place, *pairs,
        scalars=1,
    )


def settle_kernel(dp_ref, mine, got, out):
    def copy_from(ref):
        def step(start, size):
            rows = pl.ds(start, size)
            out[rows, :] = ref[rows, :]

        by_rows(out.shape[0], step)

    pl.when(dp_ref[2] == 1)(lambda: copy_from(got))
    pl.when(dp_ref[2] == 0)(lambda: copy_from(mine))


def settle_call(dp, mine, got):
    return call(settle_kernel, "settle", [struct(mine.shape)], mine.size, dp, mine, got, scalars=1, limit=SMALL)[0]


def final_kernel(count, dp_ref, *refs):
    side = lax.rem(dp_ref[0], 2)
    outs = refs[2 * count :]

    def put(start, ref):
        done = 0
        rows = ref.shape[0]
        for out in outs:
            size = out.shape[0]
            low, high = max(start, done), min(start + rows, done + size)
            if low < high:

                def step(begin, count):
                    value = ref[pl.ds(low - start + begin, count), :].astype(f32)
                    out[pl.ds(low - done + begin, count), :] = value

                by_rows(high - low, step)
            done += size

    base = 0
    for place in range(count):
        mine, got = refs[2 * place : 2 * place + 2]
        half = mine.shape[0]

        @pl.when(side == 0)
        def _():
            put(base, mine)
            put(base + half, got)

        @pl.when(side != 0)
        def _():
            put(base, got)
            put(base + half, mine)

        base += 2 * half


def final_call(dp, parts, sizes):
    width = parts[0].shape[1]
    return call(
        functools.partial(final_kernel, len(parts) // 2),
        "final",
        [struct((size, width), f32) for size in sizes],
        sum(sizes) * width,
        dp, *parts,
        scalars=1,
        limit=SMALL,
    )


def swap_core(value):
    return lax.ppermute(value, "tensor", [(place, place ^ 1) for place in range(4)])


def swap_chip(value):
    return lax.ppermute(value, "tensor", [(place, place ^ 2) for place in range(4)])


def after(value, *others):
    return lax.optimization_barrier((value, *others))[0]


def all_pieces(share):
    far = swap_chip(share)
    return share, swap_core(share), far, swap_core(far)


def ordered(bit, mine, other, axis):
    low = jnp.where(bit == 0, mine, other)
    high = jnp.where(bit == 0, other, mine)
    return jnp.concatenate([low, high], axis)


def line_pairs(pairs):
    return [(2 * source + side, 2 * target + side) for source, target in pairs for side in (0, 1)]


INWARD = line_pairs([(0, 1), (3, 2)])
MIDDLE = line_pairs([(1, 2), (2, 1)])
OUTWARD = line_pairs([(1, 0), (2, 3)])
ACROSS = [(place, place ^ 1) for place in range(8)]
ACROSS_MIDDLE = [(2, 3), (3, 2), (4, 5), (5, 4)]


def hop(value, pairs):
    return lax.ppermute(value, "dp", pairs)


STAGES = (ACROSS, INWARD, MIDDLE, OUTWARD, ACROSS)


class CellSum:
    def __init__(self, groups, dp, parts):
        self.groups, self.dp = groups, dp
        self.mine, self.got = parts
        self.stage = -1

    def step(self):
        self.stage += 1
        if self.groups != 8:
            return
        send = self.got
        if self.stage == 4:
            send = self.mine = settle_call(self.dp, self.mine, self.got)
        elif self.stage > 0:
            send = self.mine = add_call(self.mine, self.got)
        self.got = hop(send, STAGES[self.stage])

    def plain(self):
        value = ordered(self.dp[0] % 2, self.mine, self.got, 0)
        return lax.psum(value, "dp").astype(f32)


def finish(sums, sizes):
    if sums[0].groups == 8:
        return final_call(sums[0].dp, [piece for item in sums for piece in (item.mine, item.got)], sizes)
    value = jnp.concatenate([item.plain() for item in sums], 0)
    ends = [sum(sizes[: place + 1]) for place in range(len(sizes))]
    return [value[end - size : end] for end, size in zip(ends, sizes)]


def end_round(sums, *values):
    held = lax.optimization_barrier((*[item.got for item in sums], *values))
    for item, got in zip(sums, held):
        item.got = got
    return held[len(sums) :]


def body(
    groups,
    tokens,
    first_gain,
    first_shift,
    triple_weight,
    triple_bias,
    output_weight,
    output_bias,
    second_gain,
    second_shift,
    up_weight,
    up_bias,
    down_weight,
    down_bias,
    cotangent,
    lengths,
):
    share = tokens.shape[1]
    width = triple_weight.shape[0]
    index = lax.axis_index("tensor").astype(jnp.int32)
    core, chip = index % 2, index // 2
    place = index.reshape(1)
    row = lax.axis_index("dp").astype(jnp.int32)
    at_end = ((row < 2) | (row >= groups - 2)).astype(jnp.int32)
    dp = jnp.stack([row, jnp.int32(groups // 2), at_end])
    CHAIN.clear()
    fence = lambda *values: lax.optimization_barrier(values)
    token_own, grad_own = tokens.T, cotangent.T
    token_far, token_near = swap_chip(token_own), swap_core(token_own)
    grad_near, weight_near = swap_core(grad_own), swap_core(output_weight)
    triple_t = triple_weight.transpose(1, 2, 0).reshape(3 * share, width)
    bias_flat = jnp.concatenate([triple_bias[0], jnp.zeros((share,), f32), triple_bias[1]])[:, None]
    columns = jnp.stack(
        [first_gain, first_shift, output_bias, second_gain, second_shift, up_bias, down_bias], 1
    )
    up_t, triple_plain = up_weight.T, triple_t.T
    token_far, token_near, up_t, triple_plain, columns, bias_flat, out_weight = fence(
        token_far, token_near, up_t, triple_plain, columns, bias_flat, output_weight
    )
    token_both = swap_core(token_far)
    weight_far = swap_chip(out_weight)
    own_t = out_weight.T
    token_both, own_t = fence(token_both, own_t)
    rows_all, first_normed, triple, probs, context = front_call(
        place, lengths, (token_own, token_near, token_far, token_both), columns, triple_t, bias_flat
    )
    context_far, context_near = swap_chip(context), swap_core(context)
    weight_far, weight_near, down_plain, _ = fence(weight_far, weight_near, down_weight, context)
    weight_both = swap_core(weight_far)
    weights = own_t, weight_near.T, weight_far.T, weight_both.T
    down_t = down_plain.T
    context_far, context_near, down_t, grad_own, *weights = fence(
        context_far, context_near, down_t, grad_own, *weights
    )
    context_both = swap_core(context_far)
    grad_far = swap_chip(grad_own)
    resid, second_normed, hidden, slope = middle_call(
        (context, context_near, context_far, context_both), weights, rows_all, columns, up_t
    )
    grad_far, _ = fence(grad_far, second_normed)
    grad_both = swap_core(grad_far)
    grad_rows, cotangent_sums = spread_call(place, (grad_own, grad_near, grad_far, grad_both))
    half = width // 2

    def cell_sum(ranges, *pairs):
        return CellSum(groups, dp, grad_call(dp, ranges, *pairs))

    down_low = cell_sum([(0, half)], hidden, grad_rows)
    down_low.step()
    pre_low, keep, send, pre_sums = turn_call(place, grad_rows, slope, down_weight, up_weight)
    keep, send = end_round([down_low], keep, send)
    near = swap_core(send)
    down_low.step()
    down_keep, down_send = down_call(place, hidden, down_t)
    near = add_call(keep, near)
    far = swap_chip(near)
    down_high = cell_sum([(half, width)], hidden, grad_rows)
    down_high.step()
    down_got = swap_core(down_send)
    up_low = cell_sum([(0, half)], second_normed, pre_low)
    up_high = cell_sum([(half, width)], second_normed, pre_low)
    far, down_got, near, _ = end_round([down_low, down_high], far, down_got, near, up_high.mine)
    mine = add_call(near, far)
    other = swap_core(mine)
    for item in (down_high, down_low, up_low, up_high):
        item.step()
    down_keep, down_send = down_add_call(place, down_keep, down_got)
    down_got = swap_chip(down_send)
    dh, low, triple_low, keep, send, back_sums, bias_sums = back_call(
        place, mine, other, resid, grad_rows, columns, output_weight, triple, probs, triple_plain
    )
    keep, send, down_got = end_round([down_low, down_high, up_low, up_high], keep, send, down_got)
    near = swap_core(send)
    early = cell_sum([(0, 2 * share)], triple_low, first_normed)
    near = add_call(keep, near)
    far = swap_chip(near)
    for item in (up_low, down_high, down_low, early):
        item.step()
    late = cell_sum([(2 * share, 3 * share), (0, share)], triple_low, first_normed, context, low)
    far, near, _ = end_round([early, down_low, down_high, up_low, up_high], far, near, late.mine)
    mine = add_call(near, far)
    other = swap_core(mine)
    for item in (early, up_low, down_high, late):
        item.step()
    input_grad, small = last_call(
        place, mine, other, rows_all, dh, columns, cotangent_sums, pre_sums, back_sums, bias_sums
    )
    (small,) = end_round([down_low, down_high, up_low, up_high, early, late], small)
    shifts = (1, 4, 2)
    if groups != 8:
        small = lax.psum(small, "dp")
    rounds = [
        (late, early, up_low, down_low),
        (up_high, late, early, down_high),
        (up_high, late, up_low),
        (early, up_high),
        (up_high, late),
    ]
    for place_in, items in enumerate(rounds):
        if groups == 8 and place_in < 3:
            got = hop(small, [(spot, spot ^ shifts[place_in]) for spot in range(8)])
        for item in items:
            item.step()
        if place_in == 2:
            down_grad = finish([down_low, down_high], [width])[0]
        if place_in == 0:
            layer_out = layer_out_call(place, down_keep, down_got, resid, columns)
        if groups == 8 and place_in < 3:
            (got,) = end_round(list(items), got)
            small = add_wide_call(small, got)
        elif place_in < 4:
            end_round(list(items))
    up_grad = finish([up_low, up_high], [width])[0]
    triple_grad, output_grad = finish([early, late], [3 * share, share])
    triple_grad = triple_grad.reshape(3, share, width).transpose(2, 0, 1)
    return (
        layer_out.T,
        input_grad.T,
        small[0],
        small[1],
        triple_grad,
        small[7:9, :share],
        output_grad,
        small[6],
        small[4],
        small[5],
        up_grad,
        small[3],
        down_grad,
        small[2],
    )


def solution(mesh):
    placed = (
        P("dp", "tensor"),
        P(),
        P(),
        P(None, None, "tensor"),
        P(None, "tensor"),
        P("tensor", None),
        P(),
        P(),
        P(),
        P(None, "tensor"),
        P("tensor"),
        P("tensor", None),
        P(),
        P("dp", "tensor"),
        P("dp"),
    )
    return jax.shard_map(
        functools.partial(body, mesh.shape["dp"]),
        mesh=mesh,
        in_specs=placed,
        out_specs=(
            P("dp", "tensor"),
            P("dp", "tensor"),
            P(),
            P(),
            P(None, None, "tensor"),
            P(None, "tensor"),
            P("tensor", None),
            P(),
            P(),
            P(),
            P(None, "tensor"),
            P("tensor"),
            P("tensor", None),
            P(),
        ),
        check_vma=False,
    )
```
